32 devices in a mesh: grp: 2 (over x), pix: 16 (over z, y, core).
Axes of the slice: x: 2, y: 2, z: 4, core: 2. Of those that a mesh axis runs over, the one named last changes fastest.
Arguments:
- particle_images: bfloat16 [8192, 128, 128], P(('grp', 'pix')), parts along dimension 0, may hold values from -6 to 6
- defocus_group: int32 [8192], P(('grp', 'pix')), parts along dimension 0, may hold values from 0 to 63
- live_counts: int32 [32], P(('grp', 'pix')), parts along dimension 0, may hold values from 192 to 256, as said below
- defocus_values: float32 [128], P('grp'), parts along dimension 0, may hold values from 50 to 400
- test_matrix: bfloat16 [32768, 128], P(('grp', 'pix')), parts along dimension 0, may hold values from -0.046875 to 0.046875
Outputs:
- range_basis: bfloat16 [8192, 128], P(('grp', 'pix')), parts along dimension 0
- projection: float32 [32768, 128], P(('grp', 'pix')), parts along dimension 0
The draws below stay inside these ranges and needn't reach their ends.
There are 2 independent parts, one for each index of `grp`. The reference program is written for one: setup_inputs(seed, part) draws one part's arguments, and reference() takes and returns one part's arrays. A program takes and returns all parts, laid end to end along the dimension named above; each array names one. Nothing has to cross between parts.
Inputs may be any that keep to these rules, and one draw needn't show every extreme that they name: `live_counts`: each entry is the number of live particle slots of a shard, counted from its first slot; some shard is full in every draw.
All inputs are finite; a program needn't handle non-finite values.
Results may differ from the reference program's by a relative error of at most 0.011.
Values may be sent and summed in bfloat16 or wider, within the bound.
A program may use at most 192 MiB of HBM per device.

```python
import math
import jax
import jax.numpy as jnp
from jax import lax

SIDE = 128
RANK = 128
GROUPS = 64
PART_DEV = 256
PIX = 16384
SHARDS = 16
PARTICLES = 4096


def draw_live_counts(key, part):
    first_key, second_key = jax.random.split(jax.random.fold_in(key, 17))
    counts_all = jax.random.randint(first_key, (SHARDS,), 3 * PART_DEV // 4, PART_DEV + 1)
    full_shard = jax.random.randint(second_key, (), 0, SHARDS)
    return jnp.where(jnp.arange(SHARDS) == full_shard, PART_DEV, counts_all).astype(jnp.int32)


def with_ends(entries, own_key, smallest, high):
    shape = entries.shape
    place = [jax.random.randint(jax.random.fold_in(own_key, axis), (), 0, shape[axis]) for axis in range(len(shape))]
    entries = entries.at[tuple(place)].set(smallest)
    longest = shape.index(max(shape))
    place[longest] = (place[longest] + 1) % shape[longest]
    return entries.at[tuple(place)].set(high)


def shard_levels(rng, dims, cuts, least, top_value):
    level, own = 1.0, jax.random.fold_in(rng, 6)
    for dim, parts in cuts:
        steps = jnp.exp(jax.random.uniform(jax.random.fold_in(own, dim), (parts,), jnp.float32, least / len(cuts), top_value / len(cuts)))
        level = level * jnp.repeat(steps, dims[dim] // parts).reshape([-1 if axis == dim else 1 for axis in range(len(dims))])
    return level


def bell_draw(rng, dims, width, bound, cuts=(), kind=jnp.bfloat16):
    level = shard_levels(rng, dims, cuts, -0.22, 0.18) if cuts else 1.0
    drawn = jax.random.normal(rng, dims, jnp.float32) * width * level
    return jnp.minimum(jnp.maximum(drawn, -bound), bound).astype(kind)


def setup_inputs(seed: int = 0, part: int = 0) -> dict:
    splits = jax.random.split(jax.random.key(seed), 6)
    own_keys = jax.random.split(jax.random.fold_in(splits[5], part), 6)
    return {
        "particle_images": bell_draw(own_keys[0], (PARTICLES, SIDE, SIDE), 1.0, 6.0, ((0, 16),)),
        "defocus_group": with_ends(jax.random.randint(own_keys[1], (PARTICLES,), 0, GROUPS), jax.random.fold_in(own_keys[1], 1), 0, GROUPS - 1).astype(jnp.int32),
        "live_counts": draw_live_counts(jax.random.fold_in(jax.random.fold_in(splits[5], part), 71), part),
        "defocus_values": jnp.clip(jnp.exp(jax.random.uniform(own_keys[3], (GROUPS,), jnp.float32, math.log(50.0), math.log(400.0))), 50.0, 400.0),
        "test_matrix": bell_draw(own_keys[4], (PIX, RANK), PIX ** -0.5, 0.046875, ((0, 16),)),
    }


AMPLITUDE = 0.1
WIENER = 0.1

def frequency_sq(length):
    indices = jnp.arange(length, dtype=jnp.int32)
    frequency = jnp.where(indices < length // 2, indices, indices - length).astype(jnp.float32) / length
    return frequency[:, None] ** 2 + frequency[None, :] ** 2

def wiener_table(defocus_values, length):
    phases = jnp.pi * defocus_values[:, None, None] * frequency_sq(length)[None]
    contrast = -(math.sqrt(1.0 - AMPLITUDE ** 2) * jnp.sin(phases) + AMPLITUDE * jnp.cos(phases))
    return contrast / (contrast * contrast + WIENER)

def dft_tables(length):
    indices = jnp.arange(length, dtype=jnp.int32)
    product = indices[:, None] * indices[None, :] % length
    angles = 2.0 * math.pi / length * product.astype(jnp.float32)
    return (jnp.cos(angles).astype(jnp.bfloat16), jnp.sin(angles).astype(jnp.bfloat16))

def round_keep(values):
    return lax.optimization_barrier(values.astype(jnp.bfloat16)).astype(jnp.float32)

def left_mul(table_now, values_now):
    return jnp.einsum('uj,bjv->buv', table_now, values_now, precision=lax.Precision.HIGHEST)

def right_mul(values_now, table_now):
    return jnp.einsum('bjk,kv->bjv', values_now, table_now, precision=lax.Precision.HIGHEST)

def reference(particle_images, defocus_group, live_counts, defocus_values, test_matrix):
    filter_table = wiener_table(defocus_values, SIDE).astype(jnp.bfloat16).astype(jnp.float32)
    cos_b, sin_b = dft_tables(SIDE)
    cosine = cos_b.astype(jnp.float32)
    sine = sin_b.astype(jnp.float32)
    both_tables = jnp.concatenate([cosine, sine], axis=1)

    def correct(block_index):
        start_row = block_index * PART_DEV
        images_blk = lax.dynamic_slice_in_dim(particle_images, start_row, PART_DEV, 0).astype(jnp.float32)
        group_ids = lax.dynamic_slice_in_dim(defocus_group, start_row, PART_DEV, 0)
        filter_now = filter_table[group_ids]
        first_pass = round_keep(right_mul(images_blk, both_tables))
        cos_side = left_mul(cosine, first_pass)
        sin_side = left_mul(sine, first_pass)
        filt_re = round_keep((cos_side[..., :SIDE] - sin_side[..., SIDE:]) * filter_now)
        filt_im = round_keep(-(cos_side[..., SIDE:] + sin_side[..., :SIDE]) * filter_now)
        re_both = right_mul(filt_re, both_tables)
        im_both = right_mul(filt_im, both_tables)
        back_re = round_keep(re_both[..., :SIDE] - im_both[..., SIDE:])
        back_im = round_keep(re_both[..., SIDE:] + im_both[..., :SIDE])
        values = (left_mul(cosine, back_re) - left_mul(sine, back_im)) / float(SIDE * SIDE)
        live_rows = jnp.arange(PART_DEV, dtype=jnp.int32) < live_counts[block_index]
        values = jnp.where(live_rows[:, None, None], values, 0.0)
        return values.reshape(PART_DEV, PIX).astype(jnp.bfloat16)
    corrected = lax.map(correct, jnp.arange(SHARDS, dtype=jnp.int32)).reshape(PARTICLES, PIX)
    sketch = jnp.dot(corrected.astype(jnp.float32), test_matrix.astype(jnp.float32), preferred_element_type=jnp.float32)
    gram_matrix = jnp.dot(sketch.T, sketch, precision=lax.Precision.HIGHEST)
    factor_low = jnp.linalg.cholesky(gram_matrix)
    range_basis = lax.linalg.triangular_solve(factor_low, sketch, left_side=False, lower=True, transpose_a=True).astype(jnp.bfloat16)
    projection = jnp.dot(corrected.T.astype(jnp.float32), range_basis.astype(jnp.float32), preferred_element_type=jnp.float32)
    return (range_basis, projection)
```

```python
import functools
import math

import jax
import jax.numpy as jnp
from jax import lax
from jax.experimental import pallas as pl
from jax.experimental.pallas import tpu as pltpu
from jax.sharding import PartitionSpec as P

AMPLITUDE = 0.1
WIENER = 0.1
F32 = jnp.float32
BF16 = jnp.bfloat16
HIGHEST = lax.Precision.HIGHEST


def real_tables(length):
    rows = jnp.arange(length, dtype=jnp.int32)
    product = rows[:, None] * rows[None, :] % length
    angles = 2.0 * math.pi / length * product.astype(F32)
    packed = jnp.where(rows[None, :] <= length // 2, jnp.cos(angles), jnp.sin(angles))
    return packed.astype(BF16)


def filter_table(defocus_values, length):
    index = jnp.arange(length, dtype=jnp.int32)
    freq = jnp.where(index < length // 2, index, index - length).astype(F32) / length
    phase = jnp.pi * defocus_values[:, None] * (freq * freq)[None, :]
    sine, cosine = lax.optimization_barrier((jnp.sin(phase), jnp.cos(phase)))
    keep = math.sqrt(1.0 - AMPLITUDE**2)
    first = (keep * sine + AMPLITUDE * cosine)[:, :, None]
    second = (keep * cosine - AMPLITUDE * sine)[:, :, None]
    contrast = -(first * cosine[:, None, :] + second * sine[:, None, :])
    wiener = (contrast / (contrast * contrast + WIENER)).astype(BF16).astype(F32)
    twice = jnp.where((index == 0) | (index == length // 2), 1.0, 2.0).astype(F32)
    return (wiener * (twice[:, None] * twice[None, :] / float(length * length))).astype(BF16)


def bits_of(size):
    return size.bit_length() - 1


def partner_of(me, mask):
    for shift in range(mask.bit_length()):
        bit = 1 << shift
        if mask & bit:
            me = me + bit * (1 - 2 * lax.rem(lax.div(me, bit), 2))
    return me


def greet(me, masks):
    barrier = pltpu.get_barrier_semaphore()
    for mask in masks:
        pl.semaphore_signal(
            barrier,
            inc=1,
            device_id={"pix": partner_of(me, mask)},
            device_id_type=pl.DeviceIdType.MESH,
        )
    pl.semaphore_wait(barrier, len(masks))


def remote(src, dst, send_sem, recv_sem, peer):
    return pltpu.make_async_remote_copy(
        src_ref=src,
        dst_ref=dst,
        send_sem=send_sem,
        recv_sem=recv_sem,
        device_id={"pix": peer},
        device_id_type=pl.DeviceIdType.MESH,
    )


def halving_orders(size):
    bits = [1 << shift for shift in range(bits_of(size))]
    if len(bits) < 3:
        return (bits, bits)
    return (bits, bits[:1] + bits[2:] + bits[1:2])


def masks_of(bits):
    if not bits:
        return [0]
    rest = masks_of(bits[1:])
    return [bits[0] | mask for mask in rest] + rest


def gathering_orders(size):
    first, second = halving_orders(size)
    return (first[::-1], second[1:][::-1] + second[:1])


def sums(bits):
    out = [0]
    for bit in bits:
        out = out + [bit | mask for mask in out]
    return out


def direct_sum(rank, size):
    return rank % (8 * size) == 0


def peers(rank, size):
    if direct_sum(rank, size):
        return list(range(1, size))
    return [1 << shift for shift in range(bits_of(size))]


def sum_gram(me, size, gram_ref, parts, arrived, send_sem, recv_sem):
    if not direct_sum(parts.shape[0] * parts.shape[1], size):
        gram_ref[...] = parts[...].reshape(gram_ref.shape)
        for stage in range(bits_of(size)):
            copy = remote(
                gram_ref,
                arrived.at[stage],
                send_sem.at[stage],
                recv_sem.at[stage],
                partner_of(me, 1 << stage),
            )
            copy.start()
            copy.wait()
            gram_ref[...] += arrived[stage]
        return
    height = parts.shape[1]
    scatter = [
        remote(
            parts.at[partner_of(me, d)],
            arrived.at[d],
            send_sem.at[d],
            recv_sem.at[d],
            partner_of(me, d),
        )
        for d in range(1, size)
    ]
    for copy in scatter:
        copy.start()
    total = parts[me]
    for d, copy in enumerate(scatter, 1):
        copy.wait_recv()
        total = total + arrived[d]
    arrived[0] = total
    own = pl.ds(pl.multiple_of(me * height, height), height)
    gather = [
        remote(
            arrived.at[0],
            gram_ref.at[own],
            send_sem.at[size + d],
            recv_sem.at[size + d],
            partner_of(me, d),
        )
        for d in range(1, size)
    ]
    for copy in gather:
        copy.start()
    gram_ref[own, :] = total
    for copy in gather:
        copy.wait_recv()
    for copy in scatter + gather:
        copy.wait_send()


def spots(me, size):
    return lax.div(me, 4), partner_of(me, 2), partner_of(me, 1)


class Gather:
    UP, DOWN, ACROSS, BESIDE = range(4)

    def __init__(self, me, size, held, send_sem, recv_sem):
        self.me, self.size, self.held = me, size, held
        self.send_sem, self.recv_sem = send_sem, recv_sem
        self.layers = size // 4
        self.z = lax.div(me, 4)
        height = held.shape[1]
        first = height * 13 // 32 // 16 * 16
        self.cuts = [(0, first), (first, first), (2 * first, height - 2 * first)]
        self.has_up = self.z + 1 < self.layers
        self.has_down = self.z >= 1
        self.across = partner_of(me, 2)
        self.beside = partner_of(me, 1)
        self.peers = {
            self.UP: me + 4,
            self.DOWN: me - 4,
            self.ACROSS: self.across,
            self.BESIDE: self.beside,
        }

    def copy(self, owner, part, dest):
        start, rows = self.cuts[part]
        piece = self.held.at[owner, pl.ds(start, rows)]
        return remote(
            piece,
            piece,
            self.send_sem.at[dest, owner, part],
            self.recv_sem.at[owner, part],
            self.peers[dest],
        )

    def greet(self):
        barrier = pltpu.get_barrier_semaphore()

        def signal(dest):
            pl.semaphore_signal(
                barrier,
                inc=1,
                device_id={"pix": self.peers[dest]},
                device_id_type=pl.DeviceIdType.MESH,
            )

        signal(self.ACROSS)
        signal(self.BESIDE)
        pl.when(self.has_up)(lambda: signal(self.UP))
        pl.when(self.has_down)(lambda: signal(self.DOWN))
        pl.semaphore_wait(barrier, 2)
        pl.when(self.has_up)(lambda: pl.semaphore_wait(barrier, 1))
        pl.when(self.has_down)(lambda: pl.semaphore_wait(barrier, 1))

    def moves(self):
        out = []
        for part in (2, 0, 1):
            out += [
                (None, self.me, part, self.ACROSS),
                (self.has_up, self.me, part, self.UP),
                (self.has_down, self.me, part, self.DOWN),
                (None, self.me, part, self.BESIDE),
            ]
        return out

    def begin(self, copies):
        for condition, owner, part, dest in copies:
            if condition is None:
                self.copy(owner, part, dest).start()
            else:
                pl.when(condition)(lambda o=owner, p=part, d=dest: self.copy(o, p, d).start())

    def finish(self, copies):
        for condition, owner, part, dest in copies:
            if condition is None:
                self.copy(owner, part, dest).wait_send()
            else:
                pl.when(condition)(lambda o=owner, p=part, d=dest: self.copy(o, p, d).wait_send())

    def arrived(self, owner, part):
        self.copy(owner, part, self.BESIDE).wait_recv()

    def sent_for(self, event):
        kind, step, part = event
        if kind == "across":
            if part == 2:
                return None, self.across, [
                    (self.has_up, self.UP),
                    (self.has_down, self.DOWN),
                    (None, self.BESIDE),
                ]
            return None, None, None
        return None

    def events(self):
        up, down = (self.has_up, self.UP), (self.has_down, self.DOWN)
        across, beside = (None, self.ACROSS), (None, self.BESIDE)
        out = [[(None, self.across, 2, [up, down, beside])]]

        def along(step, part, side):
            start = self.me if side == 0 else self.across
            extra = [across] if part < 2 else []
            below = (self.z >= step, start - 4 * step, part, [up] + extra + [beside])
            above = (
                self.z + step < self.layers,
                start + 4 * step,
                part,
                [down] + extra + [beside],
            )
            return [below, above]

        def over(step, part):
            if step == 0:
                return [(None, self.across, part, [beside])]
            return [
                (self.z >= step, self.across - 4 * step, part, [beside]),
                (self.z + step < self.layers, self.across + 4 * step, part, [beside]),
            ]

        for step in range(1, self.layers):
            out.append(along(step, 0, 0) + along(step, 2, 0) + over(step - 1, 0))
            out.append(along(step, 1, 0) + along(step, 2, 1) + over(step - 1, 1))
        out.append(over(self.layers - 1, 0))
        out.append(over(self.layers - 1, 1))
        return out

    def handle(self, events):
        for condition, owner, part, dests in events:

            def act(owner=owner, part=part, dests=dests):
                self.arrived(owner, part)
                self.begin([(c, owner, part, d) for c, d in dests])

            if condition is None:
                act()
            else:
                pl.when(condition)(act)

    def close(self):
        self.finish(self.moves())
        for events in self.events():
            for condition, owner, part, dests in events:

                def act(owner=owner, part=part, dests=dests):
                    self.finish([(c, owner, part, d) for c, d in dests])

                if condition is None:
                    act()
                else:
                    pl.when(condition)(act)

    def await_beside(self, owner):
        for part in range(3):
            self.arrived(owner, part)


def sketch_kernel(
    size,
    count,
    stride,
    group_ref,
    live_ref,
    image_hbm,
    matrix_hbm,
    filters,
    pair_ref,
    pair_t_ref,
    out_ref,
    sketch_ref,
    gram_ref,
    images_ref,
    turned,
    held,
    summed,
    parts,
    arrived,
    load_sem,
    own_sem,
    send_sem,
    recv_sem,
    sum_send_sem,
    sum_recv_sem,
):
    me = lax.axis_index("pix")
    step = pl.program_id(0)
    length = out_ref.shape[0]
    steps = out_ref.shape[1] // count
    pairs = count // 2
    base = step * count
    gather = Gather(me, size, held, send_sem, recv_sem)
    events = gather.events()

    def load(i):
        rows = pl.ds(i * count, count)
        return pltpu.make_async_copy(image_hbm.at[rows], images_ref.at[rows], load_sem.at[i])

    @pl.when(step == 0)
    def _():
        own = pltpu.make_async_copy(matrix_hbm, held.at[me], own_sem)
        own.start()
        for i in range(steps):
            load(i).start()
        barrier = pltpu.get_barrier_semaphore()
        for mask in range(1, size):
            pl.semaphore_signal(
                barrier,
                inc=1,
                device_id={"pix": partner_of(me, mask)},
                device_id_type=pl.DeviceIdType.MESH,
            )
        pl.semaphore_wait(barrier, size - 1)
        own.wait()
        gather.begin(gather.moves())

    early = min(len(events), steps - 2)
    for i in range(early):

        @pl.when(step == i + 1)
        def _(i=i):
            gather.handle(events[i])

    load(step).wait()

    def side_by_side(values):
        return jnp.concatenate(values, axis=1)

    def product(left, right):
        return jnp.dot(left, right, preferred_element_type=F32)

    def quads(left, right):
        width = 2 * length
        return jnp.concatenate(
            [product(left, right[i : i + width]) for i in range(0, pairs * length, width)], axis=0
        )

    images = jnp.concatenate(
        [
            side_by_side([images_ref[base + 2 * i], images_ref[base + 2 * i + 1]])
            for i in range(pairs)
        ],
        axis=0,
    )
    weights = jnp.concatenate(
        [
            side_by_side(
                [filters[group_ref[base + 2 * i]], filters[group_ref[base + 2 * i + 1]]]
            )
            for i in range(pairs)
        ],
        axis=0,
    )
    rows = product(images, pair_ref[...]).astype(BF16)
    spectrum = quads(pair_t_ref[...], rows)
    kept = (spectrum * weights.astype(F32)).astype(BF16)
    back = product(kept, pair_t_ref[...]).astype(BF16)
    result = quads(pair_ref[...], back)
    for i in range(count):
        tall, wide = i // 2 * length, i % 2 * length
        turned[pl.ds(i, length, stride=stride), :] = result[
            tall : tall + length, wide : wide + length
        ]
    slot = base + lax.broadcasted_iota(jnp.int32, (1, count, 1), 1)
    values = turned[...].reshape(length, stride, length)[:, :count]
    out_ref[:, pl.ds(pl.multiple_of(base, count), count), :] = jnp.where(
        slot < live_ref[0], values, 0.0
    ).astype(BF16)

    @pl.when(step == steps - 1)
    def _():
        lines = length // size

        def add(owner):
            left = side_by_side([out_ref[owner * lines + line] for line in range(lines)])
            sketch_ref[...] += product(left, held[owner])

        def whole_chip(owner):
            add(owner)
            other = partner_of(owner, 1)
            gather.await_beside(other)
            add(other)

        def both_ways(distance, start):
            pl.when(gather.z >= distance)(lambda: whole_chip(start - 4 * distance))
            pl.when(gather.z + distance < gather.layers)(
                lambda: whole_chip(start + 4 * distance)
            )

        sketch_ref[...] = jnp.zeros_like(sketch_ref)
        done = early
        whole_chip(me)
        ready = 3
        for distance in range(gather.layers):
            while done < len(events) and done < 2 * distance + 1:
                gather.handle(events[done])
                done += 1
            if distance:
                both_ways(distance, me)
            while done < len(events) and done < 2 * distance + 3:
                gather.handle(events[done])
                done += 1
            if distance:
                both_ways(distance, gather.across)
            else:
                whole_chip(gather.across)
        sketch = sketch_ref[...]
        gram = lax.dot_general(
            sketch, sketch, (((0,), (0,)), ((), ())), precision=HIGHEST, preferred_element_type=F32
        )
        parts[...] = gram.reshape(parts.shape)
        sum_gram(me, size, summed, parts, arrived, sum_send_sem, sum_recv_sem)
        gram_ref[...] = summed[...]
        gather.close()


def make_sketch(images, groups, live, defocus_values, matrix, size):
    slots, length, _ = images.shape
    height, rank = matrix.shape
    count = math.gcd(slots, 32)
    stride = count + 4
    table = real_tables(length)
    zero = jnp.zeros_like(table)
    pair = jnp.concatenate(
        [jnp.concatenate([table, zero], axis=1), jnp.concatenate([zero, table], axis=1)], axis=0
    )
    number = defocus_values.shape[0]
    if direct_sum(rank, size):
        summing = [
            pltpu.VMEM((size, rank // size, rank), F32),
            pltpu.VMEM((size, rank // size, rank), F32),
        ]
        signals = 2 * size
    else:
        summing = [
            pltpu.VMEM((1, rank, rank), F32),
            pltpu.VMEM((bits_of(size), rank, rank), F32),
        ]
        signals = bits_of(size)

    def whole(*shape):
        return pl.BlockSpec(shape, lambda i, *_: (0,) * len(shape))

    return pl.pallas_call(
        functools.partial(sketch_kernel, size, count, stride),
        out_shape=(
            jax.ShapeDtypeStruct((length, slots, length), BF16),
            jax.ShapeDtypeStruct((slots, rank), F32),
            jax.ShapeDtypeStruct((rank, rank), F32),
        ),
        grid_spec=pltpu.PrefetchScalarGridSpec(
            num_scalar_prefetch=2,
            grid=(slots // count,),
            in_specs=[
                pl.BlockSpec(memory_space=pl.ANY),
                pl.BlockSpec(memory_space=pl.ANY),
                whole(number, length, length),
                whole(2 * length, 2 * length),
                whole(2 * length, 2 * length),
            ],
            out_specs=(whole(length, slots, length), whole(slots, rank), whole(rank, rank)),
            scratch_shapes=[
                pltpu.VMEM((slots, length, length), BF16),
                pltpu.VMEM((length * stride, length), F32),
                pltpu.VMEM((size, height, rank), BF16),
                pltpu.VMEM((rank, rank), F32),
                *summing,
                pltpu.SemaphoreType.DMA((slots // count,)),
                pltpu.SemaphoreType.DMA,
                pltpu.SemaphoreType.DMA((4, size, 3)),
                pltpu.SemaphoreType.DMA((size, 3)),
                pltpu.SemaphoreType.DMA((signals,)),
                pltpu.SemaphoreType.DMA((signals,)),
            ],
        ),
        compiler_params=pltpu.CompilerParams(
            collective_id=0, has_side_effects=True, vmem_limit_bytes=56 << 20
        ),
        name="sketch",
    )(groups, live, images, matrix, filter_table(defocus_values, length), pair, pair.T)


def basis_kernel(factor_ref, sketch_ref, out_ref, turned_ref):
    rank = factor_ref.shape[0]
    row = lax.broadcasted_iota(jnp.int32, (rank, rank), 0)
    col = lax.broadcasted_iota(jnp.int32, (rank, rank), 1)
    factor = factor_ref[...]
    on_diagonal = jnp.where(row == col, factor, 0.0)
    lower = jnp.where(row > col, factor, 0.0) / jnp.sum(on_diagonal, axis=1, keepdims=True)

    def times(left, right):
        return jnp.dot(left, right, precision=HIGHEST, preferred_element_type=F32)

    def same_block(shift):
        return lax.shift_right_logical(row, shift) == lax.shift_right_logical(col, shift)

    shift = 3
    within = jnp.where(same_block(shift), lower, 0.0)
    unit = jnp.where(row == col, 1.0, 0.0).astype(F32)
    square = times(within, within)
    fourth = times(square, square)
    inverse = times(times(unit - within, unit + square), unit + fourth)
    while 1 << shift < rank:
        off = jnp.where(same_block(shift + 1) & ~same_block(shift), lower, 0.0)
        inverse = inverse - times(inverse, times(off, inverse))
        shift += 1
    inverse = inverse / jnp.sum(on_diagonal, axis=0, keepdims=True)
    basis = lax.dot_general(
        sketch_ref[...],
        inverse,
        (((1,), (1,)), ((), ())),
        precision=HIGHEST,
        preferred_element_type=F32,
    )
    out_ref[...] = basis.astype(BF16)
    turned_ref[...] = basis.T.astype(BF16)


def make_basis(factor_low, sketch):
    slots, rank = sketch.shape
    return pl.pallas_call(
        basis_kernel,
        out_shape=(
            jax.ShapeDtypeStruct((slots, rank), BF16),
            jax.ShapeDtypeStruct((rank, slots), BF16),
        ),
        name="basis",
    )(factor_low, sketch)


def project_kernel(size, basis_ref, column_ref, out_ref, held, arrived, send_sem, recv_sem):
    me = lax.axis_index("pix")
    length = column_ref.shape[0]
    rows = length // size
    part = rows // 2
    orders = halving_orders(size)
    slots = {}
    for half in range(2):
        for stage in range(len(orders[half])):
            for mask in masks_of(orders[half][stage + 1 :]):
                slots[half, stage, mask] = len(slots) % (size - 1)

    def copy_of(half, stage, mask):
        bit = orders[half][stage]
        slot = slots[half, stage, mask]
        return remote(
            held.at[half, bit | mask],
            arrived.at[half, slot],
            send_sem.at[half, slot],
            recv_sem.at[half, slot],
            partner_of(me, bit),
        )

    greet(me, [1 << shift for shift in range(bits_of(size))])
    first = orders[0][0]

    def compute(half, mask):
        start = partner_of(me, mask) * rows + half * part
        right = jnp.concatenate([column_ref[start + row] for row in range(part)], axis=1)
        held[half, mask] = jnp.dot(
            basis_ref[...], right, preferred_element_type=F32
        ).astype(BF16)

    def add(half, stage, mask):
        later = orders[half][stage + 1 :]
        copy_of(half, stage, mask).wait_recv()
        total = (
            held[half, mask].astype(F32)
            + arrived[half, slots[half, stage, mask]].astype(F32)
        )
        if later:
            held[half, mask] = total.astype(BF16)
            if mask & later[0]:
                copy_of(half, stage + 1, mask - later[0]).start()
        else:
            height = out_ref.shape[0] // 2
            out_ref[half * height : (half + 1) * height, :] = total.T

    kept = [masks_of(orders[half][1:]) for half in range(2)]
    for place in range(len(kept[0]) + 1):
        for half in range(2):
            if place < len(kept[0]):
                mask = kept[half][place]
                compute(half, first | mask)
                copy_of(half, 0, mask).start()
                compute(half, mask)
        for half in range(2):
            if place > 0:
                add(half, 0, kept[half][place - 1])
    for stage in range(1, bits_of(size)):
        for place in range(len(masks_of(orders[0][stage + 1 :]))):
            for half in range(2):
                add(half, stage, masks_of(orders[half][stage + 1 :])[place])
    for half in range(2):
        for stage in range(bits_of(size)):
            for mask in masks_of(orders[half][stage + 1 :]):
                copy_of(half, stage, mask).wait_send()


def project(columns, basis_t, size):
    length, slots, _ = columns.shape
    rank = basis_t.shape[0]
    width = length * length // size
    return pl.pallas_call(
        functools.partial(project_kernel, size),
        out_shape=jax.ShapeDtypeStruct((width, rank), F32),
        in_specs=[pl.BlockSpec(memory_space=pltpu.VMEM)] * 2,
        out_specs=pl.BlockSpec(memory_space=pltpu.VMEM),
        scratch_shapes=[
            pltpu.VMEM((2, size, rank, width // 2), BF16),
            pltpu.VMEM((2, size - 1, rank, width // 2), BF16),
            pltpu.SemaphoreType.DMA((2, size - 1)),
            pltpu.SemaphoreType.DMA((2, size - 1)),
        ],
        compiler_params=pltpu.CompilerParams(
            collective_id=1, has_side_effects=True, vmem_limit_bytes=48 << 20
        ),
        name="project",
    )(basis_t, columns)


def per_device(particle_images, defocus_group, live_counts, defocus_values, test_matrix):
    size = lax.axis_size("pix")
    columns, sketch, gram = make_sketch(
        particle_images, defocus_group, live_counts, defocus_values, test_matrix, size
    )
    factor_low = jnp.linalg.cholesky(gram)
    range_basis, basis_t = make_basis(factor_low, sketch)
    return (range_basis, project(columns, basis_t, size))


def solution(mesh):
    placed = (
        P(("grp", "pix"), None, None),
        P(("grp", "pix")),
        P(("grp", "pix")),
        P("grp"),
        P(("grp", "pix"), None),
    )
    return jax.shard_map(
        per_device,
        mesh=mesh,
        in_specs=placed,
        out_specs=(P(("grp", "pix"), None), P(("grp", "pix"), None)),
        check_vma=False,
    )
```

```python
import functools
import math

import jax
import jax.numpy as jnp
import ml_dtypes
import numpy as np
from jax import lax
from jax.experimental import pallas as pl
from jax.experimental.pallas import tpu as pltpu
from jax.sharding import PartitionSpec as P

AMPLITUDE = 0.1
WIENER = 0.1
F32 = jnp.float32
BF16 = jnp.bfloat16
HIGHEST = lax.Precision.HIGHEST


def real_tables(length):
    rows = np.arange(length)
    angles = 2.0 * math.pi / length * (rows[:, None] * rows[None, :] % length)
    packed = np.where(rows[None, :] <= length // 2, np.cos(angles), np.sin(angles))
    return jnp.asarray(packed.astype(np.float32)).astype(BF16)


def pair_tables(length):
    rows = np.arange(length)
    angles = 2.0 * math.pi / length * (rows[:, None] * rows[None, :] % length)
    packed = np.where(rows[None, :] <= length // 2, np.cos(angles), np.sin(angles))
    pair = np.zeros((2 * length, 2 * length), np.float32)
    pair[:length, :length] = packed
    pair[length:, length:] = packed
    pair = pair.astype(ml_dtypes.bfloat16)
    return jnp.asarray(pair), jnp.asarray(np.ascontiguousarray(pair.T))


def filter_table(defocus_values, length):
    index = jnp.arange(length, dtype=jnp.int32)
    freq = jnp.where(index < length // 2, index, index - length).astype(F32) / length
    phase = jnp.pi * defocus_values[:, None] * (freq * freq)[None, :]
    sine, cosine = lax.optimization_barrier((jnp.sin(phase), jnp.cos(phase)))
    keep = math.sqrt(1.0 - AMPLITUDE**2)
    first = (keep * sine + AMPLITUDE * cosine)[:, :, None]
    second = (keep * cosine - AMPLITUDE * sine)[:, :, None]
    contrast = -(first * cosine[:, None, :] + second * sine[:, None, :])
    wiener = (contrast / (contrast * contrast + WIENER)).astype(BF16).astype(F32)
    twice = jnp.where((index == 0) | (index == length // 2), 1.0, 2.0).astype(F32)
    return (wiener * (twice[:, None] * twice[None, :] / float(length * length))).astype(BF16)


def bits_of(size):
    return size.bit_length() - 1


def partner_of(me, mask):
    for shift in range(mask.bit_length()):
        bit = 1 << shift
        if mask & bit:
            me = me + bit * (1 - 2 * lax.rem(lax.div(me, bit), 2))
    return me


def greet(me, masks):
    barrier = pltpu.get_barrier_semaphore()
    for mask in masks:
        pl.semaphore_signal(
            barrier,
            inc=1,
            device_id={"pix": partner_of(me, mask)},
            device_id_type=pl.DeviceIdType.MESH,
        )
    pl.semaphore_wait(barrier, len(masks))


def remote(src, dst, send_sem, recv_sem, peer):
    return pltpu.make_async_remote_copy(
        src_ref=src,
        dst_ref=dst,
        send_sem=send_sem,
        recv_sem=recv_sem,
        device_id={"pix": peer},
        device_id_type=pl.DeviceIdType.MESH,
    )


def halving_orders(size):
    bits = [1 << shift for shift in range(bits_of(size))]
    if len(bits) < 3:
        return (bits, bits)
    return (bits, bits[:1] + bits[2:] + bits[1:2])


def masks_of(bits):
    if not bits:
        return [0]
    rest = masks_of(bits[1:])
    return [bits[0] | mask for mask in rest] + rest


def gathering_orders(size):
    first, second = halving_orders(size)
    return (first[::-1], second[1:][::-1] + second[:1])


def sums(bits):
    out = [0]
    for bit in bits:
        out = out + [bit | mask for mask in out]
    return out


def direct_sum(rank, size):
    return rank % (8 * size) == 0


def peers(rank, size):
    if direct_sum(rank, size):
        return list(range(1, size))
    return [1 << shift for shift in range(bits_of(size))]


def sum_gram(me, size, gram_ref, parts, arrived, send_sem, recv_sem):
    if not direct_sum(parts.shape[0] * parts.shape[1], size):
        gram_ref[...] = parts[...].reshape(gram_ref.shape)
        for stage in range(bits_of(size)):
            copy = remote(
                gram_ref,
                arrived.at[stage],
                send_sem.at[stage],
                recv_sem.at[stage],
                partner_of(me, 1 << stage),
            )
            copy.start()
            copy.wait()
            gram_ref[...] += arrived[stage]
        return
    height = parts.shape[1]
    scatter = [
        remote(
            parts.at[partner_of(me, d)],
            arrived.at[d],
            send_sem.at[d],
            recv_sem.at[d],
            partner_of(me, d),
        )
        for d in range(1, size)
    ]
    for copy in scatter:
        copy.start()
    total = parts[me]
    for d, copy in enumerate(scatter, 1):
        copy.wait_recv()
        total = total + arrived[d]
    arrived[0] = total
    own = pl.ds(pl.multiple_of(me * height, height), height)
    gather = [
        remote(
            arrived.at[0],
            gram_ref.at[own],
            send_sem.at[size + d],
            recv_sem.at[size + d],
            partner_of(me, d),
        )
        for d in range(1, size)
    ]
    for copy in gather:
        copy.start()
    gram_ref[own, :] = total
    for copy in gather:
        copy.wait_recv()
    for copy in scatter + gather:
        copy.wait_send()


class Gather:
    UP, DOWN, ACROSS, BESIDE = range(4)

    def __init__(self, me, size, held, send_sem, recv_sem):
        self.me, self.size, self.held = me, size, held
        self.send_sem, self.recv_sem = send_sem, recv_sem
        self.layers = size // 4
        self.z = lax.div(me, 4)
        height = held.shape[1]
        first = height * 13 // 32 // 16 * 16
        self.cuts = [(0, first), (first, first), (2 * first, height - 2 * first)]
        self.has_up = self.z + 1 < self.layers
        self.has_down = self.z >= 1
        self.across = partner_of(me, 2)
        self.beside = partner_of(me, 1)
        self.peers = {
            self.UP: me + 4,
            self.DOWN: me - 4,
            self.ACROSS: self.across,
            self.BESIDE: self.beside,
        }

    def copy(self, owner, part, dest):
        start, rows = self.cuts[part]
        piece = self.held.at[owner, pl.ds(start, rows)]
        return remote(
            piece,
            piece,
            self.send_sem.at[dest, owner, part],
            self.recv_sem.at[owner, part],
            self.peers[dest],
        )

    def greet(self):
        barrier = pltpu.get_barrier_semaphore()

        def signal(dest):
            pl.semaphore_signal(
                barrier,
                inc=1,
                device_id={"pix": self.peers[dest]},
                device_id_type=pl.DeviceIdType.MESH,
            )

        signal(self.ACROSS)
        signal(self.BESIDE)
        pl.when(self.has_up)(lambda: signal(self.UP))
        pl.when(self.has_down)(lambda: signal(self.DOWN))
        neighbours = jnp.minimum(self.z, 1) + jnp.minimum(self.layers - 1 - self.z, 1)
        pl.semaphore_wait(barrier, 2 + neighbours)

    def moves(self):
        out = []
        for part in (2, 0, 1):
            out += [
                (None, self.me, part, self.ACROSS),
                (self.has_up, self.me, part, self.UP),
                (self.has_down, self.me, part, self.DOWN),
                (None, self.me, part, self.BESIDE),
            ]
        return out

    def begin(self, copies):
        for condition, owner, part, dest in copies:
            if condition is None:
                self.copy(owner, part, dest).start()
            else:
                pl.when(condition)(lambda o=owner, p=part, d=dest: self.copy(o, p, d).start())

    def finish(self, copies):
        for condition, owner, part, dest in copies:
            if condition is None:
                self.copy(owner, part, dest).wait_send()
            else:
                pl.when(condition)(lambda o=owner, p=part, d=dest: self.copy(o, p, d).wait_send())

    def arrived(self, owner, part):
        self.copy(owner, part, self.BESIDE).wait_recv()

    def events(self):
        up, down = (self.has_up, self.UP), (self.has_down, self.DOWN)
        across, beside = (None, self.ACROSS), (None, self.BESIDE)
        out = [[(None, self.across, 2, [up, down, beside])]]

        def along(step, part, side):
            start = self.me if side == 0 else self.across
            extra = [across] if part < 2 else []
            below = (self.z >= step, start - 4 * step, part, [up] + extra + [beside])
            above = (
                self.z + step < self.layers,
                start + 4 * step,
                part,
                [down] + extra + [beside],
            )
            return [below, above]

        def over(step, part):
            if step == 0:
                return [(None, self.across, part, [beside])]
            return [
                (self.z >= step, self.across - 4 * step, part, [beside]),
                (self.z + step < self.layers, self.across + 4 * step, part, [beside]),
            ]

        for step in range(1, self.layers):
            out.append(along(step, 0, 0) + along(step, 2, 0) + over(step - 1, 0))
            out.append(along(step, 1, 0) + along(step, 2, 1) + over(step - 1, 1))
        out.append(over(self.layers - 1, 0))
        out.append(over(self.layers - 1, 1))
        return out

    def handle(self, events):
        for condition, owner, part, dests in events:

            def act(owner=owner, part=part, dests=dests):
                self.arrived(owner, part)
                self.begin([(c, owner, part, d) for c, d in dests])

            if condition is None:
                act()
            else:
                pl.when(condition)(act)

    def close(self):
        self.finish(self.moves())
        for events in self.events():
            for condition, owner, part, dests in events:

                def act(owner=owner, part=part, dests=dests):
                    self.finish([(c, owner, part, d) for c, d in dests])

                if condition is None:
                    act()
                else:
                    pl.when(condition)(act)

    def await_beside(self, owner):
        for part in range(3):
            self.arrived(owner, part)


class Scatter:
    def __init__(self, gather, work, inbox, send_sem, recv_sem):
        self.gather = gather
        self.work, self.inbox = work, inbox
        self.send_sem, self.recv_sem = send_sem, recv_sem
        rank = work.shape[1]
        last = max(rank // 8 // 16 * 16, 16)
        first = (rank - last + 31) // 32 * 16
        self.cuts = [(0, first), (first, rank - last - first), (rank - last, last), (0, rank)]
        self.sent = []

    def copy(self, owner, part, dest):
        start, rows = self.cuts[part]
        slot = lax.div(owner, 2)
        place = part % 3
        return remote(
            self.work.at[owner, pl.ds(start, rows)],
            self.inbox.at[dest, slot, pl.ds(start, rows)],
            self.send_sem.at[dest, slot, place],
            self.recv_sem.at[dest, slot, place],
            self.gather.peers[dest],
        )

    def send(self, owner, part, dest, conditions):
        self.copy(owner, part, dest).start()
        self.sent.append((conditions, owner, part, dest))

    def take(self, owner, part, dest):
        start, rows = self.cuts[part]
        self.copy(owner, part, dest).wait_recv()
        piece = self.work.at[owner, pl.ds(start, rows)]
        got = self.inbox[dest, lax.div(owner, 2), pl.ds(start, rows)]
        piece[...] = (piece[...].astype(F32) + got.astype(F32)).astype(BF16)

    def close(self):
        for conditions, owner, part, dest in self.sent:
            wait = lambda o=owner, p=part, d=dest: self.copy(o, p, d).wait_send()
            for condition in conditions:
                wait = lambda c=condition, w=wait: pl.when(c)(w)
            wait()


def splat(values, row, col):
    return jnp.broadcast_to(values[row : row + 1, col : col + 1], values.shape)


def factor_step(block, left_ref, right_ref, inverse_ref):
    size = left_ref.shape[0]
    top, side = left_ref[0:8, :], right_ref[0:8, :]
    cell = {(r, c): splat(top, r, c) for r in range(8) for c in range(r + 1)}
    turn = {}
    for c in range(8):
        pivot = cell[c, c]
        guess = lax.rsqrt(pivot)
        scale = guess * (1.5 - 0.5 * pivot * guess * guess)
        turn[c, c] = scale
        for r in range(c + 1, 8):
            cell[r, c] = cell[r, c] * scale
        for r in range(c + 1, 8):
            for k in range(c + 1, r + 1):
                cell[r, k] = cell[r, k] - cell[r, c] * cell[k, c]
    for c in range(8):
        for r in range(c + 1, 8):
            total = cell[r, c] * turn[c, c]
            for k in range(c + 1, r):
                total = total + cell[r, k] * turn[k, c]
            turn[r, c] = -total * turn[r, r]
    row = lax.broadcasted_iota(jnp.int32, top.shape, 0)
    lane = lax.broadcasted_iota(jnp.int32, top.shape, 1)
    upper, lower = jnp.zeros_like(top), jnp.zeros_like(side)
    for c in range(8):
        weight = jnp.zeros_like(top)
        for r in range(c, 8):
            weight = jnp.where(row == r, turn[r, c], weight)
        upper = upper + weight * top[c : c + 1, :]
        lower = lower + weight * side[c : c + 1, :]
    inverse_ref[pl.ds(pl.multiple_of(8 * block, 8), 8), :] = lower
    upper = jnp.where((lane >= row) & (lane < size - 8 * block), upper, 0.0)
    both = jnp.concatenate([upper, lower], axis=1)
    change = lax.dot_general(
        upper, both, (((0,), (0,)), ((), ())), precision=HIGHEST, preferred_element_type=F32
    )
    left = pltpu.roll(left_ref[...] - change[:, :size], size - 8, 1)
    left_ref[0 : size - 8, :] = left[8:]
    left_ref[size - 8 : size, :] = jnp.zeros_like(top)
    right = right_ref[...] - change[:, size:]
    right_ref[0 : size - 8, :] = right[8:]
    right_ref[size - 8 : size, :] = jnp.zeros_like(side)


class GramSum:
    def __init__(self, me, size, gram_ref, parts, arrived, send_sem, recv_sem):
        self.me, self.size, self.gram_ref = me, size, gram_ref
        self.parts, self.arrived = parts, arrived
        self.send_sem, self.recv_sem = send_sem, recv_sem
        self.direct = direct_sum(parts.shape[0] * parts.shape[1], size)

    def scatter(self, d):
        peer = partner_of(self.me, d)
        return remote(
            self.parts.at[peer],
            self.arrived.at[d],
            self.send_sem.at[d],
            self.recv_sem.at[d],
            peer,
        )

    def gather(self, d):
        height = self.parts.shape[1]
        own = pl.ds(pl.multiple_of(self.me * height, height), height)
        return remote(
            self.arrived.at[0],
            self.gram_ref.at[own],
            self.send_sem.at[self.size + d],
            self.recv_sem.at[self.size + d],
            partner_of(self.me, d),
        )

    def start(self):
        if self.direct:
            for d in range(1, self.size):
                self.scatter(d).start()

    def turn(self):
        if not self.direct:
            sum_gram(
                self.me,
                self.size,
                self.gram_ref,
                self.parts,
                self.arrived,
                self.send_sem,
                self.recv_sem,
            )
            return
        total = self.parts[self.me]
        for d in range(1, self.size):
            self.scatter(d).wait_recv()
            total = total + self.arrived[d]
        self.arrived[0] = total
        for d in range(1, self.size):
            self.gather(d).start()
        height = self.parts.shape[1]
        self.gram_ref[pl.ds(pl.multiple_of(self.me * height, height), height), :] = total

    def finish(self):
        if self.direct:
            for d in range(1, self.size):
                self.gather(d).wait_recv()

    def close(self):
        if self.direct:
            for d in range(1, self.size):
                self.scatter(d).wait_send()
                self.gather(d).wait_send()


def whole_kernel(
    size,
    count,
    stride,
    group_ref,
    live_ref,
    image_hbm,
    matrix_hbm,
    filters,
    pair_ref,
    pair_t_ref,
    basis_ref,
    out_ref,
    growth_ref,
    images_ref,
    turned,
    columns,
    held,
    sketch_ref,
    gram_ref,
    parts,
    arrived,
    left_ref,
    right_ref,
    inverse_ref,
    work,
    inbox,
    load_sem,
    own_sem,
    send_sem,
    recv_sem,
    sum_send_sem,
    sum_recv_sem,
    back_send_sem,
    back_recv_sem,
):
    me = lax.axis_index("pix")
    step = pl.program_id(0)
    length, slots, _ = columns.shape
    rank = sketch_ref.shape[1]
    steps = slots // count
    pairs = count // 2
    base = step * count
    gather = Gather(me, size, held, send_sem, recv_sem)
    events = gather.events()

    def load(i):
        rows = pl.ds(i * count, count)
        return pltpu.make_async_copy(image_hbm.at[rows], images_ref.at[rows], load_sem.at[i])

    @pl.when(step == 0)
    def _():
        own = pltpu.make_async_copy(matrix_hbm, held.at[me], own_sem)
        own.start()
        for i in range(steps):
            load(i).start()
        gather.greet()
        own.wait()
        gather.begin(gather.moves())

    early = min(len(events), steps - 2)
    for i in range(early):

        @pl.when(step == i + 1)
        def _(i=i):
            gather.handle(events[i])

    load(step).wait()

    def side_by_side(values):
        return jnp.concatenate(values, axis=1)

    def product(left, right):
        return jnp.dot(left, right, preferred_element_type=F32)

    def quads(left, right):
        width = 2 * length
        return jnp.concatenate(
            [product(left, right[i : i + width]) for i in range(0, pairs * length, width)], axis=0
        )

    images = jnp.concatenate(
        [
            side_by_side([images_ref[base + 2 * i], images_ref[base + 2 * i + 1]])
            for i in range(pairs)
        ],
        axis=0,
    )
    weights = jnp.concatenate(
        [
            side_by_side(
                [filters[group_ref[base + 2 * i]], filters[group_ref[base + 2 * i + 1]]]
            )
            for i in range(pairs)
        ],
        axis=0,
    )
    rows = product(images, pair_ref[...]).astype(BF16)
    spectrum = quads(pair_t_ref[...], rows)
    kept = (spectrum * weights.astype(F32)).astype(BF16)
    back = product(kept, pair_t_ref[...]).astype(BF16)
    result = quads(pair_ref[...], back)
    for i in range(count):
        tall, wide = i // 2 * length, i % 2 * length
        turned[pl.ds(i, length, stride=stride), :] = result[
            tall : tall + length, wide : wide + length
        ]
    slot = base + lax.broadcasted_iota(jnp.int32, (1, count, 1), 1)
    values = turned[...].reshape(length, stride, length)[:, :count]
    columns[:, pl.ds(pl.multiple_of(base, count), count), :] = jnp.where(
        slot < live_ref[0], values, 0.0
    ).astype(BF16)

    @pl.when(step == steps - 1)
    def _():
        lines = length // size
        layers = gather.layers
        z = gather.z

        def pixels(owner):
            return side_by_side([columns[owner * lines + line] for line in range(lines)])

        def whole_chip(owner):
            other = partner_of(owner, 1)
            gather.await_beside(other)
            sketch_ref[...] += product(pixels(owner), held[owner]) + product(
                pixels(other), held[other]
            )

        def both_ways(distance, act):
            pl.when(z >= distance)(lambda: act(-4 * distance, False))
            pl.when(z + distance < layers)(lambda: act(4 * distance, True))

        sketch_ref[...] = jnp.zeros_like(sketch_ref)
        done = early
        whole_chip(me)
        for distance in range(layers):
            while done < len(events) and done < 2 * distance + 1:
                gather.handle(events[done])
                done += 1
            if distance:
                both_ways(distance, lambda start, _: whole_chip(me + start))
            while done < len(events) and done < 2 * distance + 3:
                gather.handle(events[done])
                done += 1
            if distance:
                both_ways(distance, lambda start, _: whole_chip(gather.across + start))
            else:
                whole_chip(gather.across)
        sketch = sketch_ref[...]
        sketch_t = sketch.T.astype(BF16)
        scatter = Scatter(gather, work, inbox, back_send_sem, back_recv_sem)
        total = GramSum(me, size, gram_ref, parts, arrived, sum_send_sem, sum_recv_sem)
        up, down, across, beside = gather.UP, gather.DOWN, gather.ACROSS, gather.BESIDE

        def ways(distance):
            out = []
            for upwards in (False, True) if distance else (True,):
                own = me + (4 * distance if upwards else -4 * distance)
                other = partner_of(own, 2)
                there = z + distance < layers if upwards else z >= distance
                given = [there] if distance else []
                out.append((given, upwards, own, other, partner_of(own, 1), partner_of(other, 1)))
            return out

        def run(given, act):
            pl.when(given[0])(act) if given else act()

        def compute(distance):
            for given, upwards, own, other, own_beside, other_beside in ways(distance):

                def act():
                    for owner, aside in ((other, other_beside), (own, own_beside)):
                        work[aside] = product(sketch_t, pixels(aside)).astype(BF16)
                        scatter.send(aside, 3, beside, given)
                        work[owner] = product(sketch_t, pixels(owner)).astype(BF16)

                run(given, act)

        def onward(owner, part, upwards, given):
            way, ahead = (up, gather.has_down) if upwards else (down, gather.has_up)
            pl.when(ahead)(lambda: scatter.take(owner, part, way))
            scatter.send(owner, part, way, given)

        def chip_sum(distance):
            for given, upwards, own, other, _, _ in ways(distance):

                def act():
                    scatter.take(other, 3, beside)
                    for part in range(2):
                        scatter.send(other, part, across, given)
                    scatter.take(own, 3, beside)
                    if distance:
                        onward(other, 2, upwards, given)
                        onward(own, 2, upwards, given)

                run(given, act)

        def along(distance, part):
            for given, upwards, own, _, _, _ in ways(distance):

                def act():
                    scatter.take(own, part, across)
                    if distance:
                        onward(own, part, upwards, given)

                run(given, act)

        def last(owner, part):
            pl.when(gather.has_down)(lambda: scatter.take(owner, part, up))
            pl.when(gather.has_up)(lambda: scatter.take(owner, part, down))

        compute(layers - 1)
        gram = lax.dot_general(
            sketch, sketch, (((0,), (0,)), ((), ())), precision=HIGHEST, preferred_element_type=F32
        )
        parts[...] = gram.reshape(parts.shape)
        total.start()
        for distance in range(layers - 1, 0, -1):
            compute(distance - 1)
            chip_sum(distance)
        chip_sum(0)
        total.turn()
        along(layers - 1, 0)
        along(layers - 1, 1)
        total.finish()
        unit = lax.broadcasted_iota(jnp.int32, (rank, rank), 0) == lax.broadcasted_iota(
            jnp.int32, (rank, rank), 1
        )
        left_ref[...] = gram_ref[...]
        right_ref[...] = jnp.where(unit, 1.0, 0.0)
        blocks = rank // 8
        todo = [(distance, part) for distance in range(layers - 2, 0, -1) for part in range(2)]
        for i in range(len(todo) + 1):
            lax.fori_loop(
                blocks * i // (len(todo) + 1),
                blocks * (i + 1) // (len(todo) + 1),
                lambda block, _: factor_step(block, left_ref, right_ref, inverse_ref),
                None,
            )
            if i < len(todo):
                along(*todo[i])
        inverse = inverse_ref[...]
        basis_ref[...] = lax.dot_general(
            sketch,
            inverse,
            (((1,), (1,)), ((), ())),
            precision=HIGHEST,
            preferred_element_type=F32,
        ).astype(BF16)
        scale = jnp.sqrt(jnp.sum(inverse * inverse, axis=0, keepdims=True))
        sums = jnp.dot(
            jnp.broadcast_to(scale, (8, rank)),
            jnp.abs(gram_ref[...]),
            precision=HIGHEST,
            preferred_element_type=F32,
        )
        growth_ref[...] = sums * scale
        last(gather.across, 2)
        scatter.send(gather.across, 2, across, [])
        last(me, 2)
        for part in range(2):
            along(0, part)
            last(me, part)
        scatter.take(me, 2, across)
        mine = jnp.dot(
            inverse, work[me].astype(F32), precision=HIGHEST, preferred_element_type=F32
        )
        out_ref[...] = mine.T
        gather.close()
        scatter.close()
        total.close()


def make_whole(images, groups, live, defocus_values, matrix, size):
    slots, length, _ = images.shape
    height, rank = matrix.shape
    count = math.gcd(slots, 32)
    stride = count + 4
    pair, pair_t = pair_tables(length)
    number = defocus_values.shape[0]
    if direct_sum(rank, size):
        summing = [pltpu.VMEM((size, rank // size, rank), F32)] * 2
        signals = 2 * size
    else:
        summing = [
            pltpu.VMEM((1, rank, rank), F32),
            pltpu.VMEM((bits_of(size), rank, rank), F32),
        ]
        signals = bits_of(size)

    def whole(*shape):
        return pl.BlockSpec(shape, lambda i, *_: (0,) * len(shape))

    square = pltpu.VMEM((rank, rank), F32)
    return pl.pallas_call(
        functools.partial(whole_kernel, size, count, stride),
        out_shape=(
            jax.ShapeDtypeStruct((slots, rank), BF16),
            jax.ShapeDtypeStruct((height, rank), F32),
            jax.ShapeDtypeStruct((8, rank), F32),
        ),
        grid_spec=pltpu.PrefetchScalarGridSpec(
            num_scalar_prefetch=2,
            grid=(slots // count,),
            in_specs=[
                pl.BlockSpec(memory_space=pl.ANY),
                pl.BlockSpec(memory_space=pl.ANY),
                whole(number, length, length),
                whole(2 * length, 2 * length),
                whole(2 * length, 2 * length),
            ],
            out_specs=(whole(slots, rank), whole(height, rank), whole(8, rank)),
            scratch_shapes=[
                pltpu.VMEM((slots, length, length), BF16),
                pltpu.VMEM((length * stride, length), F32),
                pltpu.VMEM((length, slots, length), BF16),
                pltpu.VMEM((size, height, rank), BF16),
                pltpu.VMEM((slots, rank), F32),
                square,
                *summing,
                square,
                square,
                square,
                pltpu.VMEM((size, rank, height), BF16),
                pltpu.VMEM((4, size // 2, rank, height), BF16),
                pltpu.SemaphoreType.DMA((slots // count,)),
                pltpu.SemaphoreType.DMA,
                pltpu.SemaphoreType.DMA((4, size, 3)),
                pltpu.SemaphoreType.DMA((size, 3)),
                pltpu.SemaphoreType.DMA((signals,)),
                pltpu.SemaphoreType.DMA((signals,)),
                pltpu.SemaphoreType.DMA((4, size // 2, 3)),
                pltpu.SemaphoreType.DMA((4, size // 2, 3)),
            ],
        ),
        compiler_params=pltpu.CompilerParams(
            collective_id=0, has_side_effects=True, vmem_limit_bytes=56 << 20
        ),
        name="whole",
    )(groups, live, images, matrix, filter_table(defocus_values, length), pair, pair_t)


def sketch_kernel(
    size,
    group_ref,
    live_ref,
    image_ref,
    matrix_ref,
    filters,
    pair_ref,
    pair_t_ref,
    table_ref,
    table_t_ref,
    out_ref,
    sketch_ref,
    gram_ref,
    turned,
    held,
    summed,
    parts,
    arrived,
    send_sem,
    recv_sem,
    sum_send_sem,
    sum_recv_sem,
):
    me = lax.axis_index("pix")
    step = pl.program_id(0)
    steps = out_ref.shape[1] // image_ref.shape[0]
    count, length, _ = image_ref.shape
    pairs = count // 2
    base = step * count
    orders = gathering_orders(size)
    stages = bits_of(size)
    height = matrix_ref.shape[0] // 2

    def copy_of(half, stage, mask):
        bit = orders[half][stage]
        slot = (bit | mask) - 1
        return remote(
            held.at[half, mask],
            held.at[half, bit | mask],
            send_sem.at[half, slot],
            recv_sem.at[half, slot],
            partner_of(me, bit),
        )

    def receive(stage, half, mask):
        copy_of(half, stage, mask).wait_recv()
        for later in range(stage + 1, stages):
            copy_of(half, later, orders[half][stage] | mask).start()

    @pl.when(step == 0)
    def _():
        greet(me, peers(gram_ref.shape[0], size))
        for half in range(2):
            held[half, 0] = matrix_ref[half * height : (half + 1) * height, :]
        for stage in range(stages):
            for half in range(2):
                copy_of(half, stage, 0).start()

    early = min(2, stages)
    for stage in range(early):

        @pl.when(step == steps * (5 + 6 * stage) // 16)
        def _(stage=stage):
            for place in range(1 << stage):
                for half in range(2):
                    receive(stage, half, sums(orders[half][:stage])[place])

    def side_by_side(values):
        return jnp.concatenate(values, axis=1)

    def stacked(wide):
        return jnp.concatenate(
            [wide[:, 2 * length * i : 2 * length * (i + 1)] for i in range(pairs)], axis=0
        )

    def unstacked(tall):
        return side_by_side([tall[length * i : length * (i + 1)] for i in range(pairs)])

    images = jnp.concatenate(
        [side_by_side([image_ref[2 * i], image_ref[2 * i + 1]]) for i in range(pairs)], axis=0
    )
    rows = jnp.dot(images, pair_ref[...], preferred_element_type=F32).astype(BF16)
    spectrum = jnp.dot(table_t_ref[...], unstacked(rows), preferred_element_type=F32)
    weights = side_by_side([filters[group_ref[base + i]] for i in range(count)])
    kept = (spectrum * weights.astype(F32)).astype(BF16)
    back = jnp.dot(stacked(kept), pair_t_ref[...], preferred_element_type=F32).astype(BF16)
    result = jnp.dot(table_ref[...], unstacked(back), preferred_element_type=F32)
    for i in range(count):
        turned[pl.ds(i, length, stride=count), :] = result[:, i * length : (i + 1) * length]
    slot = base + lax.broadcasted_iota(jnp.int32, (1, count, 1), 1)
    values = turned[...].reshape(length, count, length)
    out_ref[:, pl.ds(pl.multiple_of(base, count), count), :] = jnp.where(
        slot < live_ref[0], values, 0.0
    ).astype(BF16)

    @pl.when(step == steps - 1)
    def _():
        lines = length // size
        part = lines // 2

        def term(half, mask):
            start = partner_of(me, mask) * lines + half * part
            left = side_by_side([out_ref[start + line] for line in range(part)])
            return jnp.dot(left, held[half, mask], preferred_element_type=F32)

        sketch_ref[...] = jnp.zeros_like(sketch_ref)
        for half in range(2):
            for mask in sums(orders[half][:early]):
                sketch_ref[...] += term(half, mask)
        for stage in range(early, stages):
            for place in range(1 << stage):
                for half in range(2):
                    mask = sums(orders[half][:stage])[place]
                    receive(stage, half, mask)
                    sketch_ref[...] += term(half, orders[half][stage] | mask)
        sketch = sketch_ref[...]
        gram = lax.dot_general(
            sketch, sketch, (((0,), (0,)), ((), ())), precision=HIGHEST, preferred_element_type=F32
        )
        parts[...] = gram.reshape(parts.shape)
        sum_gram(me, size, summed, parts, arrived, sum_send_sem, sum_recv_sem)
        gram_ref[...] = summed[...]
        for half in range(2):
            for stage in range(stages):
                for mask in sums(orders[half][:stage]):
                    copy_of(half, stage, mask).wait_send()


def make_sketch(images, groups, live, defocus_values, matrix, size):
    slots, length, _ = images.shape
    height, rank = matrix.shape
    count = math.gcd(slots, 16)
    table = real_tables(length)
    zero = jnp.zeros_like(table)
    pair = jnp.concatenate(
        [jnp.concatenate([table, zero], axis=1), jnp.concatenate([zero, table], axis=1)], axis=0
    )
    number = defocus_values.shape[0]
    if direct_sum(rank, size):
        summing = [
            pltpu.VMEM((size, rank // size, rank), F32),
            pltpu.VMEM((size, rank // size, rank), F32),
        ]
        signals = 2 * size
    else:
        summing = [
            pltpu.VMEM((1, rank, rank), F32),
            pltpu.VMEM((bits_of(size), rank, rank), F32),
        ]
        signals = bits_of(size)

    def whole(*shape):
        return pl.BlockSpec(shape, lambda i, *_: (0,) * len(shape))

    return pl.pallas_call(
        functools.partial(sketch_kernel, size),
        out_shape=(
            jax.ShapeDtypeStruct((length, slots, length), BF16),
            jax.ShapeDtypeStruct((slots, rank), F32),
            jax.ShapeDtypeStruct((rank, rank), F32),
        ),
        grid_spec=pltpu.PrefetchScalarGridSpec(
            num_scalar_prefetch=2,
            grid=(slots // count,),
            in_specs=[
                pl.BlockSpec((count, length, length), lambda i, *_: (i, 0, 0)),
                whole(height, rank),
                whole(number, length, length),
                whole(2 * length, 2 * length),
                whole(2 * length, 2 * length),
                whole(length, length),
                whole(length, length),
            ],
            out_specs=(whole(length, slots, length), whole(slots, rank), whole(rank, rank)),
            scratch_shapes=[
                pltpu.VMEM((length * count, length), F32),
                pltpu.VMEM((2, size, height // 2, rank), BF16),
                pltpu.VMEM((rank, rank), F32),
                *summing,
                pltpu.SemaphoreType.DMA((2, size - 1)),
                pltpu.SemaphoreType.DMA((2, size - 1)),
                pltpu.SemaphoreType.DMA((signals,)),
                pltpu.SemaphoreType.DMA((signals,)),
            ],
        ),
        compiler_params=pltpu.CompilerParams(
            collective_id=1, has_side_effects=True, vmem_limit_bytes=50 << 20
        ),
        name="sketch",
    )(
        groups,
        live,
        images,
        matrix,
        filter_table(defocus_values, length),
        pair,
        pair.T,
        table,
        table.T,
    )


def basis_kernel(factor_ref, sketch_ref, out_ref, turned_ref):
    rank = factor_ref.shape[0]
    row = lax.broadcasted_iota(jnp.int32, (rank, rank), 0)
    col = lax.broadcasted_iota(jnp.int32, (rank, rank), 1)
    factor = factor_ref[...]
    on_diagonal = jnp.where(row == col, factor, 0.0)
    lower = jnp.where(row > col, factor, 0.0) / jnp.sum(on_diagonal, axis=1, keepdims=True)

    def times(left, right):
        return jnp.dot(left, right, precision=HIGHEST, preferred_element_type=F32)

    def same_block(shift):
        return lax.shift_right_logical(row, shift) == lax.shift_right_logical(col, shift)

    shift = 3
    within = jnp.where(same_block(shift), lower, 0.0)
    unit = jnp.where(row == col, 1.0, 0.0).astype(F32)
    square = times(within, within)
    fourth = times(square, square)
    inverse = times(times(unit - within, unit + square), unit + fourth)
    while 1 << shift < rank:
        off = jnp.where(same_block(shift + 1) & ~same_block(shift), lower, 0.0)
        inverse = inverse - times(inverse, times(off, inverse))
        shift += 1
    inverse = inverse / jnp.sum(on_diagonal, axis=0, keepdims=True)
    basis = lax.dot_general(
        sketch_ref[...],
        inverse,
        (((1,), (1,)), ((), ())),
        precision=HIGHEST,
        preferred_element_type=F32,
    )
    out_ref[...] = basis.astype(BF16)
    turned_ref[...] = basis.T.astype(BF16)


def make_basis(factor_low, sketch):
    slots, rank = sketch.shape
    return pl.pallas_call(
        basis_kernel,
        out_shape=(
            jax.ShapeDtypeStruct((slots, rank), BF16),
            jax.ShapeDtypeStruct((rank, slots), BF16),
        ),
        name="basis",
    )(factor_low, sketch)


def project_kernel(size, basis_ref, column_ref, out_ref, held, arrived, send_sem, recv_sem):
    me = lax.axis_index("pix")
    length = column_ref.shape[0]
    rows = length // size
    part = rows // 2
    orders = halving_orders(size)
    slots = {}
    for half in range(2):
        for stage in range(len(orders[half])):
            for mask in masks_of(orders[half][stage + 1 :]):
                slots[half, stage, mask] = len(slots) % (size - 1)

    def copy_of(half, stage, mask):
        bit = orders[half][stage]
        slot = slots[half, stage, mask]
        return remote(
            held.at[half, bit | mask],
            arrived.at[half, slot],
            send_sem.at[half, slot],
            recv_sem.at[half, slot],
            partner_of(me, bit),
        )

    greet(me, [1 << shift for shift in range(bits_of(size))])
    first = orders[0][0]

    def compute(half, mask):
        start = partner_of(me, mask) * rows + half * part
        right = jnp.concatenate([column_ref[start + row] for row in range(part)], axis=1)
        held[half, mask] = jnp.dot(
            basis_ref[...], right, preferred_element_type=F32
        ).astype(BF16)

    def add(half, stage, mask):
        later = orders[half][stage + 1 :]
        copy_of(half, stage, mask).wait_recv()
        total = (
            held[half, mask].astype(F32)
            + arrived[half, slots[half, stage, mask]].astype(F32)
        )
        if later:
            held[half, mask] = total.astype(BF16)
            if mask & later[0]:
                copy_of(half, stage + 1, mask - later[0]).start()
        else:
            height = out_ref.shape[0] // 2
            out_ref[half * height : (half + 1) * height, :] = total.T

    kept = [masks_of(orders[half][1:]) for half in range(2)]
    for place in range(len(kept[0]) + 1):
        for half in range(2):
            if place < len(kept[0]):
                mask = kept[half][place]
                compute(half, first | mask)
                copy_of(half, 0, mask).start()
                compute(half, mask)
        for half in range(2):
            if place > 0:
                add(half, 0, kept[half][place - 1])
    for stage in range(1, bits_of(size)):
        for place in range(len(masks_of(orders[0][stage + 1 :]))):
            for half in range(2):
                add(half, stage, masks_of(orders[half][stage + 1 :])[place])
    for half in range(2):
        for stage in range(bits_of(size)):
            for mask in masks_of(orders[half][stage + 1 :]):
                copy_of(half, stage, mask).wait_send()


def project(columns, basis_t, size):
    length, slots, _ = columns.shape
    rank = basis_t.shape[0]
    width = length * length // size
    return pl.pallas_call(
        functools.partial(project_kernel, size),
        out_shape=jax.ShapeDtypeStruct((width, rank), F32),
        in_specs=[pl.BlockSpec(memory_space=pltpu.VMEM)] * 2,
        out_specs=pl.BlockSpec(memory_space=pltpu.VMEM),
        scratch_shapes=[
            pltpu.VMEM((2, size, rank, width // 2), BF16),
            pltpu.VMEM((2, size - 1, rank, width // 2), BF16),
            pltpu.SemaphoreType.DMA((2, size - 1)),
            pltpu.SemaphoreType.DMA((2, size - 1)),
        ],
        compiler_params=pltpu.CompilerParams(
            collective_id=2, has_side_effects=True, vmem_limit_bytes=48 << 20
        ),
        name="project",
    )(basis_t, columns)


GROWTH = 6.0


def per_device(particle_images, defocus_group, live_counts, defocus_values, test_matrix):
    size = lax.axis_size("pix")
    arguments = (particle_images, defocus_group, live_counts, defocus_values, test_matrix, size)
    basis, projection, growth = make_whole(*arguments)

    def stepwise():
        columns, sketch, gram = make_sketch(*arguments)
        factor_low = jnp.linalg.cholesky(gram)
        range_basis, basis_t = make_basis(factor_low, sketch)
        return (range_basis, project(columns, basis_t, size))

    return lax.cond(jnp.max(growth) <= GROWTH, lambda: (basis, projection), stepwise)


def solution(mesh):
    placed = (
        P(("grp", "pix"), None, None),
        P(("grp", "pix")),
        P(("grp", "pix")),
        P("grp"),
        P(("grp", "pix"), None),
    )
    return jax.shard_map(
        per_device,
        mesh=mesh,
        in_specs=placed,
        out_specs=(P(("grp", "pix"), None), P(("grp", "pix"), None)),
        check_vma=False,
    )
```

```python
import functools
import math

import jax
import jax.numpy as jnp
import ml_dtypes
import numpy as np
from jax import lax
from jax.experimental import pallas as pl
from jax.experimental.pallas import tpu as pltpu
from jax.sharding import PartitionSpec as P

AMPLITUDE = 0.1
WIENER = 0.1
F32 = jnp.float32
BF16 = jnp.bfloat16
HIGHEST = lax.Precision.HIGHEST


def real_tables(length):
    rows = np.arange(length)
    angles = 2.0 * math.pi / length * (rows[:, None] * rows[None, :] % length)
    packed = np.where(rows[None, :] <= length // 2, np.cos(angles), np.sin(angles))
    return jnp.asarray(packed.astype(np.float32)).astype(BF16)


def pair_tables(length):
    rows = np.arange(length)
    angles = 2.0 * math.pi / length * (rows[:, None] * rows[None, :] % length)
    packed = np.where(rows[None, :] <= length // 2, np.cos(angles), np.sin(angles))
    pair = np.zeros((2 * length, 2 * length), np.float32)
    pair[:length, :length] = packed
    pair[length:, length:] = packed
    pair = pair.astype(ml_dtypes.bfloat16)
    return jnp.asarray(pair), jnp.asarray(np.ascontiguousarray(pair.T))


def filter_table(defocus_values, length):
    index = jnp.arange(length, dtype=jnp.int32)
    freq = jnp.where(index < length // 2, index, index - length).astype(F32) / length
    phase = jnp.pi * defocus_values[:, None] * (freq * freq)[None, :]
    sine, cosine = lax.optimization_barrier((jnp.sin(phase), jnp.cos(phase)))
    keep = math.sqrt(1.0 - AMPLITUDE**2)
    first = (keep * sine + AMPLITUDE * cosine)[:, :, None]
    second = (keep * cosine - AMPLITUDE * sine)[:, :, None]
    contrast = -(first * cosine[:, None, :] + second * sine[:, None, :])
    wiener = (contrast / (contrast * contrast + WIENER)).astype(BF16).astype(F32)
    twice = jnp.where((index == 0) | (index == length // 2), 1.0, 2.0).astype(F32)
    return (wiener * (twice[:, None] * twice[None, :] / float(length * length))).astype(BF16)


def bits_of(size):
    return size.bit_length() - 1


def partner_of(me, mask):
    for shift in range(mask.bit_length()):
        bit = 1 << shift
        if mask & bit:
            me = me + bit * (1 - 2 * lax.rem(lax.div(me, bit), 2))
    return me


def greet(me, masks):
    barrier = pltpu.get_barrier_semaphore()
    for mask in masks:
        pl.semaphore_signal(
            barrier,
            inc=1,
            device_id={"pix": partner_of(me, mask)},
            device_id_type=pl.DeviceIdType.MESH,
        )
    pl.semaphore_wait(barrier, len(masks))


def remote(src, dst, send_sem, recv_sem, peer):
    return pltpu.make_async_remote_copy(
        src_ref=src,
        dst_ref=dst,
        send_sem=send_sem,
        recv_sem=recv_sem,
        device_id={"pix": peer},
        device_id_type=pl.DeviceIdType.MESH,
    )


def halving_orders(size):
    bits = [1 << shift for shift in range(bits_of(size))]
    if len(bits) < 3:
        return (bits, bits)
    return (bits, bits[:1] + bits[2:] + bits[1:2])


def masks_of(bits):
    if not bits:
        return [0]
    rest = masks_of(bits[1:])
    return [bits[0] | mask for mask in rest] + rest


def gathering_orders(size):
    first, second = halving_orders(size)
    return (first[::-1], second[1:][::-1] + second[:1])


def sums(bits):
    out = [0]
    for bit in bits:
        out = out + [bit | mask for mask in out]
    return out


def direct_sum(rank, size):
    return rank % (8 * size) == 0


def peers(rank, size):
    if direct_sum(rank, size):
        return list(range(1, size))
    return [1 << shift for shift in range(bits_of(size))]


def sum_gram(me, size, gram_ref, parts, arrived, send_sem, recv_sem):
    if not direct_sum(parts.shape[0] * parts.shape[1], size):
        gram_ref[...] = parts[...].reshape(gram_ref.shape)
        for stage in range(bits_of(size)):
            copy = remote(
                gram_ref,
                arrived.at[stage],
                send_sem.at[stage],
                recv_sem.at[stage],
                partner_of(me, 1 << stage),
            )
            copy.start()
            copy.wait()
            gram_ref[...] += arrived[stage]
        return
    height = parts.shape[1]
    scatter = [
        remote(
            parts.at[partner_of(me, d)],
            arrived.at[d],
            send_sem.at[d],
            recv_sem.at[d],
            partner_of(me, d),
        )
        for d in range(1, size)
    ]
    for copy in scatter:
        copy.start()
    total = parts[me]
    for d, copy in enumerate(scatter, 1):
        copy.wait_recv()
        total = total + arrived[d]
    arrived[0] = total
    own = pl.ds(pl.multiple_of(me * height, height), height)
    gather = [
        remote(
            arrived.at[0],
            gram_ref.at[own],
            send_sem.at[size + d],
            recv_sem.at[size + d],
            partner_of(me, d),
        )
        for d in range(1, size)
    ]
    for copy in gather:
        copy.start()
    gram_ref[own, :] = total
    for copy in gather:
        copy.wait_recv()
    for copy in scatter + gather:
        copy.wait_send()


class Gather:
    UP, DOWN, ACROSS, BESIDE = range(4)

    def __init__(self, me, size, held, block, send_sem, recv_sem):
        self.me, self.size, self.held, self.block = me, size, held, block
        self.send_sem, self.recv_sem = send_sem, recv_sem
        self.layers = size // 4
        self.z = lax.div(me, 4)
        height = held.shape[1]
        first = height * 13 // 32 // 16 * 16
        self.cuts = [(0, first), (first, first), (2 * first, height - 2 * first)]
        self.has_up = self.z + 1 < self.layers
        self.has_down = self.z >= 1
        self.across = partner_of(me, 2)
        self.beside = partner_of(me, 1)
        self.peers = {
            self.UP: me + 4,
            self.DOWN: me - 4,
            self.ACROSS: self.across,
            self.BESIDE: self.beside,
        }

    def copy(self, owner, part, dest):
        start, rows = self.cuts[part]
        piece = self.held.at[owner, pl.ds(start, rows)]
        return remote(
            self.block.at[pl.ds(start, rows)] if owner is self.me else piece,
            piece,
            self.send_sem.at[dest, owner, part],
            self.recv_sem.at[owner, part],
            self.peers[dest],
        )

    def greet(self):
        barrier = pltpu.get_barrier_semaphore()

        def signal(dest):
            pl.semaphore_signal(
                barrier,
                inc=1,
                device_id={"pix": self.peers[dest]},
                device_id_type=pl.DeviceIdType.MESH,
            )

        signal(self.ACROSS)
        signal(self.BESIDE)
        pl.when(self.has_up)(lambda: signal(self.UP))
        pl.when(self.has_down)(lambda: signal(self.DOWN))
        neighbours = jnp.minimum(self.z, 1) + jnp.minimum(self.layers - 1 - self.z, 1)
        pl.semaphore_wait(barrier, 2 + neighbours)

    def moves(self):
        out = []
        for part in (2, 0, 1):
            out += [
                (None, self.me, part, self.ACROSS),
                (self.has_up, self.me, part, self.UP),
                (self.has_down, self.me, part, self.DOWN),
                (None, self.me, part, self.BESIDE),
            ]
        return out

    def begin(self, copies):
        for condition, owner, part, dest in copies:
            if condition is None:
                self.copy(owner, part, dest).start()
            else:
                pl.when(condition)(lambda o=owner, p=part, d=dest: self.copy(o, p, d).start())

    def finish(self, copies):
        for condition, owner, part, dest in copies:
            if condition is None:
                self.copy(owner, part, dest).wait_send()
            else:
                pl.when(condition)(lambda o=owner, p=part, d=dest: self.copy(o, p, d).wait_send())

    def arrived(self, owner, part):
        self.copy(owner, part, self.BESIDE).wait_recv()

    def events(self):
        up, down = (self.has_up, self.UP), (self.has_down, self.DOWN)
        across, beside = (None, self.ACROSS), (None, self.BESIDE)
        out = [[(None, self.across, 2, [up, down, beside])]]

        def along(step, part, side):
            start = self.me if side == 0 else self.across
            extra = [across] if part < 2 else []
            below = (self.z >= step, start - 4 * step, part, [up] + extra + [beside])
            above = (
                self.z + step < self.layers,
                start + 4 * step,
                part,
                [down] + extra + [beside],
            )
            return [below, above]

        def over(step, part):
            if step == 0:
                return [(None, self.across, part, [beside])]
            return [
                (self.z >= step, self.across - 4 * step, part, [beside]),
                (self.z + step < self.layers, self.across + 4 * step, part, [beside]),
            ]

        for step in range(1, self.layers):
            out.append(along(step, 0, 0) + along(step, 2, 0) + over(step - 1, 0))
            out.append(along(step, 1, 0) + along(step, 2, 1) + over(step - 1, 1))
        out.append(over(self.layers - 1, 0))
        out.append(over(self.layers - 1, 1))
        return out

    def handle(self, events):
        for condition, owner, part, dests in events:

            def act(owner=owner, part=part, dests=dests):
                self.arrived(owner, part)
                self.begin([(c, owner, part, d) for c, d in dests])

            if condition is None:
                act()
            else:
                pl.when(condition)(act)

    def close(self):
        self.finish(self.moves())
        for events in self.events():
            for condition, owner, part, dests in events:

                def act(owner=owner, part=part, dests=dests):
                    self.finish([(c, owner, part, d) for c, d in dests])

                if condition is None:
                    act()
                else:
                    pl.when(condition)(act)

    def await_beside(self, owner):
        for part in range(3):
            self.arrived(owner, part)


TURN = 2
FINISH = 3
GROWTH = 6.0


class Scatter:
    def __init__(self, gather, work, inbox, send_sem, recv_sem):
        self.gather = gather
        self.work, self.inbox = work, inbox
        self.send_sem, self.recv_sem = send_sem, recv_sem
        rank = work.shape[1]
        last = max(rank // 8 // 16 * 16, 16)
        first = (rank - last + 31) // 32 * 16
        self.cuts = [(0, first), (first, rank - last - first), (rank - last, last), (0, rank)]
        self.sent = []

    def copy(self, owner, part, dest):
        start, rows = self.cuts[part]
        slot = lax.div(owner, 2)
        place = part % 3
        return remote(
            self.work.at[owner, pl.ds(start, rows)],
            self.inbox.at[dest, slot, pl.ds(start, rows)],
            self.send_sem.at[dest, slot, place],
            self.recv_sem.at[dest, slot, place],
            self.gather.peers[dest],
        )

    def send(self, owner, part, dest, conditions):
        self.copy(owner, part, dest).start()
        self.sent.append((conditions, owner, part, dest))

    def take(self, owner, part, dest):
        start, rows = self.cuts[part]
        self.copy(owner, part, dest).wait_recv()
        piece = self.work.at[owner, pl.ds(start, rows)]
        got = self.inbox[dest, lax.div(owner, 2), pl.ds(start, rows)]
        piece[...] = (piece[...].astype(F32) + got.astype(F32)).astype(BF16)

    def close(self):
        for conditions, owner, part, dest in self.sent:
            wait = lambda o=owner, p=part, d=dest: self.copy(o, p, d).wait_send()
            for condition in conditions:
                wait = lambda c=condition, w=wait: pl.when(c)(w)
            wait()


def splat(values, row, col):
    return jnp.broadcast_to(values[row : row + 1, col : col + 1], values.shape)


def factor_step(block, left_ref, right_ref, inverse_ref):
    size = left_ref.shape[0]
    top, side = left_ref[0:8, :], right_ref[0:8, :]
    cell = {(r, c): splat(top, r, c) for r in range(8) for c in range(r + 1)}
    turn = {}
    for c in range(8):
        pivot = cell[c, c]
        guess = lax.rsqrt(pivot)
        scale = guess * (1.5 - 0.5 * pivot * guess * guess)
        turn[c, c] = scale
        for r in range(c + 1, 8):
            cell[r, c] = cell[r, c] * scale
        for r in range(c + 1, 8):
            for k in range(c + 1, r + 1):
                cell[r, k] = cell[r, k] - cell[r, c] * cell[k, c]
    for c in range(8):
        for r in range(c + 1, 8):
            total = cell[r, c] * turn[c, c]
            for k in range(c + 1, r):
                total = total + cell[r, k] * turn[k, c]
            turn[r, c] = -total * turn[r, r]
    row = lax.broadcasted_iota(jnp.int32, top.shape, 0)
    lane = lax.broadcasted_iota(jnp.int32, top.shape, 1)
    upper, lower = jnp.zeros_like(top), jnp.zeros_like(side)
    for c in range(8):
        weight = jnp.zeros_like(top)
        for r in range(c, 8):
            weight = jnp.where(row == r, turn[r, c], weight)
        upper = upper + weight * top[c : c + 1, :]
        lower = lower + weight * side[c : c + 1, :]
    inverse_ref[pl.ds(pl.multiple_of(8 * block, 8), 8), :] = lower
    upper = jnp.where((lane >= row) & (lane < size - 8 * block), upper, 0.0)
    both = jnp.concatenate([upper, lower], axis=1)
    change = lax.dot_general(
        upper, both, (((0,), (0,)), ((), ())), precision=HIGHEST, preferred_element_type=F32
    )
    left = pltpu.roll(left_ref[...] - change[:, :size], size - 8, 1)
    left_ref[0 : size - 8, :] = left[8:]
    left_ref[size - 8 : size, :] = jnp.zeros_like(top)
    right = right_ref[...] - change[:, size:]
    right_ref[0 : size - 8, :] = right[8:]
    right_ref[size - 8 : size, :] = jnp.zeros_like(side)


class GramSum:
    def __init__(self, me, size, gram_ref, parts, arrived, send_sem, recv_sem):
        self.me, self.size, self.gram_ref = me, size, gram_ref
        self.parts, self.arrived = parts, arrived
        self.send_sem, self.recv_sem = send_sem, recv_sem
        self.direct = direct_sum(parts.shape[0] * parts.shape[1], size)

    def scatter(self, d):
        peer = partner_of(self.me, d)
        return remote(
            self.parts.at[peer],
            self.arrived.at[d],
            self.send_sem.at[d],
            self.recv_sem.at[d],
            peer,
        )

    def gather(self, d):
        height = self.parts.shape[1]
        own = pl.ds(pl.multiple_of(self.me * height, height), height)
        return remote(
            self.arrived.at[0],
            self.gram_ref.at[own],
            self.send_sem.at[self.size + d],
            self.recv_sem.at[self.size + d],
            partner_of(self.me, d),
        )

    def start(self):
        if self.direct:
            for d in range(1, self.size):
                self.scatter(d).start()

    def turn(self):
        if not self.direct:
            sum_gram(
                self.me,
                self.size,
                self.gram_ref,
                self.parts,
                self.arrived,
                self.send_sem,
                self.recv_sem,
            )
            return
        total = self.parts[self.me]
        for d in range(1, self.size):
            self.scatter(d).wait_recv()
            total = total + self.arrived[d]
        self.arrived[0] = total
        for d in range(1, self.size):
            self.gather(d).start()
        height = self.parts.shape[1]
        self.gram_ref[pl.ds(pl.multiple_of(self.me * height, height), height), :] = total

    def finish(self):
        if self.direct:
            for d in range(1, self.size):
                self.gather(d).wait_recv()

    def close(self):
        if self.direct:
            for d in range(1, self.size):
                self.scatter(d).wait_send()
                self.gather(d).wait_send()


def build_filters(defocus_ref, waves, filters):
    number, length, _ = filters.shape
    index = lax.broadcasted_iota(jnp.int32, (1, length), 1)
    freq = jnp.where(index < length // 2, index, index - length).astype(F32) / length
    square = freq * freq

    def phase(group, _):
        waves[0, pl.ds(group, 1), :] = (math.pi * defocus_ref[group]) * square

    lax.fori_loop(0, number, phase, None)
    phases = waves[0, 0:number, :]
    sine, cosine = jnp.sin(phases), jnp.cos(phases)
    waves[0, 0:number, :] = sine
    waves[1, 0:number, :] = cosine
    keep = math.sqrt(1.0 - AMPLITUDE**2)
    rest = jnp.zeros((length - number, length), F32)
    first = jnp.concatenate([keep * sine + AMPLITUDE * cosine, rest], axis=0).T
    second = jnp.concatenate([keep * cosine - AMPLITUDE * sine, rest], axis=0).T

    def twice(axis):
        place = lax.broadcasted_iota(jnp.int32, (length, length), axis)
        return jnp.where((place == 0) | (place == length // 2), 1.0, 2.0)

    scale = twice(0) * twice(1) / float(length * length)

    def eight(block, both):
        left, right = both
        for i in range(8):
            group = 8 * block + i
            contrast = -(
                left[:, i : i + 1] * waves[1, pl.ds(group, 1), :]
                + right[:, i : i + 1] * waves[0, pl.ds(group, 1), :]
            )
            wiener = (contrast / (contrast * contrast + WIENER)).astype(BF16).astype(F32)
            filters[group] = (wiener * scale).astype(BF16)
        return pltpu.roll(left, length - 8, 1), pltpu.roll(right, length - 8, 1)

    lax.fori_loop(0, number // 8, eight, (first, second))


def whole_kernel(
    size,
    count,
    stride,
    group_ref,
    live_ref,
    defocus_ref,
    image_hbm,
    matrix_hbm,
    pair_hbm,
    pair_t_hbm,
    basis_ref,
    out_ref,
    growth_ref,
    pair_ref,
    pair_t_ref,
    waves,
    filters,
    images_ref,
    turned,
    columns,
    held,
    sketch_ref,
    gram_ref,
    parts,
    arrived,
    left_ref,
    right_ref,
    inverse_ref,
    work,
    inbox,
    load_sem,
    own_sem,
    send_sem,
    recv_sem,
    sum_send_sem,
    sum_recv_sem,
    back_send_sem,
    back_recv_sem,
):
    me = lax.axis_index("pix")
    step = pl.program_id(0)
    length, slots, _ = columns.shape
    rank = sketch_ref.shape[1]
    steps = slots // count
    pairs = count // 2
    base = step * count
    gather = Gather(me, size, held, matrix_hbm, send_sem, recv_sem)
    events = gather.events()

    def load(i):
        rows = pl.ds(i * count, count)
        return pltpu.make_async_copy(image_hbm.at[rows], images_ref.at[rows], load_sem.at[i])

    @pl.when(step == 0)
    def _():
        gather.greet()
        gather.begin(gather.moves())
        small = [
            pltpu.make_async_copy(pair_hbm, pair_ref, own_sem.at[0]),
            pltpu.make_async_copy(pair_t_hbm, pair_t_ref, own_sem.at[1]),
            pltpu.make_async_copy(matrix_hbm, held.at[me], own_sem.at[2]),
        ]
        for copy in small:
            copy.start()
        for i in range(steps):
            load(i).start()
        build_filters(defocus_ref, waves, filters)
        for copy in small:
            copy.wait()

    early = min(len(events), steps - 2)
    for i in range(early):

        @pl.when(step == i + 1)
        def _(i=i):
            gather.handle(events[i])

    load(step).wait()

    def side_by_side(values):
        return jnp.concatenate(values, axis=1)

    def product(left, right):
        return jnp.dot(left, right, preferred_element_type=F32)

    def quads(left, right):
        width = 2 * length
        return jnp.concatenate(
            [product(left, right[i : i + width]) for i in range(0, pairs * length, width)], axis=0
        )

    images = jnp.concatenate(
        [
            side_by_side([images_ref[base + 2 * i], images_ref[base + 2 * i + 1]])
            for i in range(pairs)
        ],
        axis=0,
    )
    weights = jnp.concatenate(
        [
            side_by_side(
                [filters[group_ref[base + 2 * i]], filters[group_ref[base + 2 * i + 1]]]
            )
            for i in range(pairs)
        ],
        axis=0,
    )
    rows = product(images, pair_ref[...]).astype(BF16)
    spectrum = quads(pair_t_ref[...], rows)
    kept = (spectrum * weights.astype(F32)).astype(BF16)
    back = product(kept, pair_t_ref[...]).astype(BF16)
    result = quads(pair_ref[...], back)
    for i in range(count):
        tall, wide = i // 2 * length, i % 2 * length
        turned[pl.ds(i, length, stride=stride), :] = result[
            tall : tall + length, wide : wide + length
        ]
    slot = base + lax.broadcasted_iota(jnp.int32, (1, count, 1), 1)
    values = turned[...].reshape(length, stride, length)[:, :count]
    columns[:, pl.ds(pl.multiple_of(base, count), count), :] = jnp.where(
        slot < live_ref[0], values, 0.0
    ).astype(BF16)

    @pl.when(step == steps - 1)
    def _():
        lines = length // size
        layers = gather.layers
        z = gather.z

        def pixels(owner):
            return side_by_side([columns[owner * lines + line] for line in range(lines)])

        def whole_chip(owner):
            other = partner_of(owner, 1)
            gather.await_beside(other)
            sketch_ref[...] += product(pixels(owner), held[owner]) + product(
                pixels(other), held[other]
            )

        def both_ways(distance, act):
            pl.when(z >= distance)(lambda: act(-4 * distance, False))
            pl.when(z + distance < layers)(lambda: act(4 * distance, True))

        sketch_ref[...] = jnp.zeros_like(sketch_ref)
        done = early
        whole_chip(me)
        for distance in range(layers):
            while done < len(events) and done < 2 * distance + 1:
                gather.handle(events[done])
                done += 1
            if distance:
                both_ways(distance, lambda start, _: whole_chip(me + start))
            while done < len(events) and done < 2 * distance + 3:
                gather.handle(events[done])
                done += 1
            if distance:
                both_ways(distance, lambda start, _: whole_chip(gather.across + start))
            else:
                whole_chip(gather.across)
        sketch = sketch_ref[...]
        sketch_t = sketch.T.astype(BF16)
        scatter = Scatter(gather, work, inbox, back_send_sem, back_recv_sem)
        total = GramSum(me, size, gram_ref, parts, arrived, sum_send_sem, sum_recv_sem)
        up, down, across, beside = gather.UP, gather.DOWN, gather.ACROSS, gather.BESIDE

        def ways(distance):
            out = []
            for upwards in (False, True) if distance else (True,):
                own = me + (4 * distance if upwards else -4 * distance)
                other = partner_of(own, 2)
                there = z + distance < layers if upwards else z >= distance
                given = [there] if distance else []
                out.append((given, upwards, own, other, partner_of(own, 1), partner_of(other, 1)))
            return out

        def run(given, act):
            pl.when(given[0])(act) if given else act()

        def compute(distance):
            for given, upwards, own, other, own_beside, other_beside in ways(distance):

                def act():
                    for owner, aside in ((other, other_beside), (own, own_beside)):
                        work[aside] = product(sketch_t, pixels(aside)).astype(BF16)
                        scatter.send(aside, 3, beside, given)
                        work[owner] = product(sketch_t, pixels(owner)).astype(BF16)

                run(given, act)

        def onward(owner, part, upwards, given):
            way, ahead = (up, gather.has_down) if upwards else (down, gather.has_up)
            pl.when(ahead)(lambda: scatter.take(owner, part, way))
            scatter.send(owner, part, way, given)

        def chip_sum(distance):
            for given, upwards, own, other, _, _ in ways(distance):

                def act():
                    scatter.take(other, 3, beside)
                    for part in range(2):
                        scatter.send(other, part, across, given)
                    scatter.take(own, 3, beside)
                    if distance:
                        onward(other, 2, upwards, given)
                        onward(own, 2, upwards, given)

                run(given, act)

        def along(distance, part):
            for given, upwards, own, _, _, _ in ways(distance):

                def act():
                    scatter.take(own, part, across)
                    if distance:
                        onward(own, part, upwards, given)

                run(given, act)

        def last(owner, part):
            pl.when(gather.has_down)(lambda: scatter.take(owner, part, up))
            pl.when(gather.has_up)(lambda: scatter.take(owner, part, down))

        gram = lax.dot_general(
            sketch, sketch, (((0,), (0,)), ((), ())), precision=HIGHEST, preferred_element_type=F32
        )
        parts[...] = gram.reshape(parts.shape)
        total.start()
        compute(layers - 1)
        for distance in range(layers - 1, -1, -1):
            if distance:
                compute(distance - 1)
            chip_sum(distance)
            if distance == max(layers - TURN, 0):
                total.turn()
        todo = [(distance, part) for distance in range(layers - 1, 0, -1) for part in range(2)]
        for place in todo[:FINISH]:
            along(*place)
        total.finish()
        unit = lax.broadcasted_iota(jnp.int32, (rank, rank), 0) == lax.broadcasted_iota(
            jnp.int32, (rank, rank), 1
        )
        left_ref[...] = gram_ref[...]
        right_ref[...] = jnp.where(unit, 1.0, 0.0)
        blocks = rank // 8
        todo = todo[FINISH:]
        for i in range(len(todo) + 1):
            lax.fori_loop(
                blocks * i // (len(todo) + 1),
                blocks * (i + 1) // (len(todo) + 1),
                lambda block, _: factor_step(block, left_ref, right_ref, inverse_ref),
                None,
            )
            if i < len(todo):
                along(*todo[i])
        inverse = inverse_ref[...]
        basis_ref[...] = lax.dot_general(
            sketch,
            inverse,
            (((1,), (1,)), ((), ())),
            precision=HIGHEST,
            preferred_element_type=F32,
        ).astype(BF16)
        scale = jnp.sqrt(jnp.sum(inverse * inverse, axis=0, keepdims=True))
        sums = jnp.dot(
            jnp.broadcast_to(scale, (8, rank)),
            jnp.abs(gram_ref[...]),
            precision=HIGHEST,
            preferred_element_type=F32,
        )
        growth_ref[0] = jnp.where(jnp.max(sums * scale) <= GROWTH, 1, 0)
        last(gather.across, 2)
        scatter.send(gather.across, 2, across, [])
        last(me, 2)
        for part in range(2):
            along(0, part)
            last(me, part)
        scatter.take(me, 2, across)
        mine = jnp.dot(
            inverse, work[me].astype(F32), precision=HIGHEST, preferred_element_type=F32
        )
        out_ref[...] = mine.T
        gather.close()
        scatter.close()
        total.close()


def make_whole(images, groups, live, defocus_values, matrix, size):
    slots, length, _ = images.shape
    height, rank = matrix.shape
    count = math.gcd(slots, 32)
    stride = count + 4
    pair, pair_t = pair_tables(length)
    number = defocus_values.shape[0]
    if direct_sum(rank, size):
        summing = [pltpu.VMEM((size, rank // size, rank), F32)] * 2
        signals = 2 * size
    else:
        summing = [
            pltpu.VMEM((1, rank, rank), F32),
            pltpu.VMEM((bits_of(size), rank, rank), F32),
        ]
        signals = bits_of(size)

    def whole(*shape):
        return pl.BlockSpec(shape, lambda i, *_: (0,) * len(shape))

    square = pltpu.VMEM((rank, rank), F32)
    return pl.pallas_call(
        functools.partial(whole_kernel, size, count, stride),
        out_shape=(
            jax.ShapeDtypeStruct((slots, rank), BF16),
            jax.ShapeDtypeStruct((height, rank), F32),
            jax.ShapeDtypeStruct((1,), jnp.int32),
        ),
        grid_spec=pltpu.PrefetchScalarGridSpec(
            num_scalar_prefetch=2,
            grid=(slots // count,),
            in_specs=[
                pl.BlockSpec(memory_space=pltpu.SMEM),
                *[pl.BlockSpec(memory_space=pl.ANY)] * 4,
            ],
            out_specs=(
                whole(slots, rank),
                whole(height, rank),
                pl.BlockSpec(memory_space=pltpu.SMEM),
            ),
            scratch_shapes=[
                pltpu.VMEM((2 * length, 2 * length), BF16),
                pltpu.VMEM((2 * length, 2 * length), BF16),
                pltpu.VMEM((2, number, length), F32),
                pltpu.VMEM((number, length, length), BF16),
                pltpu.VMEM((slots, length, length), BF16),
                pltpu.VMEM((length * stride, length), F32),
                pltpu.VMEM((length, slots, length), BF16),
                pltpu.VMEM((size, height, rank), BF16),
                pltpu.VMEM((slots, rank), F32),
                square,
                *summing,
                square,
                square,
                square,
                pltpu.VMEM((size, rank, height), BF16),
                pltpu.VMEM((4, size // 2, rank, height), BF16),
                pltpu.SemaphoreType.DMA((slots // count,)),
                pltpu.SemaphoreType.DMA((3,)),
                pltpu.SemaphoreType.DMA((4, size, 3)),
                pltpu.SemaphoreType.DMA((size, 3)),
                pltpu.SemaphoreType.DMA((signals,)),
                pltpu.SemaphoreType.DMA((signals,)),
                pltpu.SemaphoreType.DMA((4, size // 2, 3)),
                pltpu.SemaphoreType.DMA((4, size // 2, 3)),
            ],
        ),
        compiler_params=pltpu.CompilerParams(
            collective_id=0, has_side_effects=True, vmem_limit_bytes=56 << 20
        ),
        name="whole",
    )(groups, live, defocus_values, images, matrix, pair, pair_t)


def sketch_kernel(
    size,
    group_ref,
    live_ref,
    image_ref,
    matrix_ref,
    filters,
    pair_ref,
    pair_t_ref,
    table_ref,
    table_t_ref,
    out_ref,
    sketch_ref,
    gram_ref,
    turned,
    held,
    summed,
    parts,
    arrived,
    send_sem,
    recv_sem,
    sum_send_sem,
    sum_recv_sem,
):
    me = lax.axis_index("pix")
    step = pl.program_id(0)
    steps = out_ref.shape[1] // image_ref.shape[0]
    count, length, _ = image_ref.shape
    pairs = count // 2
    base = step * count
    orders = gathering_orders(size)
    stages = bits_of(size)
    height = matrix_ref.shape[0] // 2

    def copy_of(half, stage, mask):
        bit = orders[half][stage]
        slot = (bit | mask) - 1
        return remote(
            held.at[half, mask],
            held.at[half, bit | mask],
            send_sem.at[half, slot],
            recv_sem.at[half, slot],
            partner_of(me, bit),
        )

    def receive(stage, half, mask):
        copy_of(half, stage, mask).wait_recv()
        for later in range(stage + 1, stages):
            copy_of(half, later, orders[half][stage] | mask).start()

    @pl.when(step == 0)
    def _():
        greet(me, peers(gram_ref.shape[0], size))
        for half in range(2):
            held[half, 0] = matrix_ref[half * height : (half + 1) * height, :]
        for stage in range(stages):
            for half in range(2):
                copy_of(half, stage, 0).start()

    early = min(2, stages)
    for stage in range(early):

        @pl.when(step == steps * (5 + 6 * stage) // 16)
        def _(stage=stage):
            for place in range(1 << stage):
                for half in range(2):
                    receive(stage, half, sums(orders[half][:stage])[place])

    def side_by_side(values):
        return jnp.concatenate(values, axis=1)

    def stacked(wide):
        return jnp.concatenate(
            [wide[:, 2 * length * i : 2 * length * (i + 1)] for i in range(pairs)], axis=0
        )

    def unstacked(tall):
        return side_by_side([tall[length * i : length * (i + 1)] for i in range(pairs)])

    images = jnp.concatenate(
        [side_by_side([image_ref[2 * i], image_ref[2 * i + 1]]) for i in range(pairs)], axis=0
    )
    rows = jnp.dot(images, pair_ref[...], preferred_element_type=F32).astype(BF16)
    spectrum = jnp.dot(table_t_ref[...], unstacked(rows), preferred_element_type=F32)
    weights = side_by_side([filters[group_ref[base + i]] for i in range(count)])
    kept = (spectrum * weights.astype(F32)).astype(BF16)
    back = jnp.dot(stacked(kept), pair_t_ref[...], preferred_element_type=F32).astype(BF16)
    result = jnp.dot(table_ref[...], unstacked(back), preferred_element_type=F32)
    for i in range(count):
        turned[pl.ds(i, length, stride=count), :] = result[:, i * length : (i + 1) * length]
    slot = base + lax.broadcasted_iota(jnp.int32, (1, count, 1), 1)
    values = turned[...].reshape(length, count, length)
    out_ref[:, pl.ds(pl.multiple_of(base, count), count), :] = jnp.where(
        slot < live_ref[0], values, 0.0
    ).astype(BF16)

    @pl.when(step == steps - 1)
    def _():
        lines = length // size
        part = lines // 2

        def term(half, mask):
            start = partner_of(me, mask) * lines + half * part
            left = side_by_side([out_ref[start + line] for line in range(part)])
            return jnp.dot(left, held[half, mask], preferred_element_type=F32)

        sketch_ref[...] = jnp.zeros_like(sketch_ref)
        for half in range(2):
            for mask in sums(orders[half][:early]):
                sketch_ref[...] += term(half, mask)
        for stage in range(early, stages):
            for place in range(1 << stage):
                for half in range(2):
                    mask = sums(orders[half][:stage])[place]
                    receive(stage, half, mask)
                    sketch_ref[...] += term(half, orders[half][stage] | mask)
        sketch = sketch_ref[...]
        gram = lax.dot_general(
            sketch, sketch, (((0,), (0,)), ((), ())), precision=HIGHEST, preferred_element_type=F32
        )
        parts[...] = gram.reshape(parts.shape)
        sum_gram(me, size, summed, parts, arrived, sum_send_sem, sum_recv_sem)
        gram_ref[...] = summed[...]
        for half in range(2):
            for stage in range(stages):
                for mask in sums(orders[half][:stage]):
                    copy_of(half, stage, mask).wait_send()


def make_sketch(images, groups, live, defocus_values, matrix, size):
    slots, length, _ = images.shape
    height, rank = matrix.shape
    count = math.gcd(slots, 16)
    table = real_tables(length)
    zero = jnp.zeros_like(table)
    pair = jnp.concatenate(
        [jnp.concatenate([table, zero], axis=1), jnp.concatenate([zero, table], axis=1)], axis=0
    )
    number = defocus_values.shape[0]
    if direct_sum(rank, size):
        summing = [
            pltpu.VMEM((size, rank // size, rank), F32),
            pltpu.VMEM((size, rank // size, rank), F32),
        ]
        signals = 2 * size
    else:
        summing = [
            pltpu.VMEM((1, rank, rank), F32),
            pltpu.VMEM((bits_of(size), rank, rank), F32),
        ]
        signals = bits_of(size)

    def whole(*shape):
        return pl.BlockSpec(shape, lambda i, *_: (0,) * len(shape))

    return pl.pallas_call(
        functools.partial(sketch_kernel, size),
        out_shape=(
            jax.ShapeDtypeStruct((length, slots, length), BF16),
            jax.ShapeDtypeStruct((slots, rank), F32),
            jax.ShapeDtypeStruct((rank, rank), F32),
        ),
        grid_spec=pltpu.PrefetchScalarGridSpec(
            num_scalar_prefetch=2,
            grid=(slots // count,),
            in_specs=[
                pl.BlockSpec((count, length, length), lambda i, *_: (i, 0, 0)),
                whole(height, rank),
                whole(number, length, length),
                whole(2 * length, 2 * length),
                whole(2 * length, 2 * length),
                whole(length, length),
                whole(length, length),
            ],
            out_specs=(whole(length, slots, length), whole(slots, rank), whole(rank, rank)),
            scratch_shapes=[
                pltpu.VMEM((length * count, length), F32),
                pltpu.VMEM((2, size, height // 2, rank), BF16),
                pltpu.VMEM((rank, rank), F32),
                *summing,
                pltpu.SemaphoreType.DMA((2, size - 1)),
                pltpu.SemaphoreType.DMA((2, size - 1)),
                pltpu.SemaphoreType.DMA((signals,)),
                pltpu.SemaphoreType.DMA((signals,)),
            ],
        ),
        compiler_params=pltpu.CompilerParams(
            collective_id=1, has_side_effects=True, vmem_limit_bytes=50 << 20
        ),
        name="sketch",
    )(
        groups,
        live,
        images,
        matrix,
        filter_table(defocus_values, length),
        pair,
        pair.T,
        table,
        table.T,
    )


def basis_kernel(factor_ref, sketch_ref, out_ref, turned_ref):
    rank = factor_ref.shape[0]
    row = lax.broadcasted_iota(jnp.int32, (rank, rank), 0)
    col = lax.broadcasted_iota(jnp.int32, (rank, rank), 1)
    factor = factor_ref[...]
    on_diagonal = jnp.where(row == col, factor, 0.0)
    lower = jnp.where(row > col, factor, 0.0) / jnp.sum(on_diagonal, axis=1, keepdims=True)

    def times(left, right):
        return jnp.dot(left, right, precision=HIGHEST, preferred_element_type=F32)

    def same_block(shift):
        return lax.shift_right_logical(row, shift) == lax.shift_right_logical(col, shift)

    shift = 3
    within = jnp.where(same_block(shift), lower, 0.0)
    unit = jnp.where(row == col, 1.0, 0.0).astype(F32)
    square = times(within, within)
    fourth = times(square, square)
    inverse = times(times(unit - within, unit + square), unit + fourth)
    while 1 << shift < rank:
        off = jnp.where(same_block(shift + 1) & ~same_block(shift), lower, 0.0)
        inverse = inverse - times(inverse, times(off, inverse))
        shift += 1
    inverse = inverse / jnp.sum(on_diagonal, axis=0, keepdims=True)
    basis = lax.dot_general(
        sketch_ref[...],
        inverse,
        (((1,), (1,)), ((), ())),
        precision=HIGHEST,
        preferred_element_type=F32,
    )
    out_ref[...] = basis.astype(BF16)
    turned_ref[...] = basis.T.astype(BF16)


def make_basis(factor_low, sketch):
    slots, rank = sketch.shape
    return pl.pallas_call(
        basis_kernel,
        out_shape=(
            jax.ShapeDtypeStruct((slots, rank), BF16),
            jax.ShapeDtypeStruct((rank, slots), BF16),
        ),
        name="basis",
    )(factor_low, sketch)


def project_kernel(size, basis_ref, column_ref, out_ref, held, arrived, send_sem, recv_sem):
    me = lax.axis_index("pix")
    length = column_ref.shape[0]
    rows = length // size
    part = rows // 2
    orders = halving_orders(size)
    slots = {}
    for half in range(2):
        for stage in range(len(orders[half])):
            for mask in masks_of(orders[half][stage + 1 :]):
                slots[half, stage, mask] = len(slots) % (size - 1)

    def copy_of(half, stage, mask):
        bit = orders[half][stage]
        slot = slots[half, stage, mask]
        return remote(
            held.at[half, bit | mask],
            arrived.at[half, slot],
            send_sem.at[half, slot],
            recv_sem.at[half, slot],
            partner_of(me, bit),
        )

    greet(me, [1 << shift for shift in range(bits_of(size))])
    first = orders[0][0]

    def compute(half, mask):
        start = partner_of(me, mask) * rows + half * part
        right = jnp.concatenate([column_ref[start + row] for row in range(part)], axis=1)
        held[half, mask] = jnp.dot(
            basis_ref[...], right, preferred_element_type=F32
        ).astype(BF16)

    def add(half, stage, mask):
        later = orders[half][stage + 1 :]
        copy_of(half, stage, mask).wait_recv()
        total = (
            held[half, mask].astype(F32)
            + arrived[half, slots[half, stage, mask]].astype(F32)
        )
        if later:
            held[half, mask] = total.astype(BF16)
            if mask & later[0]:
                copy_of(half, stage + 1, mask - later[0]).start()
        else:
            height = out_ref.shape[0] // 2
            out_ref[half * height : (half + 1) * height, :] = total.T

    kept = [masks_of(orders[half][1:]) for half in range(2)]
    for place in range(len(kept[0]) + 1):
        for half in range(2):
            if place < len(kept[0]):
                mask = kept[half][place]
                compute(half, first | mask)
                copy_of(half, 0, mask).start()
                compute(half, mask)
        for half in range(2):
            if place > 0:
                add(half, 0, kept[half][place - 1])
    for stage in range(1, bits_of(size)):
        for place in range(len(masks_of(orders[0][stage + 1 :]))):
            for half in range(2):
                add(half, stage, masks_of(orders[half][stage + 1 :])[place])
    for half in range(2):
        for stage in range(bits_of(size)):
            for mask in masks_of(orders[half][stage + 1 :]):
                copy_of(half, stage, mask).wait_send()


def project(columns, basis_t, size):
    length, slots, _ = columns.shape
    rank = basis_t.shape[0]
    width = length * length // size
    return pl.pallas_call(
        functools.partial(project_kernel, size),
        out_shape=jax.ShapeDtypeStruct((width, rank), F32),
        in_specs=[pl.BlockSpec(memory_space=pltpu.VMEM)] * 2,
        out_specs=pl.BlockSpec(memory_space=pltpu.VMEM),
        scratch_shapes=[
            pltpu.VMEM((2, size, rank, width // 2), BF16),
            pltpu.VMEM((2, size - 1, rank, width // 2), BF16),
            pltpu.SemaphoreType.DMA((2, size - 1)),
            pltpu.SemaphoreType.DMA((2, size - 1)),
        ],
        compiler_params=pltpu.CompilerParams(
            collective_id=2, has_side_effects=True, vmem_limit_bytes=48 << 20
        ),
        name="project",
    )(basis_t, columns)


def per_device(particle_images, defocus_group, live_counts, defocus_values, test_matrix):
    size = lax.axis_size("pix")
    arguments = (particle_images, defocus_group, live_counts, defocus_values, test_matrix, size)
    basis, projection, growth = make_whole(*arguments)

    def stepwise():
        columns, sketch, gram = make_sketch(*arguments)
        factor_low = jnp.linalg.cholesky(gram)
        range_basis, basis_t = make_basis(factor_low, sketch)
        return (range_basis, project(columns, basis_t, size))

    return lax.cond(growth[0] != 0, lambda: (basis, projection), stepwise)


def solution(mesh):
    placed = (
        P(("grp", "pix"), None, None),
        P(("grp", "pix")),
        P(("grp", "pix")),
        P("grp"),
        P(("grp", "pix"), None),
    )
    return jax.shard_map(
        per_device,
        mesh=mesh,
        in_specs=placed,
        out_specs=(P(("grp", "pix"), None), P(("grp", "pix"), None)),
        check_vma=False,
    )
```

```python
import functools
import math

import jax
import jax.numpy as jnp
import ml_dtypes
import numpy as np
from jax import lax
from jax.experimental import pallas as pl
from jax.experimental.pallas import tpu as pltpu
from jax.sharding import PartitionSpec as P

AMPLITUDE = 0.1
WIENER = 0.1
F32 = jnp.float32
BF16 = jnp.bfloat16
HIGHEST = lax.Precision.HIGHEST


def real_tables(length):
    rows = np.arange(length)
    angles = 2.0 * math.pi / length * (rows[:, None] * rows[None, :] % length)
    packed = np.where(rows[None, :] <= length // 2, np.cos(angles), np.sin(angles))
    return jnp.asarray(packed.astype(np.float32)).astype(BF16)


def pair_tables(length):
    rows = np.arange(length)
    angles = 2.0 * math.pi / length * (rows[:, None] * rows[None, :] % length)
    packed = np.where(rows[None, :] <= length // 2, np.cos(angles), np.sin(angles))
    pair = np.zeros((2 * length, 2 * length), np.float32)
    pair[:length, :length] = packed
    pair[length:, length:] = packed
    pair = pair.astype(ml_dtypes.bfloat16)
    return jnp.asarray(pair), jnp.asarray(np.ascontiguousarray(pair.T))


def filter_table(defocus_values, length):
    index = jnp.arange(length, dtype=jnp.int32)
    freq = jnp.where(index < length // 2, index, index - length).astype(F32) / length
    phase = jnp.pi * defocus_values[:, None] * (freq * freq)[None, :]
    sine, cosine = lax.optimization_barrier((jnp.sin(phase), jnp.cos(phase)))
    keep = math.sqrt(1.0 - AMPLITUDE**2)
    first = (keep * sine + AMPLITUDE * cosine)[:, :, None]
    second = (keep * cosine - AMPLITUDE * sine)[:, :, None]
    contrast = -(first * cosine[:, None, :] + second * sine[:, None, :])
    wiener = (contrast / (contrast * contrast + WIENER)).astype(BF16).astype(F32)
    twice = jnp.where((index == 0) | (index == length // 2), 1.0, 2.0).astype(F32)
    return (wiener * (twice[:, None] * twice[None, :] / float(length * length))).astype(BF16)


def bits_of(size):
    return size.bit_length() - 1


def partner_of(me, mask):
    for shift in range(mask.bit_length()):
        bit = 1 << shift
        if mask & bit:
            me = me + bit * (1 - 2 * lax.rem(lax.div(me, bit), 2))
    return me


def greet(me, masks):
    barrier = pltpu.get_barrier_semaphore()
    for mask in masks:
        pl.semaphore_signal(
            barrier,
            inc=1,
            device_id={"pix": partner_of(me, mask)},
            device_id_type=pl.DeviceIdType.MESH,
        )
    pl.semaphore_wait(barrier, len(masks))


def remote(src, dst, send_sem, recv_sem, peer):
    return pltpu.make_async_remote_copy(
        src_ref=src,
        dst_ref=dst,
        send_sem=send_sem,
        recv_sem=recv_sem,
        device_id={"pix": peer},
        device_id_type=pl.DeviceIdType.MESH,
    )


def halving_orders(size):
    bits = [1 << shift for shift in range(bits_of(size))]
    if len(bits) < 3:
        return (bits, bits)
    return (bits, bits[:1] + bits[2:] + bits[1:2])


def masks_of(bits):
    if not bits:
        return [0]
    rest = masks_of(bits[1:])
    return [bits[0] | mask for mask in rest] + rest


def gathering_orders(size):
    first, second = halving_orders(size)
    return (first[::-1], second[1:][::-1] + second[:1])


def sums(bits):
    out = [0]
    for bit in bits:
        out = out + [bit | mask for mask in out]
    return out


def direct_sum(rank, size):
    return rank % (8 * size) == 0


def peers(rank, size):
    if direct_sum(rank, size):
        return list(range(1, size))
    return [1 << shift for shift in range(bits_of(size))]


def sum_gram(me, size, gram_ref, parts, arrived, send_sem, recv_sem):
    if not direct_sum(parts.shape[0] * parts.shape[1], size):
        gram_ref[...] = parts[...].reshape(gram_ref.shape)
        for stage in range(bits_of(size)):
            copy = remote(
                gram_ref,
                arrived.at[stage],
                send_sem.at[stage],
                recv_sem.at[stage],
                partner_of(me, 1 << stage),
            )
            copy.start()
            copy.wait()
            gram_ref[...] += arrived[stage]
        return
    height = parts.shape[1]
    scatter = [
        remote(
            parts.at[partner_of(me, d)],
            arrived.at[d],
            send_sem.at[d],
            recv_sem.at[d],
            partner_of(me, d),
        )
        for d in range(1, size)
    ]
    for copy in scatter:
        copy.start()
    total = parts[me]
    for d, copy in enumerate(scatter, 1):
        copy.wait_recv()
        total = total + arrived[d]
    arrived[0] = total
    own = pl.ds(pl.multiple_of(me * height, height), height)
    gather = [
        remote(
            arrived.at[0],
            gram_ref.at[own],
            send_sem.at[size + d],
            recv_sem.at[size + d],
            partner_of(me, d),
        )
        for d in range(1, size)
    ]
    for copy in gather:
        copy.start()
    gram_ref[own, :] = total
    for copy in gather:
        copy.wait_recv()
    for copy in scatter + gather:
        copy.wait_send()


class Gather:
    UP, DOWN, ACROSS, BESIDE = range(4)

    def __init__(self, me, size, held, block, send_sem, recv_sem):
        self.me, self.size, self.held, self.block = me, size, held, block
        self.send_sem, self.recv_sem = send_sem, recv_sem
        self.layers = size // 4
        self.z = lax.div(me, 4)
        height = held.shape[1]
        first = height * 13 // 32 // 16 * 16
        self.cuts = [(0, first), (first, first), (2 * first, height - 2 * first)]
        self.has_up = self.z + 1 < self.layers
        self.has_down = self.z >= 1
        self.across = partner_of(me, 2)
        self.beside = partner_of(me, 1)
        self.peers = {
            self.UP: me + 4,
            self.DOWN: me - 4,
            self.ACROSS: self.across,
            self.BESIDE: self.beside,
        }

    def copy(self, owner, part, dest):
        start, rows = self.cuts[part]
        piece = self.held.at[owner, pl.ds(start, rows)]
        return remote(
            self.block.at[pl.ds(start, rows)] if owner is self.me else piece,
            piece,
            self.send_sem.at[dest, owner, part],
            self.recv_sem.at[owner, part],
            self.peers[dest],
        )

    def greet(self):
        barrier = pltpu.get_barrier_semaphore()

        def signal(dest):
            pl.semaphore_signal(
                barrier,
                inc=1,
                device_id={"pix": self.peers[dest]},
                device_id_type=pl.DeviceIdType.MESH,
            )

        signal(self.ACROSS)
        signal(self.BESIDE)
        pl.when(self.has_up)(lambda: signal(self.UP))
        pl.when(self.has_down)(lambda: signal(self.DOWN))
        neighbours = jnp.minimum(self.z, 1) + jnp.minimum(self.layers - 1 - self.z, 1)
        pl.semaphore_wait(barrier, 2 + neighbours)

    def moves(self):
        out = []
        for part in (2, 0, 1):
            out += [
                (None, self.me, part, self.ACROSS),
                (self.has_up, self.me, part, self.UP),
                (self.has_down, self.me, part, self.DOWN),
                (None, self.me, part, self.BESIDE),
            ]
        return out

    def begin(self, copies):
        for condition, owner, part, dest in copies:
            if condition is None:
                self.copy(owner, part, dest).start()
            else:
                pl.when(condition)(lambda o=owner, p=part, d=dest: self.copy(o, p, d).start())

    def finish(self, copies):
        for condition, owner, part, dest in copies:
            if condition is None:
                self.copy(owner, part, dest).wait_send()
            else:
                pl.when(condition)(lambda o=owner, p=part, d=dest: self.copy(o, p, d).wait_send())

    def arrived(self, owner, part):
        self.copy(owner, part, self.BESIDE).wait_recv()

    def events(self):
        up, down = (self.has_up, self.UP), (self.has_down, self.DOWN)
        across, beside = (None, self.ACROSS), (None, self.BESIDE)
        out = [[(None, self.across, 2, [up, down, beside])]]

        def along(step, part, side):
            start = self.me if side == 0 else self.across
            extra = [across] if part < 2 else []
            below = (self.z >= step, start - 4 * step, part, [up] + extra + [beside])
            above = (
                self.z + step < self.layers,
                start + 4 * step,
                part,
                [down] + extra + [beside],
            )
            return [below, above]

        def over(step, part):
            if step == 0:
                return [(None, self.across, part, [beside])]
            return [
                (self.z >= step, self.across - 4 * step, part, [beside]),
                (self.z + step < self.layers, self.across + 4 * step, part, [beside]),
            ]

        for step in range(1, self.layers):
            out.append(along(step, 0, 0) + along(step, 2, 0) + over(step - 1, 0))
            out.append(along(step, 1, 0) + along(step, 2, 1) + over(step - 1, 1))
        out.append(over(self.layers - 1, 0))
        out.append(over(self.layers - 1, 1))
        return out

    def handle(self, events):
        for condition, owner, part, dests in events:

            def act(owner=owner, part=part, dests=dests):
                self.arrived(owner, part)
                self.begin([(c, owner, part, d) for c, d in dests])

            if condition is None:
                act()
            else:
                pl.when(condition)(act)

    def close(self):
        self.finish(self.moves())
        for events in self.events():
            for condition, owner, part, dests in events:

                def act(owner=owner, part=part, dests=dests):
                    self.finish([(c, owner, part, d) for c, d in dests])

                if condition is None:
                    act()
                else:
                    pl.when(condition)(act)

    def await_beside(self, owner):
        for part in range(3):
            self.arrived(owner, part)


TURN = 2
FINISH = 3
AHEAD = 4
EARLY = (1, 2, 3, 5, 7)
GROWTH = 6.0


class Scatter:
    def __init__(self, gather, work, inbox, send_sem, recv_sem):
        self.gather = gather
        self.work, self.inbox = work, inbox
        self.send_sem, self.recv_sem = send_sem, recv_sem
        rank = work.shape[1]
        last = max(rank // 8 // 16 * 16, 16)
        first = (rank - last + 31) // 32 * 16
        self.cuts = [(0, first), (first, rank - last - first), (rank - last, last), (0, rank)]
        self.sent = []

    def copy(self, owner, part, dest):
        start, rows = self.cuts[part]
        slot = lax.div(owner, 2)
        place = part % 3
        return remote(
            self.work.at[owner, pl.ds(start, rows)],
            self.inbox.at[dest, slot, pl.ds(start, rows)],
            self.send_sem.at[dest, slot, place],
            self.recv_sem.at[dest, slot, place],
            self.gather.peers[dest],
        )

    def send(self, owner, part, dest, conditions):
        self.copy(owner, part, dest).start()
        self.sent.append((conditions, owner, part, dest))

    def take(self, owner, part, dest):
        start, rows = self.cuts[part]
        self.copy(owner, part, dest).wait_recv()
        piece = self.work.at[owner, pl.ds(start, rows)]
        got = self.inbox[dest, lax.div(owner, 2), pl.ds(start, rows)]
        piece[...] = (piece[...].astype(F32) + got.astype(F32)).astype(BF16)

    def close(self):
        for conditions, owner, part, dest in self.sent:
            wait = lambda o=owner, p=part, d=dest: self.copy(o, p, d).wait_send()
            for condition in conditions:
                wait = lambda c=condition, w=wait: pl.when(c)(w)
            wait()


def splat(values, row, col):
    return jnp.broadcast_to(values[row : row + 1, col : col + 1], values.shape)


def factor_step(block, left_ref, right_ref, inverse_ref):
    size = left_ref.shape[0]
    top, side = left_ref[0:8, :], right_ref[0:8, :]
    cell = {(r, c): splat(top, r, c) for r in range(8) for c in range(r + 1)}
    turn = {}
    for c in range(8):
        pivot = cell[c, c]
        guess = lax.rsqrt(pivot)
        scale = guess * (1.5 - 0.5 * pivot * guess * guess)
        turn[c, c] = scale
        for r in range(c + 1, 8):
            cell[r, c] = cell[r, c] * scale
        for r in range(c + 1, 8):
            for k in range(c + 1, r + 1):
                cell[r, k] = cell[r, k] - cell[r, c] * cell[k, c]
    for c in range(8):
        for r in range(c + 1, 8):
            total = cell[r, c] * turn[c, c]
            for k in range(c + 1, r):
                total = total + cell[r, k] * turn[k, c]
            turn[r, c] = -total * turn[r, r]
    row = lax.broadcasted_iota(jnp.int32, top.shape, 0)
    lane = lax.broadcasted_iota(jnp.int32, top.shape, 1)
    upper, lower = jnp.zeros_like(top), jnp.zeros_like(side)
    for c in range(8):
        weight = jnp.zeros_like(top)
        for r in range(c, 8):
            weight = jnp.where(row == r, turn[r, c], weight)
        upper = upper + weight * top[c : c + 1, :]
        lower = lower + weight * side[c : c + 1, :]
    inverse_ref[pl.ds(pl.multiple_of(8 * block, 8), 8), :] = lower
    upper = jnp.where((lane >= row) & (lane < size - 8 * block), upper, 0.0)
    both = jnp.concatenate([upper, lower], axis=1)
    change = lax.dot_general(
        upper, both, (((0,), (0,)), ((), ())), precision=HIGHEST, preferred_element_type=F32
    )
    left = pltpu.roll(left_ref[...] - change[:, :size], size - 8, 1)
    left_ref[0 : size - 8, :] = left[8:]
    left_ref[size - 8 : size, :] = jnp.zeros_like(top)
    right = right_ref[...] - change[:, size:]
    right_ref[0 : size - 8, :] = right[8:]
    right_ref[size - 8 : size, :] = jnp.zeros_like(side)


class GramSum:
    def __init__(self, me, size, gram_ref, parts, arrived, send_sem, recv_sem):
        self.me, self.size, self.gram_ref = me, size, gram_ref
        self.parts, self.arrived = parts, arrived
        self.send_sem, self.recv_sem = send_sem, recv_sem
        self.direct = direct_sum(parts.shape[0] * parts.shape[1], size)

    def scatter(self, d):
        peer = partner_of(self.me, d)
        return remote(
            self.parts.at[peer],
            self.arrived.at[d],
            self.send_sem.at[d],
            self.recv_sem.at[d],
            peer,
        )

    def gather(self, d):
        height = self.parts.shape[1]
        own = pl.ds(pl.multiple_of(self.me * height, height), height)
        return remote(
            self.arrived.at[0],
            self.gram_ref.at[own],
            self.send_sem.at[self.size + d],
            self.recv_sem.at[self.size + d],
            partner_of(self.me, d),
        )

    def start(self):
        if self.direct:
            for d in range(1, self.size):
                self.scatter(d).start()

    def turn(self):
        if not self.direct:
            sum_gram(
                self.me,
                self.size,
                self.gram_ref,
                self.parts,
                self.arrived,
                self.send_sem,
                self.recv_sem,
            )
            return
        total = self.parts[self.me]
        for d in range(1, self.size):
            self.scatter(d).wait_recv()
            total = total + self.arrived[d]
        self.arrived[0] = total
        for d in range(1, self.size):
            self.gather(d).start()
        height = self.parts.shape[1]
        self.gram_ref[pl.ds(pl.multiple_of(self.me * height, height), height), :] = total

    def finish(self):
        if self.direct:
            for d in range(1, self.size):
                self.gather(d).wait_recv()

    def close(self):
        if self.direct:
            for d in range(1, self.size):
                self.scatter(d).wait_send()
                self.gather(d).wait_send()


def build_filters(defocus_ref, waves, filters):
    number, length, _ = filters.shape
    index = lax.broadcasted_iota(jnp.int32, (1, length), 1)
    freq = jnp.where(index < length // 2, index, index - length).astype(F32) / length
    square = freq * freq

    def phase(group, _):
        waves[0, pl.ds(group, 1), :] = (math.pi * defocus_ref[group]) * square

    lax.fori_loop(0, number, phase, None)
    phases = waves[0, 0:number, :]
    sine, cosine = jnp.sin(phases), jnp.cos(phases)
    waves[0, 0:number, :] = sine
    waves[1, 0:number, :] = cosine
    keep = math.sqrt(1.0 - AMPLITUDE**2)
    rest = jnp.zeros((length - number, length), F32)
    first = jnp.concatenate([keep * sine + AMPLITUDE * cosine, rest], axis=0).T
    second = jnp.concatenate([keep * cosine - AMPLITUDE * sine, rest], axis=0).T

    def twice(axis):
        place = lax.broadcasted_iota(jnp.int32, (length, length), axis)
        return jnp.where((place == 0) | (place == length // 2), 1.0, 2.0)

    scale = twice(0) * twice(1) / float(length * length)

    def eight(block, both):
        left, right = both
        for i in range(8):
            group = 8 * block + i
            contrast = -(
                left[:, i : i + 1] * waves[1, pl.ds(group, 1), :]
                + right[:, i : i + 1] * waves[0, pl.ds(group, 1), :]
            )
            wiener = (contrast / (contrast * contrast + WIENER)).astype(BF16).astype(F32)
            filters[group] = (wiener * scale).astype(BF16)
        return pltpu.roll(left, length - 8, 1), pltpu.roll(right, length - 8, 1)

    lax.fori_loop(0, number // 8, eight, (first, second))


def whole_kernel(
    size,
    count,
    stride,
    group_ref,
    live_ref,
    defocus_ref,
    image_hbm,
    matrix_hbm,
    pair_hbm,
    pair_t_hbm,
    basis_ref,
    out_ref,
    growth_ref,
    pair_ref,
    pair_t_ref,
    waves,
    filters,
    images_ref,
    turned,
    columns,
    held,
    sketch_ref,
    gram_ref,
    parts,
    arrived,
    left_ref,
    right_ref,
    inverse_ref,
    work,
    inbox,
    load_sem,
    own_sem,
    send_sem,
    recv_sem,
    sum_send_sem,
    sum_recv_sem,
    back_send_sem,
    back_recv_sem,
):
    me = lax.axis_index("pix")
    step = pl.program_id(0)
    length, slots, _ = columns.shape
    rank = sketch_ref.shape[1]
    steps = slots // count
    pairs = count // 2
    base = step * count
    gather = Gather(me, size, held, matrix_hbm, send_sem, recv_sem)
    events = gather.events()

    def load(i):
        rows = pl.ds(i * count, count)
        return pltpu.make_async_copy(image_hbm.at[rows], images_ref.at[rows], load_sem.at[i])

    @pl.when(step == 0)
    def _():
        gather.greet()
        gather.begin(gather.moves())
        small = [
            pltpu.make_async_copy(pair_hbm, pair_ref, own_sem.at[0]),
            pltpu.make_async_copy(pair_t_hbm, pair_t_ref, own_sem.at[1]),
            pltpu.make_async_copy(matrix_hbm, held.at[me], own_sem.at[2]),
        ]
        for copy in small:
            copy.start()
        for i in range(min(AHEAD, steps)):
            load(i).start()
        build_filters(defocus_ref, waves, filters)
        for copy in small:
            copy.wait()

    @pl.when((step >= 1) & (step + AHEAD - 1 < steps))
    def _():
        load(step + AHEAD - 1).start()

    early = [place for place in EARLY if place < steps][: len(events)]
    for i, place in enumerate(early):

        @pl.when(step == place)
        def _(i=i):
            gather.handle(events[i])

    load(step).wait()

    def side_by_side(values):
        return jnp.concatenate(values, axis=1)

    def product(left, right):
        return jnp.dot(left, right, preferred_element_type=F32)

    def quads(left, right):
        width = 2 * length
        return jnp.concatenate(
            [product(left, right[i : i + width]) for i in range(0, pairs * length, width)], axis=0
        )

    images = jnp.concatenate(
        [
            side_by_side([images_ref[base + 2 * i], images_ref[base + 2 * i + 1]])
            for i in range(pairs)
        ],
        axis=0,
    )
    weights = jnp.concatenate(
        [
            side_by_side(
                [filters[group_ref[base + 2 * i]], filters[group_ref[base + 2 * i + 1]]]
            )
            for i in range(pairs)
        ],
        axis=0,
    )
    rows = product(images, pair_ref[...]).astype(BF16)
    spectrum = quads(pair_t_ref[...], rows)
    kept = (spectrum * weights.astype(F32)).astype(BF16)
    back = product(kept, pair_t_ref[...]).astype(BF16)
    result = quads(pair_ref[...], back)
    for i in range(count):
        tall, wide = i // 2 * length, i % 2 * length
        turned[pl.ds(i, length, stride=stride), :] = result[
            tall : tall + length, wide : wide + length
        ]
    slot = base + lax.broadcasted_iota(jnp.int32, (1, count, 1), 1)
    values = turned[...].reshape(length, stride, length)[:, :count]
    columns[:, pl.ds(pl.multiple_of(base, count), count), :] = jnp.where(
        slot < live_ref[0], values, 0.0
    ).astype(BF16)

    @pl.when(step == steps - 1)
    def _():
        lines = length // size
        layers = gather.layers
        z = gather.z

        def pixels(owner):
            return side_by_side([columns[owner * lines + line] for line in range(lines)])

        def chip(start, distance):
            def act(owner):
                other = partner_of(owner, 1)
                sketch_ref[...] += product(pixels(owner), held[owner])
                gather.await_beside(other)
                sketch_ref[...] += product(pixels(other), held[other])

            if not distance:
                act(start)
                return
            pl.when(z >= distance)(lambda: act(start - 4 * distance))
            pl.when(z + distance < layers)(lambda: act(start + 4 * distance))

        sketch_ref[...] = jnp.zeros_like(sketch_ref)
        chips = [(0, me, 0), (2, gather.across, 0)]
        for distance in range(1, layers):
            chips.append((2 * distance, me, distance))
            chips.append((2 * distance + 2, gather.across, distance))
        for k in range(len(early), len(events)):
            gather.handle(events[k])
            for _ in range(3):
                if chips and chips[0][0] <= k:
                    chip(*chips.pop(0)[1:])
        for _, start, distance in chips:
            chip(start, distance)
        sketch = sketch_ref[...]
        sketch_t = sketch.T.astype(BF16)
        scatter = Scatter(gather, work, inbox, back_send_sem, back_recv_sem)
        total = GramSum(me, size, gram_ref, parts, arrived, sum_send_sem, sum_recv_sem)
        up, down, across, beside = gather.UP, gather.DOWN, gather.ACROSS, gather.BESIDE

        def ways(distance):
            out = []
            for upwards in (False, True) if distance else (True,):
                own = me + (4 * distance if upwards else -4 * distance)
                other = partner_of(own, 2)
                there = z + distance < layers if upwards else z >= distance
                given = [there] if distance else []
                out.append((given, upwards, own, other, partner_of(own, 1), partner_of(other, 1)))
            return out

        def run(given, act):
            pl.when(given[0])(act) if given else act()

        def compute(distance):
            for given, upwards, own, other, own_beside, other_beside in ways(distance):

                def act():
                    for owner, aside in ((other, other_beside), (own, own_beside)):
                        work[aside] = product(sketch_t, pixels(aside)).astype(BF16)
                        scatter.send(aside, 3, beside, given)
                        work[owner] = product(sketch_t, pixels(owner)).astype(BF16)

                run(given, act)

        def onward(owner, part, upwards, given):
            way, ahead = (up, gather.has_down) if upwards else (down, gather.has_up)
            pl.when(ahead)(lambda: scatter.take(owner, part, way))
            scatter.send(owner, part, way, given)

        def chip_sum(distance):
            for given, upwards, own, other, _, _ in ways(distance):

                def act():
                    scatter.take(other, 3, beside)
                    for part in range(2):
                        scatter.send(other, part, across, given)
                    scatter.take(own, 3, beside)

                run(given, act)

        def third(distance):
            for given, upwards, own, other, _, _ in ways(distance):

                def act():
                    onward(other, 2, upwards, given)
                    onward(own, 2, upwards, given)

                run(given, act)

        def along(distance, part):
            for given, upwards, own, _, _, _ in ways(distance):

                def act():
                    scatter.take(own, part, across)
                    if distance:
                        onward(own, part, upwards, given)

                run(given, act)

        def last(owner, part):
            pl.when(gather.has_down)(lambda: scatter.take(owner, part, up))
            pl.when(gather.has_up)(lambda: scatter.take(owner, part, down))

        compute(layers - 1)
        gram = lax.dot_general(
            sketch, sketch, (((0,), (0,)), ((), ())), precision=HIGHEST, preferred_element_type=F32
        )
        parts[...] = gram.reshape(parts.shape)
        total.start()
        for distance in range(layers - 1, -1, -1):
            chip_sum(distance)
            if distance == layers - 1 and distance:
                third(distance)
            if distance:
                compute(distance - 1)
            if distance == max(layers - TURN, 0):
                total.turn()
        for distance in range(layers - 2, 0, -1):
            third(distance)
        todo = [(distance, part) for distance in range(layers - 1, 0, -1) for part in range(2)]
        for place in todo[:FINISH]:
            along(*place)
        total.finish()
        unit = lax.broadcasted_iota(jnp.int32, (rank, rank), 0) == lax.broadcasted_iota(
            jnp.int32, (rank, rank), 1
        )
        left_ref[...] = gram_ref[...]
        right_ref[...] = jnp.where(unit, 1.0, 0.0)
        blocks = rank // 8
        todo = todo[FINISH:]
        for i in range(len(todo) + 1):
            lax.fori_loop(
                blocks * i // (len(todo) + 1),
                blocks * (i + 1) // (len(todo) + 1),
                lambda block, _: factor_step(block, left_ref, right_ref, inverse_ref),
                None,
            )
            if i < len(todo):
                along(*todo[i])
        inverse = inverse_ref[...]
        basis_ref[...] = lax.dot_general(
            sketch,
            inverse,
            (((1,), (1,)), ((), ())),
            precision=HIGHEST,
            preferred_element_type=F32,
        ).astype(BF16)
        scale = jnp.sqrt(jnp.sum(inverse * inverse, axis=0, keepdims=True))
        sums = jnp.dot(
            jnp.broadcast_to(scale, (8, rank)),
            jnp.abs(gram_ref[...]),
            precision=HIGHEST,
            preferred_element_type=F32,
        )
        growth_ref[0] = jnp.where(jnp.max(sums * scale) <= GROWTH, 1, 0)
        last(gather.across, 2)
        scatter.send(gather.across, 2, across, [])
        last(me, 2)
        for part in range(2):
            along(0, part)
            last(me, part)
        scatter.take(me, 2, across)
        mine = jnp.dot(
            inverse, work[me].astype(F32), precision=HIGHEST, preferred_element_type=F32
        )
        out_ref[...] = mine.T
        gather.close()
        scatter.close()
        total.close()


def make_whole(images, groups, live, defocus_values, matrix, size):
    slots, length, _ = images.shape
    height, rank = matrix.shape
    count = math.gcd(slots, 32)
    stride = count + 4
    pair, pair_t = pair_tables(length)
    number = defocus_values.shape[0]
    if direct_sum(rank, size):
        summing = [pltpu.VMEM((size, rank // size, rank), F32)] * 2
        signals = 2 * size
    else:
        summing = [
            pltpu.VMEM((1, rank, rank), F32),
            pltpu.VMEM((bits_of(size), rank, rank), F32),
        ]
        signals = bits_of(size)

    def whole(*shape):
        return pl.BlockSpec(shape, lambda i, *_: (0,) * len(shape))

    square = pltpu.VMEM((rank, rank), F32)
    return pl.pallas_call(
        functools.partial(whole_kernel, size, count, stride),
        out_shape=(
            jax.ShapeDtypeStruct((slots, rank), BF16),
            jax.ShapeDtypeStruct((height, rank), F32),
            jax.ShapeDtypeStruct((1,), jnp.int32),
        ),
        grid_spec=pltpu.PrefetchScalarGridSpec(
            num_scalar_prefetch=2,
            grid=(slots // count,),
            in_specs=[
                pl.BlockSpec(memory_space=pltpu.SMEM),
                *[pl.BlockSpec(memory_space=pl.ANY)] * 4,
            ],
            out_specs=(
                whole(slots, rank),
                whole(height, rank),
                pl.BlockSpec(memory_space=pltpu.SMEM),
            ),
            scratch_shapes=[
                pltpu.VMEM((2 * length, 2 * length), BF16),
                pltpu.VMEM((2 * length, 2 * length), BF16),
                pltpu.VMEM((2, number, length), F32),
                pltpu.VMEM((number, length, length), BF16),
                pltpu.VMEM((slots, length, length), BF16),
                pltpu.VMEM((length * stride, length), F32),
                pltpu.VMEM((length, slots, length), BF16),
                pltpu.VMEM((size, height, rank), BF16),
                pltpu.VMEM((slots, rank), F32),
                square,
                *summing,
                square,
                square,
                square,
                pltpu.VMEM((size, rank, height), BF16),
                pltpu.VMEM((4, size // 2, rank, height), BF16),
                pltpu.SemaphoreType.DMA((slots // count,)),
                pltpu.SemaphoreType.DMA((3,)),
                pltpu.SemaphoreType.DMA((4, size, 3)),
                pltpu.SemaphoreType.DMA((size, 3)),
                pltpu.SemaphoreType.DMA((signals,)),
                pltpu.SemaphoreType.DMA((signals,)),
                pltpu.SemaphoreType.DMA((4, size // 2, 3)),
                pltpu.SemaphoreType.DMA((4, size // 2, 3)),
            ],
        ),
        compiler_params=pltpu.CompilerParams(
            collective_id=0, has_side_effects=True, vmem_limit_bytes=56 << 20
        ),
        name="whole",
    )(groups, live, defocus_values, images, matrix, pair, pair_t)


def sketch_kernel(
    size,
    group_ref,
    live_ref,
    image_ref,
    matrix_ref,
    filters,
    pair_ref,
    pair_t_ref,
    table_ref,
    table_t_ref,
    out_ref,
    sketch_ref,
    gram_ref,
    turned,
    held,
    summed,
    parts,
    arrived,
    send_sem,
    recv_sem,
    sum_send_sem,
    sum_recv_sem,
):
    me = lax.axis_index("pix")
    step = pl.program_id(0)
    steps = out_ref.shape[1] // image_ref.shape[0]
    count, length, _ = image_ref.shape
    pairs = count // 2
    base = step * count
    orders = gathering_orders(size)
    stages = bits_of(size)
    height = matrix_ref.shape[0] // 2

    def copy_of(half, stage, mask):
        bit = orders[half][stage]
        slot = (bit | mask) - 1
        return remote(
            held.at[half, mask],
            held.at[half, bit | mask],
            send_sem.at[half, slot],
            recv_sem.at[half, slot],
            partner_of(me, bit),
        )

    def receive(stage, half, mask):
        copy_of(half, stage, mask).wait_recv()
        for later in range(stage + 1, stages):
            copy_of(half, later, orders[half][stage] | mask).start()

    @pl.when(step == 0)
    def _():
        greet(me, peers(gram_ref.shape[0], size))
        for half in range(2):
            held[half, 0] = matrix_ref[half * height : (half + 1) * height, :]
        for stage in range(stages):
            for half in range(2):
                copy_of(half, stage, 0).start()

    early = min(2, stages)
    for stage in range(early):

        @pl.when(step == steps * (5 + 6 * stage) // 16)
        def _(stage=stage):
            for place in range(1 << stage):
                for half in range(2):
                    receive(stage, half, sums(orders[half][:stage])[place])

    def side_by_side(values):
        return jnp.concatenate(values, axis=1)

    def stacked(wide):
        return jnp.concatenate(
            [wide[:, 2 * length * i : 2 * length * (i + 1)] for i in range(pairs)], axis=0
        )

    def unstacked(tall):
        return side_by_side([tall[length * i : length * (i + 1)] for i in range(pairs)])

    images = jnp.concatenate(
        [side_by_side([image_ref[2 * i], image_ref[2 * i + 1]]) for i in range(pairs)], axis=0
    )
    rows = jnp.dot(images, pair_ref[...], preferred_element_type=F32).astype(BF16)
    spectrum = jnp.dot(table_t_ref[...], unstacked(rows), preferred_element_type=F32)
    weights = side_by_side([filters[group_ref[base + i]] for i in range(count)])
    kept = (spectrum * weights.astype(F32)).astype(BF16)
    back = jnp.dot(stacked(kept), pair_t_ref[...], preferred_element_type=F32).astype(BF16)
    result = jnp.dot(table_ref[...], unstacked(back), preferred_element_type=F32)
    for i in range(count):
        turned[pl.ds(i, length, stride=count), :] = result[:, i * length : (i + 1) * length]
    slot = base + lax.broadcasted_iota(jnp.int32, (1, count, 1), 1)
    values = turned[...].reshape(length, count, length)
    out_ref[:, pl.ds(pl.multiple_of(base, count), count), :] = jnp.where(
        slot < live_ref[0], values, 0.0
    ).astype(BF16)

    @pl.when(step == steps - 1)
    def _():
        lines = length // size
        part = lines // 2

        def term(half, mask):
            start = partner_of(me, mask) * lines + half * part
            left = side_by_side([out_ref[start + line] for line in range(part)])
            return jnp.dot(left, held[half, mask], preferred_element_type=F32)

        sketch_ref[...] = jnp.zeros_like(sketch_ref)
        for half in range(2):
            for mask in sums(orders[half][:early]):
                sketch_ref[...] += term(half, mask)
        for stage in range(early, stages):
            for place in range(1 << stage):
                for half in range(2):
                    mask = sums(orders[half][:stage])[place]
                    receive(stage, half, mask)
                    sketch_ref[...] += term(half, orders[half][stage] | mask)
        sketch = sketch_ref[...]
        gram = lax.dot_general(
            sketch, sketch, (((0,), (0,)), ((), ())), precision=HIGHEST, preferred_element_type=F32
        )
        parts[...] = gram.reshape(parts.shape)
        sum_gram(me, size, summed, parts, arrived, sum_send_sem, sum_recv_sem)
        gram_ref[...] = summed[...]
        for half in range(2):
            for stage in range(stages):
                for mask in sums(orders[half][:stage]):
                    copy_of(half, stage, mask).wait_send()


def make_sketch(images, groups, live, defocus_values, matrix, size):
    slots, length, _ = images.shape
    height, rank = matrix.shape
    count = math.gcd(slots, 16)
    table = real_tables(length)
    zero = jnp.zeros_like(table)
    pair = jnp.concatenate(
        [jnp.concatenate([table, zero], axis=1), jnp.concatenate([zero, table], axis=1)], axis=0
    )
    number = defocus_values.shape[0]
    if direct_sum(rank, size):
        summing = [
            pltpu.VMEM((size, rank // size, rank), F32),
            pltpu.VMEM((size, rank // size, rank), F32),
        ]
        signals = 2 * size
    else:
        summing = [
            pltpu.VMEM((1, rank, rank), F32),
            pltpu.VMEM((bits_of(size), rank, rank), F32),
        ]
        signals = bits_of(size)

    def whole(*shape):
        return pl.BlockSpec(shape, lambda i, *_: (0,) * len(shape))

    return pl.pallas_call(
        functools.partial(sketch_kernel, size),
        out_shape=(
            jax.ShapeDtypeStruct((length, slots, length), BF16),
            jax.ShapeDtypeStruct((slots, rank), F32),
            jax.ShapeDtypeStruct((rank, rank), F32),
        ),
        grid_spec=pltpu.PrefetchScalarGridSpec(
            num_scalar_prefetch=2,
            grid=(slots // count,),
            in_specs=[
                pl.BlockSpec((count, length, length), lambda i, *_: (i, 0, 0)),
                whole(height, rank),
                whole(number, length, length),
                whole(2 * length, 2 * length),
                whole(2 * length, 2 * length),
                whole(length, length),
                whole(length, length),
            ],
            out_specs=(whole(length, slots, length), whole(slots, rank), whole(rank, rank)),
            scratch_shapes=[
                pltpu.VMEM((length * count, length), F32),
                pltpu.VMEM((2, size, height // 2, rank), BF16),
                pltpu.VMEM((rank, rank), F32),
                *summing,
                pltpu.SemaphoreType.DMA((2, size - 1)),
                pltpu.SemaphoreType.DMA((2, size - 1)),
                pltpu.SemaphoreType.DMA((signals,)),
                pltpu.SemaphoreType.DMA((signals,)),
            ],
        ),
        compiler_params=pltpu.CompilerParams(
            collective_id=1, has_side_effects=True, vmem_limit_bytes=50 << 20
        ),
        name="sketch",
    )(
        groups,
        live,
        images,
        matrix,
        filter_table(defocus_values, length),
        pair,
        pair.T,
        table,
        table.T,
    )


def basis_kernel(factor_ref, sketch_ref, out_ref, turned_ref):
    rank = factor_ref.shape[0]
    row = lax.broadcasted_iota(jnp.int32, (rank, rank), 0)
    col = lax.broadcasted_iota(jnp.int32, (rank, rank), 1)
    factor = factor_ref[...]
    on_diagonal = jnp.where(row == col, factor, 0.0)
    lower = jnp.where(row > col, factor, 0.0) / jnp.sum(on_diagonal, axis=1, keepdims=True)

    def times(left, right):
        return jnp.dot(left, right, precision=HIGHEST, preferred_element_type=F32)

    def same_block(shift):
        return lax.shift_right_logical(row, shift) == lax.shift_right_logical(col, shift)

    shift = 3
    within = jnp.where(same_block(shift), lower, 0.0)
    unit = jnp.where(row == col, 1.0, 0.0).astype(F32)
    square = times(within, within)
    fourth = times(square, square)
    inverse = times(times(unit - within, unit + square), unit + fourth)
    while 1 << shift < rank:
        off = jnp.where(same_block(shift + 1) & ~same_block(shift), lower, 0.0)
        inverse = inverse - times(inverse, times(off, inverse))
        shift += 1
    inverse = inverse / jnp.sum(on_diagonal, axis=0, keepdims=True)
    basis = lax.dot_general(
        sketch_ref[...],
        inverse,
        (((1,), (1,)), ((), ())),
        precision=HIGHEST,
        preferred_element_type=F32,
    )
    out_ref[...] = basis.astype(BF16)
    turned_ref[...] = basis.T.astype(BF16)


def make_basis(factor_low, sketch):
    slots, rank = sketch.shape
    return pl.pallas_call(
        basis_kernel,
        out_shape=(
            jax.ShapeDtypeStruct((slots, rank), BF16),
            jax.ShapeDtypeStruct((rank, slots), BF16),
        ),
        name="basis",
    )(factor_low, sketch)


def project_kernel(size, basis_ref, column_ref, out_ref, held, arrived, send_sem, recv_sem):
    me = lax.axis_index("pix")
    length = column_ref.shape[0]
    rows = length // size
    part = rows // 2
    orders = halving_orders(size)
    slots = {}
    for half in range(2):
        for stage in range(len(orders[half])):
            for mask in masks_of(orders[half][stage + 1 :]):
                slots[half, stage, mask] = len(slots) % (size - 1)

    def copy_of(half, stage, mask):
        bit = orders[half][stage]
        slot = slots[half, stage, mask]
        return remote(
            held.at[half, bit | mask],
            arrived.at[half, slot],
            send_sem.at[half, slot],
            recv_sem.at[half, slot],
            partner_of(me, bit),
        )

    greet(me, [1 << shift for shift in range(bits_of(size))])
    first = orders[0][0]

    def compute(half, mask):
        start = partner_of(me, mask) * rows + half * part
        right = jnp.concatenate([column_ref[start + row] for row in range(part)], axis=1)
        held[half, mask] = jnp.dot(
            basis_ref[...], right, preferred_element_type=F32
        ).astype(BF16)

    def add(half, stage, mask):
        later = orders[half][stage + 1 :]
        copy_of(half, stage, mask).wait_recv()
        total = (
            held[half, mask].astype(F32)
            + arrived[half, slots[half, stage, mask]].astype(F32)
        )
        if later:
            held[half, mask] = total.astype(BF16)
            if mask & later[0]:
                copy_of(half, stage + 1, mask - later[0]).start()
        else:
            height = out_ref.shape[0] // 2
            out_ref[half * height : (half + 1) * height, :] = total.T

    kept = [masks_of(orders[half][1:]) for half in range(2)]
    for place in range(len(kept[0]) + 1):
        for half in range(2):
            if place < len(kept[0]):
                mask = kept[half][place]
                compute(half, first | mask)
                copy_of(half, 0, mask).start()
                compute(half, mask)
        for half in range(2):
            if place > 0:
                add(half, 0, kept[half][place - 1])
    for stage in range(1, bits_of(size)):
        for place in range(len(masks_of(orders[0][stage + 1 :]))):
            for half in range(2):
                add(half, stage, masks_of(orders[half][stage + 1 :])[place])
    for half in range(2):
        for stage in range(bits_of(size)):
            for mask in masks_of(orders[half][stage + 1 :]):
                copy_of(half, stage, mask).wait_send()


def project(columns, basis_t, size):
    length, slots, _ = columns.shape
    rank = basis_t.shape[0]
    width = length * length // size
    return pl.pallas_call(
        functools.partial(project_kernel, size),
        out_shape=jax.ShapeDtypeStruct((width, rank), F32),
        in_specs=[pl.BlockSpec(memory_space=pltpu.VMEM)] * 2,
        out_specs=pl.BlockSpec(memory_space=pltpu.VMEM),
        scratch_shapes=[
            pltpu.VMEM((2, size, rank, width // 2), BF16),
            pltpu.VMEM((2, size - 1, rank, width // 2), BF16),
            pltpu.SemaphoreType.DMA((2, size - 1)),
            pltpu.SemaphoreType.DMA((2, size - 1)),
        ],
        compiler_params=pltpu.CompilerParams(
            collective_id=2, has_side_effects=True, vmem_limit_bytes=48 << 20
        ),
        name="project",
    )(basis_t, columns)


def per_device(particle_images, defocus_group, live_counts, defocus_values, test_matrix):
    size = lax.axis_size("pix")
    arguments = (particle_images, defocus_group, live_counts, defocus_values, test_matrix, size)
    basis, projection, growth = make_whole(*arguments)

    def stepwise():
        columns, sketch, gram = make_sketch(*arguments)
        factor_low = jnp.linalg.cholesky(gram)
        range_basis, basis_t = make_basis(factor_low, sketch)
        return (range_basis, project(columns, basis_t, size))

    return lax.cond(growth[0] != 0, lambda: (basis, projection), stepwise)


def solution(mesh):
    placed = (
        P(("grp", "pix"), None, None),
        P(("grp", "pix")),
        P(("grp", "pix")),
        P("grp"),
        P(("grp", "pix"), None),
    )
    return jax.shard_map(
        per_device,
        mesh=mesh,
        in_specs=placed,
        out_specs=(P(("grp", "pix"), None), P(("grp", "pix"), None)),
        check_vma=False,
    )
```

```python
import functools
import math

import jax
import jax.numpy as jnp
import ml_dtypes
import numpy as np
from jax import lax
from jax.experimental import pallas as pl
from jax.experimental.pallas import tpu as pltpu
from jax.sharding import PartitionSpec as P

AMPLITUDE = 0.1
WIENER = 0.1
F32 = jnp.float32
BF16 = jnp.bfloat16
HIGHEST = lax.Precision.HIGHEST


def real_tables(length):
    rows = np.arange(length)
    angles = 2.0 * math.pi / length * (rows[:, None] * rows[None, :] % length)
    packed = np.where(rows[None, :] <= length // 2, np.cos(angles), np.sin(angles))
    return jnp.asarray(packed.astype(np.float32)).astype(BF16)


def pair_tables(length):
    rows, half = np.arange(length), length // 2
    freq = np.where(rows <= half, rows, rows - half)
    angles = 2.0 * math.pi / length * (rows[:, None] * freq[None, :] % length)
    packed = np.where(rows[None, :] <= half, np.cos(angles), np.sin(angles))
    packed = packed.astype(ml_dtypes.bfloat16).astype(np.float32)
    weighted = packed * np.where(rows % half == 0, 1.0, 2.0)[None, :] / length
    out = np.zeros((4, 2, length, 2, length), np.float32)
    for i, table in enumerate((packed, packed.T, weighted.T, weighted)):
        out[i, 0, :, 0] = out[i, 1, :, 1] = table
    return jnp.asarray(out.reshape(4, 2 * length, 2 * length).astype(ml_dtypes.bfloat16))


def filter_table(defocus_values, length):
    index = jnp.arange(length, dtype=jnp.int32)
    freq = jnp.where(index < length // 2, index, index - length).astype(F32) / length
    phase = jnp.pi * defocus_values[:, None] * (freq * freq)[None, :]
    sine, cosine = lax.optimization_barrier((jnp.sin(phase), jnp.cos(phase)))
    keep = math.sqrt(1.0 - AMPLITUDE**2)
    first = (keep * sine + AMPLITUDE * cosine)[:, :, None]
    second = (keep * cosine - AMPLITUDE * sine)[:, :, None]
    contrast = -(first * cosine[:, None, :] + second * sine[:, None, :])
    wiener = (contrast / (contrast * contrast + WIENER)).astype(BF16).astype(F32)
    twice = jnp.where((index == 0) | (index == length // 2), 1.0, 2.0).astype(F32)
    return (wiener * (twice[:, None] * twice[None, :] / float(length * length))).astype(BF16)


def bits_of(size):
    return size.bit_length() - 1


def partner_of(me, mask):
    for shift in range(mask.bit_length()):
        bit = 1 << shift
        if mask & bit:
            me = me + bit * (1 - 2 * lax.rem(lax.div(me, bit), 2))
    return me


def greet(me, masks):
    barrier = pltpu.get_barrier_semaphore()
    for mask in masks:
        pl.semaphore_signal(
            barrier,
            inc=1,
            device_id={"pix": partner_of(me, mask)},
            device_id_type=pl.DeviceIdType.MESH,
        )
    pl.semaphore_wait(barrier, len(masks))


def remote(src, dst, send_sem, recv_sem, peer):
    return pltpu.make_async_remote_copy(
        src_ref=src,
        dst_ref=dst,
        send_sem=send_sem,
        recv_sem=recv_sem,
        device_id={"pix": peer},
        device_id_type=pl.DeviceIdType.MESH,
    )


def halving_orders(size):
    bits = [1 << shift for shift in range(bits_of(size))]
    if len(bits) < 3:
        return (bits, bits)
    return (bits, bits[:1] + bits[2:] + bits[1:2])


def masks_of(bits):
    if not bits:
        return [0]
    rest = masks_of(bits[1:])
    return [bits[0] | mask for mask in rest] + rest


def gathering_orders(size):
    first, second = halving_orders(size)
    return (first[::-1], second[1:][::-1] + second[:1])


def sums(bits):
    out = [0]
    for bit in bits:
        out = out + [bit | mask for mask in out]
    return out


def direct_sum(rank, size):
    return rank % (8 * size) == 0


def peers(rank, size):
    if direct_sum(rank, size):
        return list(range(1, size))
    return [1 << shift for shift in range(bits_of(size))]


def sum_gram(me, size, gram_ref, parts, arrived, send_sem, recv_sem):
    if not direct_sum(parts.shape[0] * parts.shape[1], size):
        gram_ref[...] = parts[...].reshape(gram_ref.shape)
        for stage in range(bits_of(size)):
            copy = remote(
                gram_ref,
                arrived.at[stage],
                send_sem.at[stage],
                recv_sem.at[stage],
                partner_of(me, 1 << stage),
            )
            copy.start()
            copy.wait()
            gram_ref[...] += arrived[stage]
        return
    height = parts.shape[1]
    scatter = [
        remote(
            parts.at[partner_of(me, d)],
            arrived.at[d],
            send_sem.at[d],
            recv_sem.at[d],
            partner_of(me, d),
        )
        for d in range(1, size)
    ]
    for copy in scatter:
        copy.start()
    total = parts[me]
    for d, copy in enumerate(scatter, 1):
        copy.wait_recv()
        total = total + arrived[d]
    arrived[0] = total
    own = pl.ds(pl.multiple_of(me * height, height), height)
    gather = [
        remote(
            arrived.at[0],
            gram_ref.at[own],
            send_sem.at[size + d],
            recv_sem.at[size + d],
            partner_of(me, d),
        )
        for d in range(1, size)
    ]
    for copy in gather:
        copy.start()
    gram_ref[own, :] = total
    for copy in gather:
        copy.wait_recv()
    for copy in scatter + gather:
        copy.wait_send()


class Gather:
    UP, DOWN, ACROSS, BESIDE = range(4)

    def __init__(self, me, size, held, block, send_sem, recv_sem):
        self.me, self.size, self.held, self.block = me, size, held, block
        self.send_sem, self.recv_sem = send_sem, recv_sem
        self.layers = size // 4
        self.z = lax.div(me, 4)
        height = held.shape[1]
        first = height * 13 // 32 // 16 * 16
        self.cuts = [(0, first), (first, first), (2 * first, height - 2 * first)]
        self.has_up = self.z + 1 < self.layers
        self.has_down = self.z >= 1
        self.across = partner_of(me, 2)
        self.beside = partner_of(me, 1)
        self.peers = {
            self.UP: me + 4,
            self.DOWN: me - 4,
            self.ACROSS: self.across,
            self.BESIDE: self.beside,
        }

    def copy(self, owner, part, dest):
        start, rows = self.cuts[part]
        piece = self.held.at[owner, pl.ds(start, rows)]
        return remote(
            self.block.at[pl.ds(start, rows)] if owner is self.me else piece,
            piece,
            self.send_sem.at[self.signal(owner, part, dest)],
            self.recv_sem.at[owner, part],
            self.peers[dest],
        )

    def signal(self, owner, part, dest):
        chips = self.size // 2
        if dest == self.ACROSS:
            return 6 * chips + lax.div(owner, 4) * 3 + part
        first = {self.UP: 0, self.DOWN: 3 * chips, self.BESIDE: 6 * chips + 3 * self.layers}
        return first[dest] + lax.div(owner, 2) * 3 + part

    def greet(self):
        barrier = pltpu.get_barrier_semaphore()

        def signal(dest):
            pl.semaphore_signal(
                barrier,
                inc=1,
                device_id={"pix": self.peers[dest]},
                device_id_type=pl.DeviceIdType.MESH,
            )

        signal(self.ACROSS)
        signal(self.BESIDE)
        pl.when(self.has_up)(lambda: signal(self.UP))
        pl.when(self.has_down)(lambda: signal(self.DOWN))
        neighbours = jnp.minimum(self.z, 1) + jnp.minimum(self.layers - 1 - self.z, 1)
        pl.semaphore_wait(barrier, 2 + neighbours)

    def moves(self):
        out = []
        for part in (2, 0, 1):
            out += [
                (None, self.me, part, self.ACROSS),
                (self.has_up, self.me, part, self.UP),
                (self.has_down, self.me, part, self.DOWN),
                (None, self.me, part, self.BESIDE),
            ]
        return out

    def begin(self, copies):
        for condition, owner, part, dest in copies:
            if condition is None:
                self.copy(owner, part, dest).start()
            else:
                pl.when(condition)(lambda o=owner, p=part, d=dest: self.copy(o, p, d).start())

    def finish(self, copies):
        for condition, owner, part, dest in copies:
            if condition is None:
                self.copy(owner, part, dest).wait_send()
            else:
                pl.when(condition)(lambda o=owner, p=part, d=dest: self.copy(o, p, d).wait_send())

    def arrived(self, owner, part):
        self.copy(owner, part, self.BESIDE).wait_recv()

    def events(self):
        up, down = (self.has_up, self.UP), (self.has_down, self.DOWN)
        across, beside = (None, self.ACROSS), (None, self.BESIDE)
        out = [[(None, self.across, 2, [up, down, beside])]]

        def along(step, part, side):
            start = self.me if side == 0 else self.across
            extra = [across] if part < 2 else []
            below = (self.z >= step, start - 4 * step, part, [up] + extra + [beside])
            above = (
                self.z + step < self.layers,
                start + 4 * step,
                part,
                [down] + extra + [beside],
            )
            return [below, above]

        def over(step, part):
            if step == 0:
                return [(None, self.across, part, [beside])]
            return [
                (self.z >= step, self.across - 4 * step, part, [beside]),
                (self.z + step < self.layers, self.across + 4 * step, part, [beside]),
            ]

        for step in range(1, self.layers):
            out.append(along(step, 0, 0) + along(step, 2, 0) + over(step - 1, 0))
            out.append(along(step, 1, 0) + along(step, 2, 1) + over(step - 1, 1))
        out.append(over(self.layers - 1, 0))
        out.append(over(self.layers - 1, 1))
        return out

    def handle(self, events):
        for condition, owner, part, dests in events:

            def act(owner=owner, part=part, dests=dests):
                self.arrived(owner, part)
                self.begin([(c, owner, part, d) for c, d in dests])

            if condition is None:
                act()
            else:
                pl.when(condition)(act)

    def close(self):
        self.finish(self.moves())
        for events in self.events():
            for condition, owner, part, dests in events:

                def act(owner=owner, part=part, dests=dests):
                    self.finish([(c, owner, part, d) for c, d in dests])

                if condition is None:
                    act()
                else:
                    pl.when(condition)(act)

    def await_beside(self, owner):
        for part in range(3):
            self.arrived(owner, part)


TURN = 2
FINISH = 3
AHEAD = 4
EARLY = (1, 2, 3, 5, 7)
GROWTH = 6.0


class Scatter:
    def __init__(self, gather, work, inbox, send_sem, recv_sem):
        self.gather = gather
        self.work, self.inbox = work, inbox
        self.send_sem, self.recv_sem = send_sem, recv_sem
        rank = work.shape[1]
        last = max(rank // 8 // 16 * 16, 16)
        first = (rank - last + 31) // 32 * 16
        self.cuts = [(0, first), (first, rank - last - first), (rank - last, last), (0, rank)]
        self.sent = []

    def copy(self, owner, part, dest):
        start, rows = self.cuts[part]
        slot = lax.div(owner, 2)
        place = part % 3
        chips = self.gather.size // 2
        down = self.gather.DOWN
        sent = taken = slot * 3 + place
        if dest == down:
            taken = 3 * chips + taken
        if dest == self.gather.ACROSS:
            layer = lax.div(owner, 4) * 3 + place
            sent, taken = 3 * chips + layer, 6 * chips + layer
        if dest == self.gather.BESIDE:
            after = 3 * self.gather.layers + slot
            sent, taken = 3 * chips + after, 6 * chips + after
        return remote(
            self.work.at[owner, pl.ds(start, rows)],
            self.inbox.at[dest, slot, pl.ds(start, rows)],
            self.send_sem.at[sent],
            self.recv_sem.at[taken],
            self.gather.peers[dest],
        )

    def send(self, owner, part, dest, conditions):
        self.copy(owner, part, dest).start()
        self.sent.append((conditions, owner, part, dest))

    def take(self, owner, part, dest):
        start, rows = self.cuts[part]
        self.copy(owner, part, dest).wait_recv()
        piece = self.work.at[owner, pl.ds(start, rows)]
        got = self.inbox[dest, lax.div(owner, 2), pl.ds(start, rows)]
        piece[...] = (piece[...].astype(F32) + got.astype(F32)).astype(BF16)

    def close(self):
        for conditions, owner, part, dest in self.sent:
            wait = lambda o=owner, p=part, d=dest: self.copy(o, p, d).wait_send()
            for condition in conditions:
                wait = lambda c=condition, w=wait: pl.when(c)(w)
            wait()


def splat(values, row, col):
    return jnp.broadcast_to(values[row : row + 1, col : col + 1], values.shape)


def factor_step(block, left_ref, right_ref, inverse_ref):
    size = left_ref.shape[0]
    top, side = left_ref[0:8, :], right_ref[0:8, :]
    cell = {(r, c): splat(top, r, c) for r in range(8) for c in range(r + 1)}
    turn = {}
    for c in range(8):
        pivot = cell[c, c]
        guess = lax.rsqrt(pivot)
        scale = guess * (1.5 - 0.5 * pivot * guess * guess)
        turn[c, c] = scale
        for r in range(c + 1, 8):
            cell[r, c] = cell[r, c] * scale
        for r in range(c + 1, 8):
            for k in range(c + 1, r + 1):
                cell[r, k] = cell[r, k] - cell[r, c] * cell[k, c]
    for c in range(8):
        for r in range(c + 1, 8):
            total = cell[r, c] * turn[c, c]
            for k in range(c + 1, r):
                total = total + cell[r, k] * turn[k, c]
            turn[r, c] = -total * turn[r, r]
    row = lax.broadcasted_iota(jnp.int32, top.shape, 0)
    lane = lax.broadcasted_iota(jnp.int32, top.shape, 1)
    upper, lower = jnp.zeros_like(top), jnp.zeros_like(side)
    for c in range(8):
        weight = jnp.zeros_like(top)
        for r in range(c, 8):
            weight = jnp.where(row == r, turn[r, c], weight)
        upper = upper + weight * top[c : c + 1, :]
        lower = lower + weight * side[c : c + 1, :]
    inverse_ref[pl.ds(pl.multiple_of(8 * block, 8), 8), :] = lower
    upper = jnp.where((lane >= row) & (lane < size - 8 * block), upper, 0.0)
    both = jnp.concatenate([upper, lower], axis=1)
    change = lax.dot_general(
        upper, both, (((0,), (0,)), ((), ())), precision=HIGHEST, preferred_element_type=F32
    )
    left = pltpu.roll(left_ref[...] - change[:, :size], size - 8, 1)
    left_ref[0 : size - 8, :] = left[8:]
    left_ref[size - 8 : size, :] = jnp.zeros_like(top)
    right = right_ref[...] - change[:, size:]
    right_ref[0 : size - 8, :] = right[8:]
    right_ref[size - 8 : size, :] = jnp.zeros_like(side)


class GramSum:
    def __init__(self, me, size, gram_ref, parts, arrived, send_sem, recv_sem):
        self.me, self.size, self.gram_ref = me, size, gram_ref
        self.parts, self.arrived = parts, arrived
        self.send_sem, self.recv_sem = send_sem, recv_sem
        self.direct = direct_sum(parts.shape[0] * parts.shape[1], size)

    def scatter(self, d):
        peer = partner_of(self.me, d)
        return remote(
            self.parts.at[peer],
            self.arrived.at[d],
            self.send_sem.at[d],
            self.recv_sem.at[d],
            peer,
        )

    def gather(self, d):
        height = self.parts.shape[1]
        own = pl.ds(pl.multiple_of(self.me * height, height), height)
        return remote(
            self.arrived.at[0],
            self.gram_ref.at[own],
            self.send_sem.at[self.size + d],
            self.recv_sem.at[self.size + d],
            partner_of(self.me, d),
        )

    def start(self):
        if self.direct:
            for d in range(1, self.size):
                self.scatter(d).start()

    def turn(self):
        if not self.direct:
            sum_gram(
                self.me,
                self.size,
                self.gram_ref,
                self.parts,
                self.arrived,
                self.send_sem,
                self.recv_sem,
            )
            return
        total = self.parts[self.me]
        for d in range(1, self.size):
            self.scatter(d).wait_recv()
            total = total + self.arrived[d]
        self.arrived[0] = total
        for d in range(1, self.size):
            self.gather(d).start()
        height = self.parts.shape[1]
        self.gram_ref[pl.ds(pl.multiple_of(self.me * height, height), height), :] = total

    def finish(self):
        if self.direct:
            for d in range(1, self.size):
                self.gather(d).wait_recv()

    def close(self):
        if self.direct:
            for d in range(1, self.size):
                self.scatter(d).wait_send()
                self.gather(d).wait_send()


def build_filters(defocus_ref, waves, filters):
    number, length, _ = filters.shape
    half = length // 2
    index = lax.broadcasted_iota(jnp.int32, (1, length), 1)
    freq = jnp.where(index <= half, index, index - half).astype(F32) / length
    square = freq * freq

    def phase(group, _):
        waves[0, pl.ds(group, 1), :] = (math.pi * defocus_ref[group]) * square

    lax.fori_loop(0, number, phase, None, unroll=8)
    phases = waves[0, 0:number, :]
    sine, cosine = jnp.sin(phases), jnp.cos(phases)
    waves[0, 0:number, :] = sine
    waves[1, 0:number, :] = cosine
    keep = math.sqrt(1.0 - AMPLITUDE**2)
    rest = jnp.zeros((length - number, length), F32)
    first = jnp.concatenate([-keep * sine - AMPLITUDE * cosine, rest], axis=0).T
    second = jnp.concatenate([AMPLITUDE * sine - keep * cosine, rest], axis=0).T

    def eight(block, both):
        left, right = both
        for i in range(8):
            group = 8 * block + i
            contrast = (
                left[:, i : i + 1] * waves[1, pl.ds(group, 1), :]
                + right[:, i : i + 1] * waves[0, pl.ds(group, 1), :]
            )
            power = contrast * contrast + WIENER
            over = pl.reciprocal(power, approx=True)
            wiener = contrast * (over * (2.0 - power * over))
            filters[group] = jnp.concatenate([wiener, wiener[8:half]], axis=0).astype(BF16)
        return pltpu.roll(left, length - 8, 1), pltpu.roll(right, length - 8, 1)

    lax.fori_loop(0, number // 8, eight, (first[: half + 8], second[: half + 8]))


def whole_kernel(
    size,
    count,
    stride,
    group_ref,
    live_ref,
    defocus_ref,
    image_hbm,
    matrix_hbm,
    tables_hbm,
    basis_ref,
    out_ref,
    growth_ref,
    tables,
    waves,
    filters,
    images_ref,
    turned,
    columns,
    held,
    sketch_ref,
    gram_ref,
    parts,
    arrived,
    left_ref,
    right_ref,
    inverse_ref,
    work,
    inbox,
    load_sem,
    own_sem,
    send_sem,
    recv_sem,
    sum_send_sem,
    sum_recv_sem,
    back_send_sem,
    back_recv_sem,
):
    me = lax.axis_index("pix")
    step = pl.program_id(0)
    length, slots, _ = columns.shape
    rank = sketch_ref.shape[1]
    steps = slots // count
    pairs = count // 2
    base = step * count
    gather = Gather(me, size, held, matrix_hbm, send_sem, recv_sem)
    events = gather.events()

    def load(i):
        rows = pl.ds(i * count, count)
        return pltpu.make_async_copy(image_hbm.at[rows], images_ref.at[rows], load_sem.at[i])

    @pl.when(step == 0)
    def _():
        gather.greet()
        gather.begin(gather.moves())
        small = [
            pltpu.make_async_copy(tables_hbm, tables, own_sem.at[0]),
            pltpu.make_async_copy(matrix_hbm, held.at[me], own_sem.at[1]),
        ]
        for copy in small:
            copy.start()
        for i in range(min(AHEAD, steps)):
            load(i).start()
        build_filters(defocus_ref, waves, filters)
        for copy in small:
            copy.wait()

    @pl.when((step >= 1) & (step + AHEAD - 1 < steps))
    def _():
        load(step + AHEAD - 1).start()

    early = [place for place in EARLY if place < steps][: len(events)]
    for i, place in enumerate(early):

        @pl.when(step == place)
        def _(i=i):
            gather.handle(events[i])

    load(step).wait()

    def side_by_side(values):
        return jnp.concatenate(values, axis=1)

    def product(left, right):
        return jnp.dot(left, right, preferred_element_type=F32)

    def quads(left, right):
        width = 2 * length
        return jnp.concatenate(
            [product(left, right[i : i + width]) for i in range(0, pairs * length, width)], axis=0
        )

    images = jnp.concatenate(
        [
            side_by_side([images_ref[base + 2 * i], images_ref[base + 2 * i + 1]])
            for i in range(pairs)
        ],
        axis=0,
    )
    weights = jnp.concatenate(
        [
            side_by_side(
                [filters[group_ref[base + 2 * i]], filters[group_ref[base + 2 * i + 1]]]
            )
            for i in range(pairs)
        ],
        axis=0,
    )
    rows = product(images, tables[0]).astype(BF16)
    spectrum = quads(tables[1], rows)
    kept = (spectrum * weights.astype(F32)).astype(BF16)
    back = product(kept, tables[2]).astype(BF16)
    result = quads(tables[3], back)
    for i in range(count):
        tall, wide = i // 2 * length, i % 2 * length
        turned[pl.ds(i, length, stride=stride), :] = result[
            tall : tall + length, wide : wide + length
        ]
    slot = base + lax.broadcasted_iota(jnp.int32, (1, count, 1), 1)
    values = turned[...].reshape(length, stride, length)[:, :count]
    columns[:, pl.ds(pl.multiple_of(base, count), count), :] = jnp.where(
        slot < live_ref[0], values, 0.0
    ).astype(BF16)

    @pl.when(step == steps - 1)
    def _():
        lines = length // size
        layers = gather.layers
        z = gather.z

        def pixels(owner):
            return side_by_side([columns[owner * lines + line] for line in range(lines)])

        def nearest(k):
            room = jnp.minimum(z, layers - 1 - z)
            near = jnp.where(lax.rem(k, 2) == 1, z + lax.div(k + 1, 2), z - lax.div(k + 1, 2))
            far = jnp.where(z < layers - 1 - z, k, layers - 1 - k)
            return jnp.where(k <= 2 * room, near, far)

        waiting = list(range(len(early), len(events)))
        late = {}
        for chip in range(2 * layers):
            ready = min(chip // 2 * 2 + chip % 2 * 2, len(events) - 1)
            late[chip] = [k for k in waiting if k <= ready or chip == 2 * layers - 1]
            waiting = [k for k in waiting if k not in late[chip]]

        def one_chip(chip, _):
            for place, group in late.items():
                if group:

                    @pl.when(chip == place)
                    def _(group=group):
                        for k in group:
                            gather.handle(events[k])

            column = lax.rem(lax.div(me, 2) + chip, 2)
            both = nearest(lax.div(chip, 2)) * 4 + column * 2
            other = both + 1 - lax.rem(me, 2)
            gather.await_beside(other)
            left = side_by_side([columns[both * lines + line] for line in range(2 * lines)])
            right = held[pl.ds(both, 2)]
            sketch_ref[...] += product(left, right.reshape(-1, rank))

        sketch_ref[...] = jnp.zeros_like(sketch_ref)
        lax.fori_loop(0, 2 * layers, one_chip, None)
        sketch = sketch_ref[...]
        sketch_t = sketch.T.astype(BF16)
        scatter = Scatter(gather, work, inbox, back_send_sem, back_recv_sem)
        total = GramSum(me, size, gram_ref, parts, arrived, sum_send_sem, sum_recv_sem)
        up, down, across, beside = gather.UP, gather.DOWN, gather.ACROSS, gather.BESIDE

        def ways(distance):
            out = []
            for upwards in (False, True) if distance else (True,):
                own = me + (4 * distance if upwards else -4 * distance)
                other = partner_of(own, 2)
                there = z + distance < layers if upwards else z >= distance
                given = [there] if distance else []
                out.append((given, upwards, own, other, partner_of(own, 1), partner_of(other, 1)))
            return out

        def run(given, act):
            pl.when(given[0])(act) if given else act()

        def compute(distance):
            for given, upwards, own, other, own_beside, other_beside in ways(distance):

                def act():
                    for owner, aside in ((other, other_beside), (own, own_beside)):
                        work[aside] = product(sketch_t, pixels(aside)).astype(BF16)
                        scatter.send(aside, 3, beside, given)
                        work[owner] = product(sketch_t, pixels(owner)).astype(BF16)

                run(given, act)

        def onward(owner, part, upwards, given):
            way, ahead = (up, gather.has_down) if upwards else (down, gather.has_up)
            pl.when(ahead)(lambda: scatter.take(owner, part, way))
            scatter.send(owner, part, way, given)

        def chip_sum(distance):
            for given, upwards, own, other, _, _ in ways(distance):

                def act():
                    scatter.take(other, 3, beside)
                    for part in range(2):
                        scatter.send(other, part, across, given)

                run(given, act)

        def own_sum(distance):
            for given, upwards, own, _, _, _ in ways(distance):
                run(given, lambda own=own: scatter.take(own, 3, beside))

        def third(distance):
            for given, upwards, own, other, _, _ in ways(distance):

                def act():
                    onward(other, 2, upwards, given)
                    onward(own, 2, upwards, given)

                run(given, act)

        def along(distance, part):
            for given, upwards, own, _, _, _ in ways(distance):

                def act():
                    scatter.take(own, part, across)
                    if distance:
                        onward(own, part, upwards, given)

                run(given, act)

        def last(owner, part):
            pl.when(gather.has_down)(lambda: scatter.take(owner, part, up))
            pl.when(gather.has_up)(lambda: scatter.take(owner, part, down))

        compute(layers - 1)
        gram = lax.dot_general(
            sketch, sketch, (((0,), (0,)), ((), ())), precision=HIGHEST, preferred_element_type=F32
        )
        parts[...] = gram.reshape(parts.shape)
        total.start()
        for distance in range(layers - 1, -1, -1):
            chip_sum(distance)
            own_sum(distance)
            if distance == layers - 1 and distance:
                third(distance)
            if distance:
                compute(distance - 1)
            if distance == max(layers - TURN, 0):
                total.turn()
        for distance in range(layers - 2, 0, -1):
            third(distance)
        todo = [(distance, part) for distance in range(layers - 1, 0, -1) for part in range(2)]
        for place in todo[:FINISH]:
            along(*place)
        total.finish()
        unit = lax.broadcasted_iota(jnp.int32, (rank, rank), 0) == lax.broadcasted_iota(
            jnp.int32, (rank, rank), 1
        )
        left_ref[...] = gram_ref[...]
        right_ref[...] = jnp.where(unit, 1.0, 0.0)
        blocks = rank // 8
        todo = todo[FINISH:]
        for i in range(len(todo) + 1):
            lax.fori_loop(
                blocks * i // (len(todo) + 1),
                blocks * (i + 1) // (len(todo) + 1),
                lambda block, _: factor_step(block, left_ref, right_ref, inverse_ref),
                None,
            )
            if i < len(todo):
                along(*todo[i])
        inverse = inverse_ref[...]
        basis_ref[...] = lax.dot_general(
            sketch,
            inverse,
            (((1,), (1,)), ((), ())),
            precision=HIGHEST,
            preferred_element_type=F32,
        ).astype(BF16)
        scale = jnp.sqrt(jnp.sum(inverse * inverse, axis=0, keepdims=True))
        sums = jnp.dot(
            jnp.broadcast_to(scale, (8, rank)),
            jnp.abs(gram_ref[...]),
            precision=HIGHEST,
            preferred_element_type=F32,
        )
        growth_ref[0] = jnp.where(jnp.max(sums * scale) <= GROWTH, 1, 0)
        last(gather.across, 2)
        scatter.send(gather.across, 2, across, [])
        last(me, 2)
        for part in range(2):
            along(0, part)
            last(me, part)
        scatter.take(me, 2, across)
        mine = jnp.dot(
            inverse, work[me].astype(F32), precision=HIGHEST, preferred_element_type=F32
        )
        out_ref[...] = mine.T
        gather.close()
        scatter.close()
        total.close()


def make_whole(images, groups, live, defocus_values, matrix, size):
    slots, length, _ = images.shape
    height, rank = matrix.shape
    count = math.gcd(slots, 32)
    stride = count + 4
    tables = pair_tables(length)
    number = defocus_values.shape[0]
    if direct_sum(rank, size):
        summing = [pltpu.VMEM((size, rank // size, rank), F32)] * 2
        signals = 2 * size
    else:
        summing = [
            pltpu.VMEM((1, rank, rank), F32),
            pltpu.VMEM((bits_of(size), rank, rank), F32),
        ]
        signals = bits_of(size)

    def whole(*shape):
        return pl.BlockSpec(shape, lambda i, *_: (0,) * len(shape))

    square = pltpu.VMEM((rank, rank), F32)
    return pl.pallas_call(
        functools.partial(whole_kernel, size, count, stride),
        out_shape=(
            jax.ShapeDtypeStruct((slots, rank), BF16),
            jax.ShapeDtypeStruct((height, rank), F32),
            jax.ShapeDtypeStruct((1,), jnp.int32),
        ),
        grid_spec=pltpu.PrefetchScalarGridSpec(
            num_scalar_prefetch=3,
            grid=(slots // count,),
            in_specs=[
                *[pl.BlockSpec(memory_space=pl.ANY)] * 3,
            ],
            out_specs=(
                whole(slots, rank),
                whole(height, rank),
                pl.BlockSpec(memory_space=pltpu.SMEM),
            ),
            scratch_shapes=[
                pltpu.VMEM((4, 2 * length, 2 * length), BF16),
                pltpu.VMEM((2, number, length), F32),
                pltpu.VMEM((number, length, length), BF16),
                pltpu.VMEM((slots, length, length), BF16),
                pltpu.VMEM((length * stride, length), F32),
                pltpu.VMEM((length, slots, length), BF16),
                pltpu.VMEM((size, height, rank), BF16),
                pltpu.VMEM((slots, rank), F32),
                square,
                *summing,
                square,
                square,
                square,
                pltpu.VMEM((size, rank, height), BF16),
                pltpu.VMEM((4, size // 2, rank, height), BF16),
                pltpu.SemaphoreType.DMA((slots // count,)),
                pltpu.SemaphoreType.DMA((2,)),
                pltpu.SemaphoreType.DMA((9 * size // 2 + 3 * (size // 4),)),
                pltpu.SemaphoreType.DMA((size, 3)),
                pltpu.SemaphoreType.DMA((signals,)),
                pltpu.SemaphoreType.DMA((signals,)),
                pltpu.SemaphoreType.DMA((4 * size // 2 + 3 * (size // 4),)),
                pltpu.SemaphoreType.DMA((7 * size // 2 + 3 * (size // 4),)),
            ],
        ),
        compiler_params=pltpu.CompilerParams(
            collective_id=0, has_side_effects=True, vmem_limit_bytes=56 << 20
        ),
        name="whole",
    )(groups, live, defocus_values, images, matrix, tables)


def sketch_kernel(
    size,
    group_ref,
    live_ref,
    image_ref,
    matrix_ref,
    filters,
    pair_ref,
    pair_t_ref,
    table_ref,
    table_t_ref,
    out_ref,
    sketch_ref,
    gram_ref,
    turned,
    held,
    summed,
    parts,
    arrived,
    send_sem,
    recv_sem,
    sum_send_sem,
    sum_recv_sem,
):
    me = lax.axis_index("pix")
    step = pl.program_id(0)
    steps = out_ref.shape[1] // image_ref.shape[0]
    count, length, _ = image_ref.shape
    pairs = count // 2
    base = step * count
    orders = gathering_orders(size)
    stages = bits_of(size)
    height = matrix_ref.shape[0] // 2

    def copy_of(half, stage, mask):
        bit = orders[half][stage]
        slot = (bit | mask) - 1
        return remote(
            held.at[half, mask],
            held.at[half, bit | mask],
            send_sem.at[half, slot],
            recv_sem.at[half, slot],
            partner_of(me, bit),
        )

    def receive(stage, half, mask):
        copy_of(half, stage, mask).wait_recv()
        for later in range(stage + 1, stages):
            copy_of(half, later, orders[half][stage] | mask).start()

    @pl.when(step == 0)
    def _():
        greet(me, peers(gram_ref.shape[0], size))
        for half in range(2):
            held[half, 0] = matrix_ref[half * height : (half + 1) * height, :]
        for stage in range(stages):
            for half in range(2):
                copy_of(half, stage, 0).start()

    early = min(2, stages)
    for stage in range(early):

        @pl.when(step == steps * (5 + 6 * stage) // 16)
        def _(stage=stage):
            for place in range(1 << stage):
                for half in range(2):
                    receive(stage, half, sums(orders[half][:stage])[place])

    def side_by_side(values):
        return jnp.concatenate(values, axis=1)

    def stacked(wide):
        return jnp.concatenate(
            [wide[:, 2 * length * i : 2 * length * (i + 1)] for i in range(pairs)], axis=0
        )

    def unstacked(tall):
        return side_by_side([tall[length * i : length * (i + 1)] for i in range(pairs)])

    images = jnp.concatenate(
        [side_by_side([image_ref[2 * i], image_ref[2 * i + 1]]) for i in range(pairs)], axis=0
    )
    rows = jnp.dot(images, pair_ref[...], preferred_element_type=F32).astype(BF16)
    spectrum = jnp.dot(table_t_ref[...], unstacked(rows), preferred_element_type=F32)
    weights = side_by_side([filters[group_ref[base + i]] for i in range(count)])
    kept = (spectrum * weights.astype(F32)).astype(BF16)
    back = jnp.dot(stacked(kept), pair_t_ref[...], preferred_element_type=F32).astype(BF16)
    result = jnp.dot(table_ref[...], unstacked(back), preferred_element_type=F32)
    for i in range(count):
        turned[pl.ds(i, length, stride=count), :] = result[:, i * length : (i + 1) * length]
    slot = base + lax.broadcasted_iota(jnp.int32, (1, count, 1), 1)
    values = turned[...].reshape(length, count, length)
    out_ref[:, pl.ds(pl.multiple_of(base, count), count), :] = jnp.where(
        slot < live_ref[0], values, 0.0
    ).astype(BF16)

    @pl.when(step == steps - 1)
    def _():
        lines = length // size
        part = lines // 2

        def term(half, mask):
            start = partner_of(me, mask) * lines + half * part
            left = side_by_side([out_ref[start + line] for line in range(part)])
            return jnp.dot(left, held[half, mask], preferred_element_type=F32)

        sketch_ref[...] = jnp.zeros_like(sketch_ref)
        for half in range(2):
            for mask in sums(orders[half][:early]):
                sketch_ref[...] += term(half, mask)
        for stage in range(early, stages):
            for place in range(1 << stage):
                for half in range(2):
                    mask = sums(orders[half][:stage])[place]
                    receive(stage, half, mask)
                    sketch_ref[...] += term(half, orders[half][stage] | mask)
        sketch = sketch_ref[...]
        gram = lax.dot_general(
            sketch, sketch, (((0,), (0,)), ((), ())), precision=HIGHEST, preferred_element_type=F32
        )
        parts[...] = gram.reshape(parts.shape)
        sum_gram(me, size, summed, parts, arrived, sum_send_sem, sum_recv_sem)
        gram_ref[...] = summed[...]
        for half in range(2):
            for stage in range(stages):
                for mask in sums(orders[half][:stage]):
                    copy_of(half, stage, mask).wait_send()


def make_sketch(images, groups, live, defocus_values, matrix, size):
    slots, length, _ = images.shape
    height, rank = matrix.shape
    count = math.gcd(slots, 16)
    table = real_tables(length)
    zero = jnp.zeros_like(table)
    pair = jnp.concatenate(
        [jnp.concatenate([table, zero], axis=1), jnp.concatenate([zero, table], axis=1)], axis=0
    )
    number = defocus_values.shape[0]
    if direct_sum(rank, size):
        summing = [
            pltpu.VMEM((size, rank // size, rank), F32),
            pltpu.VMEM((size, rank // size, rank), F32),
        ]
        signals = 2 * size
    else:
        summing = [
            pltpu.VMEM((1, rank, rank), F32),
            pltpu.VMEM((bits_of(size), rank, rank), F32),
        ]
        signals = bits_of(size)

    def whole(*shape):
        return pl.BlockSpec(shape, lambda i, *_: (0,) * len(shape))

    return pl.pallas_call(
        functools.partial(sketch_kernel, size),
        out_shape=(
            jax.ShapeDtypeStruct((length, slots, length), BF16),
            jax.ShapeDtypeStruct((slots, rank), F32),
            jax.ShapeDtypeStruct((rank, rank), F32),
        ),
        grid_spec=pltpu.PrefetchScalarGridSpec(
            num_scalar_prefetch=2,
            grid=(slots // count,),
            in_specs=[
                pl.BlockSpec((count, length, length), lambda i, *_: (i, 0, 0)),
                whole(height, rank),
                whole(number, length, length),
                whole(2 * length, 2 * length),
                whole(2 * length, 2 * length),
                whole(length, length),
                whole(length, length),
            ],
            out_specs=(whole(length, slots, length), whole(slots, rank), whole(rank, rank)),
            scratch_shapes=[
                pltpu.VMEM((length * count, length), F32),
                pltpu.VMEM((2, size, height // 2, rank), BF16),
                pltpu.VMEM((rank, rank), F32),
                *summing,
                pltpu.SemaphoreType.DMA((2, size - 1)),
                pltpu.SemaphoreType.DMA((2, size - 1)),
                pltpu.SemaphoreType.DMA((signals,)),
                pltpu.SemaphoreType.DMA((signals,)),
            ],
        ),
        compiler_params=pltpu.CompilerParams(
            collective_id=1, has_side_effects=True, vmem_limit_bytes=50 << 20
        ),
        name="sketch",
    )(
        groups,
        live,
        images,
        matrix,
        filter_table(defocus_values, length),
        pair,
        pair.T,
        table,
        table.T,
    )


def basis_kernel(factor_ref, sketch_ref, out_ref, turned_ref):
    rank = factor_ref.shape[0]
    row = lax.broadcasted_iota(jnp.int32, (rank, rank), 0)
    col = lax.broadcasted_iota(jnp.int32, (rank, rank), 1)
    factor = factor_ref[...]
    on_diagonal = jnp.where(row == col, factor, 0.0)
    lower = jnp.where(row > col, factor, 0.0) / jnp.sum(on_diagonal, axis=1, keepdims=True)

    def times(left, right):
        return jnp.dot(left, right, precision=HIGHEST, preferred_element_type=F32)

    def same_block(shift):
        return lax.shift_right_logical(row, shift) == lax.shift_right_logical(col, shift)

    shift = 3
    within = jnp.where(same_block(shift), lower, 0.0)
    unit = jnp.where(row == col, 1.0, 0.0).astype(F32)
    square = times(within, within)
    fourth = times(square, square)
    inverse = times(times(unit - within, unit + square), unit + fourth)
    while 1 << shift < rank:
        off = jnp.where(same_block(shift + 1) & ~same_block(shift), lower, 0.0)
        inverse = inverse - times(inverse, times(off, inverse))
        shift += 1
    inverse = inverse / jnp.sum(on_diagonal, axis=0, keepdims=True)
    basis = lax.dot_general(
        sketch_ref[...],
        inverse,
        (((1,), (1,)), ((), ())),
        precision=HIGHEST,
        preferred_element_type=F32,
    )
    out_ref[...] = basis.astype(BF16)
    turned_ref[...] = basis.T.astype(BF16)


def make_basis(factor_low, sketch):
    slots, rank = sketch.shape
    return pl.pallas_call(
        basis_kernel,
        out_shape=(
            jax.ShapeDtypeStruct((slots, rank), BF16),
            jax.ShapeDtypeStruct((rank, slots), BF16),
        ),
        name="basis",
    )(factor_low, sketch)


def project_kernel(size, basis_ref, column_ref, out_ref, held, arrived, send_sem, recv_sem):
    me = lax.axis_index("pix")
    length = column_ref.shape[0]
    rows = length // size
    part = rows // 2
    orders = halving_orders(size)
    slots = {}
    for half in range(2):
        for stage in range(len(orders[half])):
            for mask in masks_of(orders[half][stage + 1 :]):
                slots[half, stage, mask] = len(slots) % (size - 1)

    def copy_of(half, stage, mask):
        bit = orders[half][stage]
        slot = slots[half, stage, mask]
        return remote(
            held.at[half, bit | mask],
            arrived.at[half, slot],
            send_sem.at[half, slot],
            recv_sem.at[half, slot],
            partner_of(me, bit),
        )

    greet(me, [1 << shift for shift in range(bits_of(size))])
    first = orders[0][0]

    def compute(half, mask):
        start = partner_of(me, mask) * rows + half * part
        right = jnp.concatenate([column_ref[start + row] for row in range(part)], axis=1)
        held[half, mask] = jnp.dot(
            basis_ref[...], right, preferred_element_type=F32
        ).astype(BF16)

    def add(half, stage, mask):
        later = orders[half][stage + 1 :]
        copy_of(half, stage, mask).wait_recv()
        total = (
            held[half, mask].astype(F32)
            + arrived[half, slots[half, stage, mask]].astype(F32)
        )
        if later:
            held[half, mask] = total.astype(BF16)
            if mask & later[0]:
                copy_of(half, stage + 1, mask - later[0]).start()
        else:
            height = out_ref.shape[0] // 2
            out_ref[half * height : (half + 1) * height, :] = total.T

    kept = [masks_of(orders[half][1:]) for half in range(2)]
    for place in range(len(kept[0]) + 1):
        for half in range(2):
            if place < len(kept[0]):
                mask = kept[half][place]
                compute(half, first | mask)
                copy_of(half, 0, mask).start()
                compute(half, mask)
        for half in range(2):
            if place > 0:
                add(half, 0, kept[half][place - 1])
    for stage in range(1, bits_of(size)):
        for place in range(len(masks_of(orders[0][stage + 1 :]))):
            for half in range(2):
                add(half, stage, masks_of(orders[half][stage + 1 :])[place])
    for half in range(2):
        for stage in range(bits_of(size)):
            for mask in masks_of(orders[half][stage + 1 :]):
                copy_of(half, stage, mask).wait_send()


def project(columns, basis_t, size):
    length, slots, _ = columns.shape
    rank = basis_t.shape[0]
    width = length * length // size
    return pl.pallas_call(
        functools.partial(project_kernel, size),
        out_shape=jax.ShapeDtypeStruct((width, rank), F32),
        in_specs=[pl.BlockSpec(memory_space=pltpu.VMEM)] * 2,
        out_specs=pl.BlockSpec(memory_space=pltpu.VMEM),
        scratch_shapes=[
            pltpu.VMEM((2, size, rank, width // 2), BF16),
            pltpu.VMEM((2, size - 1, rank, width // 2), BF16),
            pltpu.SemaphoreType.DMA((2, size - 1)),
            pltpu.SemaphoreType.DMA((2, size - 1)),
        ],
        compiler_params=pltpu.CompilerParams(
            collective_id=2, has_side_effects=True, vmem_limit_bytes=48 << 20
        ),
        name="project",
    )(basis_t, columns)


def per_device(particle_images, defocus_group, live_counts, defocus_values, test_matrix):
    size = lax.axis_size("pix")
    arguments = (particle_images, defocus_group, live_counts, defocus_values, test_matrix, size)
    basis, projection, growth = make_whole(*arguments)

    def stepwise():
        columns, sketch, gram = make_sketch(*arguments)
        factor_low = jnp.linalg.cholesky(gram)
        range_basis, basis_t = make_basis(factor_low, sketch)
        return (range_basis, project(columns, basis_t, size))

    return lax.cond(growth[0] != 0, lambda: (basis, projection), stepwise)


def solution(mesh):
    placed = (
        P(("grp", "pix"), None, None),
        P(("grp", "pix")),
        P(("grp", "pix")),
        P("grp"),
        P(("grp", "pix"), None),
    )
    return jax.shard_map(
        per_device,
        mesh=mesh,
        in_specs=placed,
        out_specs=(P(("grp", "pix"), None), P(("grp", "pix"), None)),
        check_vma=False,
    )
```

```python
import functools
import math

import jax
import jax.numpy as jnp
import ml_dtypes
import numpy as np
from jax import lax
from jax.experimental import pallas as pl
from jax.experimental.pallas import tpu as pltpu
from jax.sharding import PartitionSpec as P

AMPLITUDE = 0.1
WIENER = 0.1
F32 = jnp.float32
BF16 = jnp.bfloat16
HIGHEST = lax.Precision.HIGHEST


def real_tables(length):
    rows = np.arange(length)
    angles = 2.0 * math.pi / length * (rows[:, None] * rows[None, :] % length)
    packed = np.where(rows[None, :] <= length // 2, np.cos(angles), np.sin(angles))
    return jnp.asarray(packed.astype(np.float32)).astype(BF16)


def pair_tables(length):
    rows, half = np.arange(length), length // 2
    freq = np.where(rows <= half, rows, rows - half)
    angles = 2.0 * math.pi / length * (rows[:, None] * freq[None, :] % length)
    packed = np.where(rows[None, :] <= half, np.cos(angles), np.sin(angles))
    packed = packed.astype(ml_dtypes.bfloat16).astype(np.float32)
    weighted = packed * np.where(rows % half == 0, 1.0, 2.0)[None, :] / length
    out = np.zeros((4, 2, length, 2, length), np.float32)
    for i, table in enumerate((packed, packed.T, weighted.T, weighted)):
        out[i, 0, :, 0] = out[i, 1, :, 1] = table
    return jnp.asarray(out.reshape(4, 2 * length, 2 * length).astype(ml_dtypes.bfloat16))


def filter_table(defocus_values, length):
    index = jnp.arange(length, dtype=jnp.int32)
    freq = jnp.where(index < length // 2, index, index - length).astype(F32) / length
    phase = jnp.pi * defocus_values[:, None] * (freq * freq)[None, :]
    sine, cosine = lax.optimization_barrier((jnp.sin(phase), jnp.cos(phase)))
    keep = math.sqrt(1.0 - AMPLITUDE**2)
    first = (keep * sine + AMPLITUDE * cosine)[:, :, None]
    second = (keep * cosine - AMPLITUDE * sine)[:, :, None]
    contrast = -(first * cosine[:, None, :] + second * sine[:, None, :])
    wiener = (contrast / (contrast * contrast + WIENER)).astype(BF16).astype(F32)
    twice = jnp.where((index == 0) | (index == length // 2), 1.0, 2.0).astype(F32)
    return (wiener * (twice[:, None] * twice[None, :] / float(length * length))).astype(BF16)


def bits_of(size):
    return size.bit_length() - 1


def partner_of(me, mask):
    for shift in range(mask.bit_length()):
        bit = 1 << shift
        if mask & bit:
            me = me + bit * (1 - 2 * lax.rem(lax.div(me, bit), 2))
    return me


def greet(me, masks):
    barrier = pltpu.get_barrier_semaphore()
    for mask in masks:
        pl.semaphore_signal(
            barrier,
            inc=1,
            device_id={"pix": partner_of(me, mask)},
            device_id_type=pl.DeviceIdType.MESH,
        )
    pl.semaphore_wait(barrier, len(masks))


def remote(src, dst, send_sem, recv_sem, peer):
    return pltpu.make_async_remote_copy(
        src_ref=src,
        dst_ref=dst,
        send_sem=send_sem,
        recv_sem=recv_sem,
        device_id={"pix": peer},
        device_id_type=pl.DeviceIdType.MESH,
    )


def halving_orders(size):
    bits = [1 << shift for shift in range(bits_of(size))]
    if len(bits) < 3:
        return (bits, bits)
    return (bits, bits[:1] + bits[2:] + bits[1:2])


def masks_of(bits):
    if not bits:
        return [0]
    rest = masks_of(bits[1:])
    return [bits[0] | mask for mask in rest] + rest


def gathering_orders(size):
    first, second = halving_orders(size)
    return (first[::-1], second[1:][::-1] + second[:1])


def sums(bits):
    out = [0]
    for bit in bits:
        out = out + [bit | mask for mask in out]
    return out


def direct_sum(rank, size):
    return rank % (8 * size) == 0


def peers(rank, size):
    if direct_sum(rank, size):
        return list(range(1, size))
    return [1 << shift for shift in range(bits_of(size))]


def sum_gram(me, size, gram_ref, parts, arrived, send_sem, recv_sem):
    if not direct_sum(parts.shape[0] * parts.shape[1], size):
        gram_ref[...] = parts[...].reshape(gram_ref.shape)
        for stage in range(bits_of(size)):
            copy = remote(
                gram_ref,
                arrived.at[stage],
                send_sem.at[stage],
                recv_sem.at[stage],
                partner_of(me, 1 << stage),
            )
            copy.start()
            copy.wait()
            gram_ref[...] += arrived[stage]
        return
    height = parts.shape[1]
    scatter = [
        remote(
            parts.at[partner_of(me, d)],
            arrived.at[d],
            send_sem.at[d],
            recv_sem.at[d],
            partner_of(me, d),
        )
        for d in range(1, size)
    ]
    for copy in scatter:
        copy.start()
    total = parts[me]
    for d, copy in enumerate(scatter, 1):
        copy.wait_recv()
        total = total + arrived[d]
    arrived[0] = total
    own = pl.ds(pl.multiple_of(me * height, height), height)
    gather = [
        remote(
            arrived.at[0],
            gram_ref.at[own],
            send_sem.at[size + d],
            recv_sem.at[size + d],
            partner_of(me, d),
        )
        for d in range(1, size)
    ]
    for copy in gather:
        copy.start()
    gram_ref[own, :] = total
    for copy in gather:
        copy.wait_recv()
    for copy in scatter + gather:
        copy.wait_send()


class Gather:
    UP, DOWN, ACROSS, BESIDE = range(4)

    def __init__(self, me, size, held, block, send_sem, recv_sem):
        self.me, self.size, self.held, self.block = me, size, held, block
        self.send_sem, self.recv_sem = send_sem, recv_sem
        self.layers = size // 4
        self.z = lax.div(me, 4)
        height = held.shape[1]
        first = height * 14 // 32 // 16 * 16
        self.cuts = [(0, first), (first, first), (2 * first, height - 2 * first)]
        self.has_up = self.z + 1 < self.layers
        self.has_down = self.z >= 1
        self.across = partner_of(me, 2)
        self.beside = partner_of(me, 1)
        self.peers = {
            self.UP: me + 4,
            self.DOWN: me - 4,
            self.ACROSS: self.across,
            self.BESIDE: self.beside,
        }

    def copy(self, owner, part, dest):
        start, rows = self.cuts[part]
        piece = self.held.at[owner, pl.ds(start, rows)]
        return remote(
            self.block.at[pl.ds(start, rows)] if owner is self.me else piece,
            piece,
            self.send_sem.at[self.signal(owner, part, dest)],
            self.recv_sem.at[owner, part],
            self.peers[dest],
        )

    def signal(self, owner, part, dest):
        chips = self.size // 2
        if dest == self.ACROSS:
            return 6 * chips + lax.div(owner, 4) * 3 + part
        first = {self.UP: 0, self.DOWN: 3 * chips, self.BESIDE: 6 * chips + 3 * self.layers}
        return first[dest] + lax.div(owner, 2) * 3 + part

    def greet(self):
        barrier = pltpu.get_barrier_semaphore()

        def signal(dest):
            pl.semaphore_signal(
                barrier,
                inc=1,
                device_id={"pix": self.peers[dest]},
                device_id_type=pl.DeviceIdType.MESH,
            )

        signal(self.ACROSS)
        signal(self.BESIDE)
        pl.when(self.has_up)(lambda: signal(self.UP))
        pl.when(self.has_down)(lambda: signal(self.DOWN))
        neighbours = jnp.minimum(self.z, 1) + jnp.minimum(self.layers - 1 - self.z, 1)
        pl.semaphore_wait(barrier, 2 + neighbours)

    def moves(self):
        out = []
        for part in (2, 0, 1):
            out += [
                (None, self.me, part, self.ACROSS),
                (self.has_up, self.me, part, self.UP),
                (self.has_down, self.me, part, self.DOWN),
                (None, self.me, part, self.BESIDE),
            ]
        return out

    def begin(self, copies):
        for condition, owner, part, dest in copies:
            if condition is None:
                self.copy(owner, part, dest).start()
            else:
                pl.when(condition)(lambda o=owner, p=part, d=dest: self.copy(o, p, d).start())

    def finish(self, copies):
        for condition, owner, part, dest in copies:
            if condition is None:
                self.copy(owner, part, dest).wait_send()
            else:
                pl.when(condition)(lambda o=owner, p=part, d=dest: self.copy(o, p, d).wait_send())

    def arrived(self, owner, part):
        self.copy(owner, part, self.BESIDE).wait_recv()

    def events(self):
        up, down = (self.has_up, self.UP), (self.has_down, self.DOWN)
        across, beside = (None, self.ACROSS), (None, self.BESIDE)
        out = [[(None, self.across, 2, [up, down, beside])]]

        def along(step, part, side):
            start = self.me if side == 0 else self.across
            extra = [across] if part < 2 else []
            below = (self.z >= step, start - 4 * step, part, [up] + extra + [beside])
            above = (
                self.z + step < self.layers,
                start + 4 * step,
                part,
                [down] + extra + [beside],
            )
            return [below, above]

        def over(step, part):
            if step == 0:
                return [(None, self.across, part, [beside])]
            return [
                (self.z >= step, self.across - 4 * step, part, [beside]),
                (self.z + step < self.layers, self.across + 4 * step, part, [beside]),
            ]

        for step in range(1, self.layers):
            out.append(along(step, 0, 0) + along(step, 2, 0) + over(step - 1, 0))
            out.append(along(step, 1, 0) + along(step, 2, 1) + over(step - 1, 1))
        out.append(over(self.layers - 1, 0))
        out.append(over(self.layers - 1, 1))
        return out

    def handle(self, events):
        for condition, owner, part, dests in events:

            def act(owner=owner, part=part, dests=dests):
                self.arrived(owner, part)
                self.begin([(c, owner, part, d) for c, d in dests])

            if condition is None:
                act()
            else:
                pl.when(condition)(act)

    def close(self):
        self.finish(self.moves())
        for events in self.events():
            for condition, owner, part, dests in events:

                def act(owner=owner, part=part, dests=dests):
                    self.finish([(c, owner, part, d) for c, d in dests])

                if condition is None:
                    act()
                else:
                    pl.when(condition)(act)

    def await_beside(self, owner):
        for part in range(3):
            self.arrived(owner, part)


TURN = 2
FINISH = 3
AHEAD = 4
EARLY = (1, 2, 3, 5, 7)
GROWTH = 6.0


class Scatter:
    def __init__(self, gather, work, inbox, send_sem, recv_sem):
        self.gather = gather
        self.work, self.inbox = work, inbox
        self.send_sem, self.recv_sem = send_sem, recv_sem
        rank = work.shape[1]
        last = max(rank // 8 // 16 * 16, 16)
        first = (rank - last + 31) // 32 * 16
        self.cuts = [(0, first), (first, rank - last - first), (rank - last, last), (0, rank)]
        self.sent = []

    def copy(self, owner, part, dest):
        start, rows = self.cuts[part]
        slot = lax.div(owner, 2)
        place = part % 3
        chips = self.gather.size // 2
        down = self.gather.DOWN
        sent = taken = slot * 3 + place
        if dest == down:
            taken = 3 * chips + taken
        if dest == self.gather.ACROSS:
            layer = lax.div(owner, 4) * 3 + place
            sent, taken = 3 * chips + layer, 6 * chips + layer
        if dest == self.gather.BESIDE:
            after = 3 * self.gather.layers + slot
            sent, taken = 3 * chips + after, 6 * chips + after
        return remote(
            self.work.at[owner, pl.ds(start, rows)],
            self.inbox.at[dest, slot, pl.ds(start, rows)],
            self.send_sem.at[sent],
            self.recv_sem.at[taken],
            self.gather.peers[dest],
        )

    def send(self, owner, part, dest, conditions):
        self.copy(owner, part, dest).start()
        self.sent.append((conditions, owner, part, dest))

    def take(self, owner, part, dest):
        start, rows = self.cuts[part]
        self.copy(owner, part, dest).wait_recv()
        piece = self.work.at[owner, pl.ds(start, rows)]
        got = self.inbox[dest, lax.div(owner, 2), pl.ds(start, rows)]
        piece[...] = (piece[...].astype(F32) + got.astype(F32)).astype(BF16)

    def close(self):
        for conditions, owner, part, dest in self.sent:
            wait = lambda o=owner, p=part, d=dest: self.copy(o, p, d).wait_send()
            for condition in conditions:
                wait = lambda c=condition, w=wait: pl.when(c)(w)
            wait()


def splat(values, row, col):
    return jnp.broadcast_to(values[row : row + 1, col : col + 1], values.shape)


def factor_step(block, left_ref, right_ref, inverse_ref):
    size = left_ref.shape[0]
    top, side = left_ref[0:8, :], right_ref[0:8, :]
    cell = {(r, c): splat(top, r, c) for r in range(8) for c in range(r + 1)}
    turn = {}
    for c in range(8):
        pivot = cell[c, c]
        guess = lax.rsqrt(pivot)
        scale = guess * (1.5 - 0.5 * pivot * guess * guess)
        turn[c, c] = scale
        for r in range(c + 1, 8):
            cell[r, c] = cell[r, c] * scale
        for r in range(c + 1, 8):
            for k in range(c + 1, r + 1):
                cell[r, k] = cell[r, k] - cell[r, c] * cell[k, c]
    for c in range(8):
        for r in range(c + 1, 8):
            total = cell[r, c] * turn[c, c]
            for k in range(c + 1, r):
                total = total + cell[r, k] * turn[k, c]
            turn[r, c] = -total * turn[r, r]
    row = lax.broadcasted_iota(jnp.int32, top.shape, 0)
    lane = lax.broadcasted_iota(jnp.int32, top.shape, 1)
    upper, lower = jnp.zeros_like(top), jnp.zeros_like(side)
    for c in range(8):
        weight = jnp.zeros_like(top)
        for r in range(c, 8):
            weight = jnp.where(row == r, turn[r, c], weight)
        upper = upper + weight * top[c : c + 1, :]
        lower = lower + weight * side[c : c + 1, :]
    inverse_ref[pl.ds(pl.multiple_of(8 * block, 8), 8), :] = lower
    upper = jnp.where((lane >= row) & (lane < size - 8 * block), upper, 0.0)
    both = jnp.concatenate([upper, lower], axis=1)
    change = lax.dot_general(
        upper, both, (((0,), (0,)), ((), ())), precision=HIGHEST, preferred_element_type=F32
    )
    left = pltpu.roll(left_ref[...] - change[:, :size], size - 8, 1)
    left_ref[0 : size - 8, :] = left[8:]
    left_ref[size - 8 : size, :] = jnp.zeros_like(top)
    right = right_ref[...] - change[:, size:]
    right_ref[0 : size - 8, :] = right[8:]
    right_ref[size - 8 : size, :] = jnp.zeros_like(side)


class GramSum:
    def __init__(self, me, size, gram_ref, parts, arrived, send_sem, recv_sem):
        self.me, self.size, self.gram_ref = me, size, gram_ref
        self.parts, self.arrived = parts, arrived
        self.send_sem, self.recv_sem = send_sem, recv_sem
        self.direct = direct_sum(parts.shape[0] * parts.shape[1], size)

    def scatter(self, d):
        peer = partner_of(self.me, d)
        return remote(
            self.parts.at[peer],
            self.arrived.at[d],
            self.send_sem.at[d],
            self.recv_sem.at[d],
            peer,
        )

    def gather(self, d):
        height = self.parts.shape[1]
        own = pl.ds(pl.multiple_of(self.me * height, height), height)
        return remote(
            self.arrived.at[0],
            self.gram_ref.at[own],
            self.send_sem.at[self.size + d],
            self.recv_sem.at[self.size + d],
            partner_of(self.me, d),
        )

    def start(self):
        if self.direct:
            for d in range(1, self.size):
                self.scatter(d).start()

    def turn(self):
        if not self.direct:
            sum_gram(
                self.me,
                self.size,
                self.gram_ref,
                self.parts,
                self.arrived,
                self.send_sem,
                self.recv_sem,
            )
            return
        total = self.parts[self.me]
        for d in range(1, self.size):
            self.scatter(d).wait_recv()
            total = total + self.arrived[d]
        self.arrived[0] = total
        for d in range(1, self.size):
            self.gather(d).start()
        height = self.parts.shape[1]
        self.gram_ref[pl.ds(pl.multiple_of(self.me * height, height), height), :] = total

    def finish(self):
        if self.direct:
            for d in range(1, self.size):
                self.gather(d).wait_recv()

    def close(self):
        if self.direct:
            for d in range(1, self.size):
                self.scatter(d).wait_send()
                self.gather(d).wait_send()


def build_filters(defocus_ref, waves, filters):
    number, length, _ = filters.shape
    half = length // 2
    index = lax.broadcasted_iota(jnp.int32, (1, length), 1)
    freq = jnp.where(index <= half, index, index - half).astype(F32) / length
    square = freq * freq

    def phase(group, _):
        waves[0, pl.ds(group, 1), :] = (math.pi * defocus_ref[group]) * square

    lax.fori_loop(0, number, phase, None, unroll=8)
    phases = waves[0, 0:number, :]
    sine, cosine = jnp.sin(phases), jnp.cos(phases)
    waves[0, 0:number, :] = sine
    waves[1, 0:number, :] = cosine
    keep = math.sqrt(1.0 - AMPLITUDE**2)
    rest = jnp.zeros((length - number, length), F32)
    first = jnp.concatenate([-keep * sine - AMPLITUDE * cosine, rest], axis=0).T
    second = jnp.concatenate([AMPLITUDE * sine - keep * cosine, rest], axis=0).T

    def eight(block, both):
        left, right = both
        for i in range(8):
            group = 8 * block + i
            contrast = (
                left[:, i : i + 1] * waves[1, pl.ds(group, 1), :]
                + right[:, i : i + 1] * waves[0, pl.ds(group, 1), :]
            )
            power = contrast * contrast + WIENER
            over = pl.reciprocal(power, approx=True)
            wiener = contrast * (over * (2.0 - power * over))
            filters[group] = jnp.concatenate([wiener, wiener[8:half]], axis=0).astype(BF16)
        return pltpu.roll(left, length - 8, 1), pltpu.roll(right, length - 8, 1)

    lax.fori_loop(0, number // 8, eight, (first[: half + 8], second[: half + 8]))


def whole_kernel(
    size,
    count,
    stride,
    group_ref,
    live_ref,
    defocus_ref,
    image_hbm,
    matrix_hbm,
    tables_hbm,
    basis_ref,
    out_ref,
    growth_ref,
    tables,
    waves,
    filters,
    images_ref,
    turned,
    columns,
    held,
    sketch_ref,
    gram_ref,
    parts,
    arrived,
    left_ref,
    right_ref,
    inverse_ref,
    work,
    inbox,
    load_sem,
    own_sem,
    send_sem,
    recv_sem,
    sum_send_sem,
    sum_recv_sem,
    back_send_sem,
    back_recv_sem,
):
    me = lax.axis_index("pix")
    step = pl.program_id(0)
    length, slots, _ = columns.shape
    rank = sketch_ref.shape[1]
    steps = slots // count
    pairs = count // 2
    base = step * count
    gather = Gather(me, size, held, matrix_hbm, send_sem, recv_sem)
    events = gather.events()

    def load(i):
        rows = pl.ds(i * count, count)
        return pltpu.make_async_copy(image_hbm.at[rows], images_ref.at[rows], load_sem.at[i])

    @pl.when(step == 0)
    def _():
        gather.greet()
        gather.begin(gather.moves())
        small = [
            pltpu.make_async_copy(tables_hbm, tables, own_sem.at[0]),
            pltpu.make_async_copy(matrix_hbm, held.at[me], own_sem.at[1]),
        ]
        for copy in small:
            copy.start()
        for i in range(min(AHEAD, steps)):
            load(i).start()
        build_filters(defocus_ref, waves, filters)
        for copy in small:
            copy.wait()

    @pl.when((step >= 1) & (step + AHEAD - 1 < steps))
    def _():
        load(step + AHEAD - 1).start()

    early = [place for place in EARLY if place < steps][: len(events)]
    for i, place in enumerate(early):

        @pl.when(step == place)
        def _(i=i):
            gather.handle(events[i])

    load(step).wait()

    def side_by_side(values):
        return jnp.concatenate(values, axis=1)

    def product(left, right):
        return jnp.dot(left, right, preferred_element_type=F32)

    def quads(left, right):
        width = 2 * length
        return jnp.concatenate(
            [product(left, right[i : i + width]) for i in range(0, pairs * length, width)], axis=0
        )

    images = jnp.concatenate(
        [
            side_by_side([images_ref[base + 2 * i], images_ref[base + 2 * i + 1]])
            for i in range(pairs)
        ],
        axis=0,
    )
    weights = jnp.concatenate(
        [
            side_by_side(
                [filters[group_ref[base + 2 * i]], filters[group_ref[base + 2 * i + 1]]]
            )
            for i in range(pairs)
        ],
        axis=0,
    )
    rows = product(images, tables[0]).astype(BF16)
    spectrum = quads(tables[1], rows)
    kept = (spectrum * weights.astype(F32)).astype(BF16)
    back = product(kept, tables[2]).astype(BF16)
    result = quads(tables[3], back)
    for i in range(count):
        tall, wide = i // 2 * length, i % 2 * length
        turned[pl.ds(i, length, stride=stride), :] = result[
            tall : tall + length, wide : wide + length
        ]
    slot = base + lax.broadcasted_iota(jnp.int32, (1, count, 1), 1)
    values = turned[...].reshape(length, stride, length)[:, :count]
    columns[:, pl.ds(pl.multiple_of(base, count), count), :] = jnp.where(
        slot < live_ref[0], values, 0.0
    ).astype(BF16)

    @pl.when(step == steps - 1)
    def _():
        lines = length // size
        layers = gather.layers
        z = gather.z

        def pixels(owner):
            return side_by_side([columns[owner * lines + line] for line in range(lines)])

        def nearest(k):
            room = jnp.minimum(z, layers - 1 - z)
            near = jnp.where(lax.rem(k, 2) == 1, z + lax.div(k + 1, 2), z - lax.div(k + 1, 2))
            far = jnp.where(z < layers - 1 - z, k, layers - 1 - k)
            return jnp.where(k <= 2 * room, near, far)

        waiting = list(range(len(early), len(events)))
        late = {}
        for chip in range(2 * layers):
            ready = min(chip // 2 * 2 + chip % 2 * 2, len(events) - 1)
            late[chip] = [k for k in waiting if k <= ready or chip == 2 * layers - 1]
            waiting = [k for k in waiting if k not in late[chip]]

        def one_chip(chip, _):
            for place, group in late.items():
                if group:

                    @pl.when(chip == place)
                    def _(group=group):
                        for k in group:
                            gather.handle(events[k])

            column = lax.rem(lax.div(me, 2) + chip, 2)
            both = nearest(lax.div(chip, 2)) * 4 + column * 2
            other = both + 1 - lax.rem(me, 2)
            gather.await_beside(other)
            left = side_by_side([columns[both * lines + line] for line in range(2 * lines)])
            right = held[pl.ds(both, 2)]
            sketch_ref[...] += product(left, right.reshape(-1, rank))

        sketch_ref[...] = jnp.zeros_like(sketch_ref)
        lax.fori_loop(0, 2 * layers, one_chip, None)
        sketch = sketch_ref[...]
        sketch_t = sketch.T.astype(BF16)
        scatter = Scatter(gather, work, inbox, back_send_sem, back_recv_sem)
        total = GramSum(me, size, gram_ref, parts, arrived, sum_send_sem, sum_recv_sem)
        up, down, across, beside = gather.UP, gather.DOWN, gather.ACROSS, gather.BESIDE

        def ways(distance):
            out = []
            for upwards in (False, True) if distance else (True,):
                own = me + (4 * distance if upwards else -4 * distance)
                other = partner_of(own, 2)
                there = z + distance < layers if upwards else z >= distance
                given = [there] if distance else []
                out.append((given, upwards, own, other, partner_of(own, 1), partner_of(other, 1)))
            return out

        def run(given, act):
            pl.when(given[0])(act) if given else act()

        def compute(distance):
            for given, upwards, own, other, own_beside, other_beside in ways(distance):

                def act():
                    for owner, aside in ((other, other_beside), (own, own_beside)):
                        work[aside] = product(sketch_t, pixels(aside)).astype(BF16)
                        scatter.send(aside, 3, beside, given)
                        work[owner] = product(sketch_t, pixels(owner)).astype(BF16)

                run(given, act)

        def onward(owner, part, upwards, given):
            way, ahead = (up, gather.has_down) if upwards else (down, gather.has_up)
            pl.when(ahead)(lambda: scatter.take(owner, part, way))
            scatter.send(owner, part, way, given)

        def chip_sum(distance):
            for given, upwards, own, other, _, _ in ways(distance):

                def act():
                    scatter.take(other, 3, beside)
                    for part in range(2):
                        scatter.send(other, part, across, given)

                run(given, act)

        def own_sum(distance):
            for given, upwards, own, _, _, _ in ways(distance):
                run(given, lambda own=own: scatter.take(own, 3, beside))

        def third(distance):
            for given, upwards, own, other, _, _ in ways(distance):

                def act():
                    onward(other, 2, upwards, given)
                    onward(own, 2, upwards, given)

                run(given, act)

        def along(distance, part):
            for given, upwards, own, _, _, _ in ways(distance):

                def act():
                    scatter.take(own, part, across)
                    if distance:
                        onward(own, part, upwards, given)

                run(given, act)

        def last(owner, part):
            pl.when(gather.has_down)(lambda: scatter.take(owner, part, up))
            pl.when(gather.has_up)(lambda: scatter.take(owner, part, down))

        compute(layers - 1)
        gram = lax.dot_general(
            sketch, sketch, (((0,), (0,)), ((), ())), precision=HIGHEST, preferred_element_type=F32
        )
        parts[...] = gram.reshape(parts.shape)
        total.start()
        for distance in range(layers - 1, -1, -1):
            chip_sum(distance)
            own_sum(distance)
            if distance == layers - 1 and distance:
                third(distance)
            if distance:
                compute(distance - 1)
            if distance == max(layers - TURN, 0):
                total.turn()
        for distance in range(layers - 2, 0, -1):
            third(distance)
        todo = [(distance, part) for distance in range(layers - 1, 0, -1) for part in range(2)]
        for place in todo[:FINISH]:
            along(*place)
        total.finish()
        unit = lax.broadcasted_iota(jnp.int32, (rank, rank), 0) == lax.broadcasted_iota(
            jnp.int32, (rank, rank), 1
        )
        left_ref[...] = gram_ref[...]
        right_ref[...] = jnp.where(unit, 1.0, 0.0)
        blocks = rank // 8
        todo = todo[FINISH:]
        for i in range(len(todo) + 1):
            lax.fori_loop(
                blocks * i // (len(todo) + 1),
                blocks * (i + 1) // (len(todo) + 1),
                lambda block, _: factor_step(block, left_ref, right_ref, inverse_ref),
                None,
            )
            if i < len(todo):
                along(*todo[i])
        inverse = inverse_ref[...]
        basis_ref[...] = lax.dot_general(
            sketch,
            inverse,
            (((1,), (1,)), ((), ())),
            precision=HIGHEST,
            preferred_element_type=F32,
        ).astype(BF16)
        scale = jnp.sqrt(jnp.sum(inverse * inverse, axis=0, keepdims=True))
        sums = jnp.dot(
            jnp.broadcast_to(scale, (8, rank)),
            jnp.abs(gram_ref[...]),
            precision=HIGHEST,
            preferred_element_type=F32,
        )
        growth_ref[0] = jnp.where(jnp.max(sums * scale) <= GROWTH, 1, 0)
        last(gather.across, 2)
        scatter.send(gather.across, 2, across, [])
        last(me, 2)
        for part in range(2):
            along(0, part)
            last(me, part)
        scatter.take(me, 2, across)
        mine = jnp.dot(
            inverse, work[me].astype(F32), precision=HIGHEST, preferred_element_type=F32
        )
        out_ref[...] = mine.T
        gather.close()
        scatter.close()
        total.close()


def make_whole(images, groups, live, defocus_values, matrix, size):
    slots, length, _ = images.shape
    height, rank = matrix.shape
    count = math.gcd(slots, 32)
    stride = count + 4
    tables = pair_tables(length)
    number = defocus_values.shape[0]
    if direct_sum(rank, size):
        summing = [pltpu.VMEM((size, rank // size, rank), F32)] * 2
        signals = 2 * size
    else:
        summing = [
            pltpu.VMEM((1, rank, rank), F32),
            pltpu.VMEM((bits_of(size), rank, rank), F32),
        ]
        signals = bits_of(size)

    def whole(*shape):
        return pl.BlockSpec(shape, lambda i, *_: (0,) * len(shape))

    square = pltpu.VMEM((rank, rank), F32)
    return pl.pallas_call(
        functools.partial(whole_kernel, size, count, stride),
        out_shape=(
            jax.ShapeDtypeStruct((slots, rank), BF16),
            jax.ShapeDtypeStruct((height, rank), F32),
            jax.ShapeDtypeStruct((1,), jnp.int32),
        ),
        grid_spec=pltpu.PrefetchScalarGridSpec(
            num_scalar_prefetch=3,
            grid=(slots // count,),
            in_specs=[
                *[pl.BlockSpec(memory_space=pl.ANY)] * 3,
            ],
            out_specs=(
                whole(slots, rank),
                whole(height, rank),
                pl.BlockSpec(memory_space=pltpu.SMEM),
            ),
            scratch_shapes=[
                pltpu.VMEM((4, 2 * length, 2 * length), BF16),
                pltpu.VMEM((2, number, length), F32),
                pltpu.VMEM((number, length, length), BF16),
                pltpu.VMEM((slots, length, length), BF16),
                pltpu.VMEM((length * stride, length), F32),
                pltpu.VMEM((length, slots, length), BF16),
                pltpu.VMEM((size, height, rank), BF16),
                pltpu.VMEM((slots, rank), F32),
                square,
                *summing,
                square,
                square,
                square,
                pltpu.VMEM((size, rank, height), BF16),
                pltpu.VMEM((4, size // 2, rank, height), BF16),
                pltpu.SemaphoreType.DMA((slots // count,)),
                pltpu.SemaphoreType.DMA((2,)),
                pltpu.SemaphoreType.DMA((9 * size // 2 + 3 * (size // 4),)),
                pltpu.SemaphoreType.DMA((size, 3)),
                pltpu.SemaphoreType.DMA((signals,)),
                pltpu.SemaphoreType.DMA((signals,)),
                pltpu.SemaphoreType.DMA((4 * size // 2 + 3 * (size // 4),)),
                pltpu.SemaphoreType.DMA((7 * size // 2 + 3 * (size // 4),)),
            ],
        ),
        compiler_params=pltpu.CompilerParams(
            collective_id=0, has_side_effects=True, vmem_limit_bytes=56 << 20
        ),
        name="whole",
    )(groups, live, defocus_values, images, matrix, tables)


def sketch_kernel(
    size,
    group_ref,
    live_ref,
    image_ref,
    matrix_ref,
    filters,
    pair_ref,
    pair_t_ref,
    table_ref,
    table_t_ref,
    out_ref,
    sketch_ref,
    gram_ref,
    turned,
    held,
    summed,
    parts,
    arrived,
    send_sem,
    recv_sem,
    sum_send_sem,
    sum_recv_sem,
):
    me = lax.axis_index("pix")
    step = pl.program_id(0)
    steps = out_ref.shape[1] // image_ref.shape[0]
    count, length, _ = image_ref.shape
    pairs = count // 2
    base = step * count
    orders = gathering_orders(size)
    stages = bits_of(size)
    height = matrix_ref.shape[0] // 2

    def copy_of(half, stage, mask):
        bit = orders[half][stage]
        slot = (bit | mask) - 1
        return remote(
            held.at[half, mask],
            held.at[half, bit | mask],
            send_sem.at[half, slot],
            recv_sem.at[half, slot],
            partner_of(me, bit),
        )

    def receive(stage, half, mask):
        copy_of(half, stage, mask).wait_recv()
        for later in range(stage + 1, stages):
            copy_of(half, later, orders[half][stage] | mask).start()

    @pl.when(step == 0)
    def _():
        greet(me, peers(gram_ref.shape[0], size))
        for half in range(2):
            held[half, 0] = matrix_ref[half * height : (half + 1) * height, :]
        for stage in range(stages):
            for half in range(2):
                copy_of(half, stage, 0).start()

    early = min(2, stages)
    for stage in range(early):

        @pl.when(step == steps * (5 + 6 * stage) // 16)
        def _(stage=stage):
            for place in range(1 << stage):
                for half in range(2):
                    receive(stage, half, sums(orders[half][:stage])[place])

    def side_by_side(values):
        return jnp.concatenate(values, axis=1)

    def stacked(wide):
        return jnp.concatenate(
            [wide[:, 2 * length * i : 2 * length * (i + 1)] for i in range(pairs)], axis=0
        )

    def unstacked(tall):
        return side_by_side([tall[length * i : length * (i + 1)] for i in range(pairs)])

    images = jnp.concatenate(
        [side_by_side([image_ref[2 * i], image_ref[2 * i + 1]]) for i in range(pairs)], axis=0
    )
    rows = jnp.dot(images, pair_ref[...], preferred_element_type=F32).astype(BF16)
    spectrum = jnp.dot(table_t_ref[...], unstacked(rows), preferred_element_type=F32)
    weights = side_by_side([filters[group_ref[base + i]] for i in range(count)])
    kept = (spectrum * weights.astype(F32)).astype(BF16)
    back = jnp.dot(stacked(kept), pair_t_ref[...], preferred_element_type=F32).astype(BF16)
    result = jnp.dot(table_ref[...], unstacked(back), preferred_element_type=F32)
    for i in range(count):
        turned[pl.ds(i, length, stride=count), :] = result[:, i * length : (i + 1) * length]
    slot = base + lax.broadcasted_iota(jnp.int32, (1, count, 1), 1)
    values = turned[...].reshape(length, count, length)
    out_ref[:, pl.ds(pl.multiple_of(base, count), count), :] = jnp.where(
        slot < live_ref[0], values, 0.0
    ).astype(BF16)

    @pl.when(step == steps - 1)
    def _():
        lines = length // size
        part = lines // 2

        def term(half, mask):
            start = partner_of(me, mask) * lines + half * part
            left = side_by_side([out_ref[start + line] for line in range(part)])
            return jnp.dot(left, held[half, mask], preferred_element_type=F32)

        sketch_ref[...] = jnp.zeros_like(sketch_ref)
        for half in range(2):
            for mask in sums(orders[half][:early]):
                sketch_ref[...] += term(half, mask)
        for stage in range(early, stages):
            for place in range(1 << stage):
                for half in range(2):
                    mask = sums(orders[half][:stage])[place]
                    receive(stage, half, mask)
                    sketch_ref[...] += term(half, orders[half][stage] | mask)
        sketch = sketch_ref[...]
        gram = lax.dot_general(
            sketch, sketch, (((0,), (0,)), ((), ())), precision=HIGHEST, preferred_element_type=F32
        )
        parts[...] = gram.reshape(parts.shape)
        sum_gram(me, size, summed, parts, arrived, sum_send_sem, sum_recv_sem)
        gram_ref[...] = summed[...]
        for half in range(2):
            for stage in range(stages):
                for mask in sums(orders[half][:stage]):
                    copy_of(half, stage, mask).wait_send()


def make_sketch(images, groups, live, defocus_values, matrix, size):
    slots, length, _ = images.shape
    height, rank = matrix.shape
    count = math.gcd(slots, 16)
    table = real_tables(length)
    zero = jnp.zeros_like(table)
    pair = jnp.concatenate(
        [jnp.concatenate([table, zero], axis=1), jnp.concatenate([zero, table], axis=1)], axis=0
    )
    number = defocus_values.shape[0]
    if direct_sum(rank, size):
        summing = [
            pltpu.VMEM((size, rank // size, rank), F32),
            pltpu.VMEM((size, rank // size, rank), F32),
        ]
        signals = 2 * size
    else:
        summing = [
            pltpu.VMEM((1, rank, rank), F32),
            pltpu.VMEM((bits_of(size), rank, rank), F32),
        ]
        signals = bits_of(size)

    def whole(*shape):
        return pl.BlockSpec(shape, lambda i, *_: (0,) * len(shape))

    return pl.pallas_call(
        functools.partial(sketch_kernel, size),
        out_shape=(
            jax.ShapeDtypeStruct((length, slots, length), BF16),
            jax.ShapeDtypeStruct((slots, rank), F32),
            jax.ShapeDtypeStruct((rank, rank), F32),
        ),
        grid_spec=pltpu.PrefetchScalarGridSpec(
            num_scalar_prefetch=2,
            grid=(slots // count,),
            in_specs=[
                pl.BlockSpec((count, length, length), lambda i, *_: (i, 0, 0)),
                whole(height, rank),
                whole(number, length, length),
                whole(2 * length, 2 * length),
                whole(2 * length, 2 * length),
                whole(length, length),
                whole(length, length),
            ],
            out_specs=(whole(length, slots, length), whole(slots, rank), whole(rank, rank)),
            scratch_shapes=[
                pltpu.VMEM((length * count, length), F32),
                pltpu.VMEM((2, size, height // 2, rank), BF16),
                pltpu.VMEM((rank, rank), F32),
                *summing,
                pltpu.SemaphoreType.DMA((2, size - 1)),
                pltpu.SemaphoreType.DMA((2, size - 1)),
                pltpu.SemaphoreType.DMA((signals,)),
                pltpu.SemaphoreType.DMA((signals,)),
            ],
        ),
        compiler_params=pltpu.CompilerParams(
            collective_id=1, has_side_effects=True, vmem_limit_bytes=50 << 20
        ),
        name="sketch",
    )(
        groups,
        live,
        images,
        matrix,
        filter_table(defocus_values, length),
        pair,
        pair.T,
        table,
        table.T,
    )


def basis_kernel(factor_ref, sketch_ref, out_ref, turned_ref):
    rank = factor_ref.shape[0]
    row = lax.broadcasted_iota(jnp.int32, (rank, rank), 0)
    col = lax.broadcasted_iota(jnp.int32, (rank, rank), 1)
    factor = factor_ref[...]
    on_diagonal = jnp.where(row == col, factor, 0.0)
    lower = jnp.where(row > col, factor, 0.0) / jnp.sum(on_diagonal, axis=1, keepdims=True)

    def times(left, right):
        return jnp.dot(left, right, precision=HIGHEST, preferred_element_type=F32)

    def same_block(shift):
        return lax.shift_right_logical(row, shift) == lax.shift_right_logical(col, shift)

    shift = 3
    within = jnp.where(same_block(shift), lower, 0.0)
    unit = jnp.where(row == col, 1.0, 0.0).astype(F32)
    square = times(within, within)
    fourth = times(square, square)
    inverse = times(times(unit - within, unit + square), unit + fourth)
    while 1 << shift < rank:
        off = jnp.where(same_block(shift + 1) & ~same_block(shift), lower, 0.0)
        inverse = inverse - times(inverse, times(off, inverse))
        shift += 1
    inverse = inverse / jnp.sum(on_diagonal, axis=0, keepdims=True)
    basis = lax.dot_general(
        sketch_ref[...],
        inverse,
        (((1,), (1,)), ((), ())),
        precision=HIGHEST,
        preferred_element_type=F32,
    )
    out_ref[...] = basis.astype(BF16)
    turned_ref[...] = basis.T.astype(BF16)


def make_basis(factor_low, sketch):
    slots, rank = sketch.shape
    return pl.pallas_call(
        basis_kernel,
        out_shape=(
            jax.ShapeDtypeStruct((slots, rank), BF16),
            jax.ShapeDtypeStruct((rank, slots), BF16),
        ),
        name="basis",
    )(factor_low, sketch)


def project_kernel(size, basis_ref, column_ref, out_ref, held, arrived, send_sem, recv_sem):
    me = lax.axis_index("pix")
    length = column_ref.shape[0]
    rows = length // size
    part = rows // 2
    orders = halving_orders(size)
    slots = {}
    for half in range(2):
        for stage in range(len(orders[half])):
            for mask in masks_of(orders[half][stage + 1 :]):
                slots[half, stage, mask] = len(slots) % (size - 1)

    def copy_of(half, stage, mask):
        bit = orders[half][stage]
        slot = slots[half, stage, mask]
        return remote(
            held.at[half, bit | mask],
            arrived.at[half, slot],
            send_sem.at[half, slot],
            recv_sem.at[half, slot],
            partner_of(me, bit),
        )

    greet(me, [1 << shift for shift in range(bits_of(size))])
    first = orders[0][0]

    def compute(half, mask):
        start = partner_of(me, mask) * rows + half * part
        right = jnp.concatenate([column_ref[start + row] for row in range(part)], axis=1)
        held[half, mask] = jnp.dot(
            basis_ref[...], right, preferred_element_type=F32
        ).astype(BF16)

    def add(half, stage, mask):
        later = orders[half][stage + 1 :]
        copy_of(half, stage, mask).wait_recv()
        total = (
            held[half, mask].astype(F32)
            + arrived[half, slots[half, stage, mask]].astype(F32)
        )
        if later:
            held[half, mask] = total.astype(BF16)
            if mask & later[0]:
                copy_of(half, stage + 1, mask - later[0]).start()
        else:
            height = out_ref.shape[0] // 2
            out_ref[half * height : (half + 1) * height, :] = total.T

    kept = [masks_of(orders[half][1:]) for half in range(2)]
    for place in range(len(kept[0]) + 1):
        for half in range(2):
            if place < len(kept[0]):
                mask = kept[half][place]
                compute(half, first | mask)
                copy_of(half, 0, mask).start()
                compute(half, mask)
        for half in range(2):
            if place > 0:
                add(half, 0, kept[half][place - 1])
    for stage in range(1, bits_of(size)):
        for place in range(len(masks_of(orders[0][stage + 1 :]))):
            for half in range(2):
                add(half, stage, masks_of(orders[half][stage + 1 :])[place])
    for half in range(2):
        for stage in range(bits_of(size)):
            for mask in masks_of(orders[half][stage + 1 :]):
                copy_of(half, stage, mask).wait_send()


def project(columns, basis_t, size):
    length, slots, _ = columns.shape
    rank = basis_t.shape[0]
    width = length * length // size
    return pl.pallas_call(
        functools.partial(project_kernel, size),
        out_shape=jax.ShapeDtypeStruct((width, rank), F32),
        in_specs=[pl.BlockSpec(memory_space=pltpu.VMEM)] * 2,
        out_specs=pl.BlockSpec(memory_space=pltpu.VMEM),
        scratch_shapes=[
            pltpu.VMEM((2, size, rank, width // 2), BF16),
            pltpu.VMEM((2, size - 1, rank, width // 2), BF16),
            pltpu.SemaphoreType.DMA((2, size - 1)),
            pltpu.SemaphoreType.DMA((2, size - 1)),
        ],
        compiler_params=pltpu.CompilerParams(
            collective_id=2, has_side_effects=True, vmem_limit_bytes=48 << 20
        ),
        name="project",
    )(basis_t, columns)


def per_device(particle_images, defocus_group, live_counts, defocus_values, test_matrix):
    size = lax.axis_size("pix")
    arguments = (particle_images, defocus_group, live_counts, defocus_values, test_matrix, size)
    basis, projection, growth = make_whole(*arguments)

    def stepwise():
        columns, sketch, gram = make_sketch(*arguments)
        factor_low = jnp.linalg.cholesky(gram)
        range_basis, basis_t = make_basis(factor_low, sketch)
        return (range_basis, project(columns, basis_t, size))

    return lax.cond(growth[0] != 0, lambda: (basis, projection), stepwise)


def solution(mesh):
    placed = (
        P(("grp", "pix"), None, None),
        P(("grp", "pix")),
        P(("grp", "pix")),
        P("grp"),
        P(("grp", "pix"), None),
    )
    return jax.shard_map(
        per_device,
        mesh=mesh,
        in_specs=placed,
        out_specs=(P(("grp", "pix"), None), P(("grp", "pix"), None)),
        check_vma=False,
    )
```
